128 devices in a mesh: tiles: 16 (over y, x), gauss: 8 (over z, core).
Axes of the slice: x: 4, y: 4, z: 4, core: 2. Of those that a mesh axis runs over, the one named last changes fastest.
Arguments:
- params: float32 [59, 2097152], P(None, ('tiles', 'gauss')), may hold values from -9 to 4.5, as said below
- adam_m: float32 [59, 2097152], P(None, ('tiles', 'gauss')), may hold values from -0.03 to 0.03
- adam_v: float32 [59, 2097152], P(None, ('tiles', 'gauss')), may hold values from 0.05 to 2
- cameras: float32 [4, 13], replicated, may hold values from -0.5 to 2000, as said below
- exposure: float32 [4, 3], replicated, may hold values from 0.5 to 1.5
- entry_owner: int32 [512, 1024], P(('tiles', 'gauss')), may hold values from 0 to 127, as said below
- entry_local: int32 [512, 1024], P(('tiles', 'gauss')), may hold values from 0 to 16383
- block_counts: int32 [512], P(('tiles', 'gauss')), may hold values from 2 to 4, as said below
- tile_view: int32 [512], P(('tiles', 'gauss')), may hold values from 0 to 3
- tile_spot: int32 [512], P(('tiles', 'gauss')), may hold values from 12580 to 19579
- d_image: float32 [512, 3, 256], P(('tiles', 'gauss')), may hold values from -320 to 320
Outputs:
- new_params: float32 [59, 2097152], P(None, ('tiles', 'gauss'))
- new_m: float32 [59, 2097152], P(None, ('tiles', 'gauss'))
- new_v: float32 [59, 2097152], P(None, ('tiles', 'gauss'))
- exposure_grad: float32 [4, 3], replicated
The draws below stay inside these ranges and needn't reach their ends.
Inputs may be any that keep to these rules, and one draw needn't show every extreme that they name: `params`: components 0 to 2 lie in -4.5 to 4.5, components 3 to 5 in -5 to -2, component 6 in 0.5 to 1.5, component 10 in -9 to -7.5. `cameras`: each row holds a matrix whose entries differ from the identity's by at most 0.1, a translation with first two entries in -0.5 to 0.5 and third in 5 to 6, and a focal length in 1400 to 2000. `entry_owner`: of the 4096 entries of one device's lists (rendered or not), at most 48 name any one owner; in every draw one owner is named exactly 48 times by every device. `block_counts`: every device holds a tile of 4 blocks.
All inputs are finite; a program needn't handle non-finite values.
Results may differ from the reference program's by a relative error of at most 0.0003.
Values sent between devices are 32-bit elements; how exact they have to be, the bound alone decides.
No kernel may reach another device: no remote copies, remote signals or barrier semaphores. Data moves between devices by JAX's collectives and lax.ppermute only.
A program may use at most 256 MiB of HBM per device.

```python
import math
import jax
import jax.numpy as jnp
from jax import lax

G_DEV = 16384
TILE_DEV = 4
VIEWS = 4
MAXB = 4
BLOCK = 256
TILE = 16
IMG_W = 3840
IMG_H = 2160
PARAMS = 59
TPIX = 256
NDEV = 128
NG = 2097152
NTILES = 512
SLOTS = 1024
E_DEV = 4096
CAP = 48


def camera_table(key):
    streams = jax.random.split(jax.random.fold_in(key, 101), 4)
    matrix = jnp.eye(3, dtype=jnp.float32)[None] + jax.random.uniform(streams[0], (VIEWS, 3, 3), jnp.float32, -0.1, 0.1)
    sideways = jax.random.uniform(streams[1], (VIEWS, 2), jnp.float32, -0.5, 0.5)
    distance = jax.random.uniform(streams[2], (VIEWS, 1), jnp.float32, 5.0, 6.0)
    focal_len = jax.random.uniform(streams[3], (VIEWS, 1), jnp.float32, 1400.0, 2000.0)
    return jnp.concatenate([matrix.reshape(VIEWS, 9), sideways, distance, focal_len], axis=1)


def view_table(key):
    return jax.random.randint(jax.random.fold_in(key, 102), (NTILES,), 0, VIEWS).astype(jnp.int32)


def spot_table(key):
    across = IMG_W // TILE
    downward = IMG_H // TILE
    key_column, key_line = jax.random.split(jax.random.fold_in(key, 103))
    columns = across // 2 - 20 + jax.random.randint(key_column, (NTILES,), 0, 40)
    lines = downward // 2 - 15 + jax.random.randint(key_line, (NTILES,), 0, 30)
    return (lines * across + columns).astype(jnp.int32)


def local_table(key):
    return jax.random.randint(jax.random.fold_in(key, 104), (NTILES, SLOTS), 0, G_DEV).astype(jnp.int32)


def owner_table(key):
    owner_pool = jnp.arange(NDEV * CAP, dtype=jnp.int32) // CAP
    positions = jnp.arange(NDEV * CAP, dtype=jnp.int32)
    common = jax.random.randint(jax.random.fold_in(key, 11), (), 0, NDEV)

    def one_device(device_key):
        key_score, key_order = jax.random.split(device_key)
        scores = jax.random.permutation(key_score, NDEV * CAP).astype(jnp.int32)
        scores = jnp.where(owner_pool == common, -1 - positions, scores)
        chosen = owner_pool[jnp.argsort(scores, stable=True)[:E_DEV]]
        return jax.random.permutation(key_order, chosen)
    device_keys = jax.random.split(jax.random.fold_in(key, 13), NDEV)
    return jax.vmap(one_device)(device_keys).reshape(NTILES, SLOTS).astype(jnp.int32)


def draw_cameras(key, part):
    return camera_table(key)


def draw_tile_view(key, part):
    return view_table(key)


def draw_tile_spot(key, part):
    return spot_table(key)


def draw_entry_local(key, part):
    return local_table(key)


def draw_entry_owner(key, part):
    return owner_table(key)


def draw_params(key, part):
    streams = jax.random.split(key, 8)
    count = NG
    entries = NTILES * SLOTS
    loose_means = jax.random.uniform(streams[0], (3, count), jnp.float32, -2.0, 2.0)
    log_scales = -3.5 + 0.5 * jax.random.truncated_normal(streams[1], -3.0, 3.0, (3, count), jnp.float32)
    logits = jax.random.uniform(streams[4], (1, count), jnp.float32, -9.0, -7.5)
    base_color = jax.random.truncated_normal(streams[5], -3.0, 3.0, (3, count), jnp.float32)
    quat_w = jax.random.uniform(streams[2], (1, count), jnp.float32, 0.5, 1.5)
    quat_rest = 0.5 * jax.random.truncated_normal(streams[3], -3.0, 3.0, (3, count), jnp.float32)
    higher = 0.3 * jax.random.truncated_normal(streams[6], -3.0, 3.0, (45, count), jnp.float32)
    jitter = jax.random.uniform(streams[7], (5, count), jnp.float32)
    cameras = camera_table(key)
    gauss_ids = (owner_table(key) * G_DEV + local_table(key)).reshape(entries)
    first_entry = jnp.full((count,), entries, jnp.int32).at[gauss_ids].min(jnp.arange(entries, dtype=jnp.int32))
    named = first_entry < entries
    entry_at = jnp.minimum(first_entry, entries - 1)
    tile_at = entry_at // SLOTS
    slot_at = entry_at % SLOTS
    view_at = view_table(key)[tile_at]
    spot_at = spot_table(key)[tile_at]
    camera_at = jnp.take(cameras.T, view_at, axis=1)
    across = IMG_W // TILE
    depth = camera_at[11] - 1.5 + 3.0 * (slot_at.astype(jnp.float32) + jitter[0]) / SLOTS
    focal_len = camera_at[12]
    footprint = focal_len / depth * jnp.exp(jnp.max(log_scales, axis=0))
    pixel_x = (spot_at % across * TILE).astype(jnp.float32) + TILE * jitter[1] + 1.5 * (2.0 * jitter[2] - 1.0) * footprint
    pixel_y = (spot_at // across * TILE).astype(jnp.float32) + TILE * jitter[3] + 1.5 * (2.0 * jitter[4] - 1.0) * footprint
    relative = [(pixel_x - 0.5 * IMG_W) * depth / focal_len - camera_at[9], (pixel_y - 0.5 * IMG_H) * depth / focal_len - camera_at[10], depth - camera_at[11]]
    matrix = [[camera_at[3 * row_at + col_at] for col_at in range(3)] for row_at in range(3)]
    cofactor = [[matrix[(row_at + 1) % 3][(col_at + 1) % 3] * matrix[(row_at + 2) % 3][(col_at + 2) % 3] - matrix[(row_at + 1) % 3][(col_at + 2) % 3] * matrix[(row_at + 2) % 3][(col_at + 1) % 3] for col_at in range(3)] for row_at in range(3)]
    determinant = matrix[0][0] * cofactor[0][0] + matrix[0][1] * cofactor[0][1] + matrix[0][2] * cofactor[0][2]
    placed = jnp.stack([(cofactor[0][col_at] * relative[0] + cofactor[1][col_at] * relative[1] + cofactor[2][col_at] * relative[2]) / determinant for col_at in range(3)])
    centres = jnp.where(named[None, :], placed, loose_means)
    return jnp.concatenate([centres, log_scales, quat_w, quat_rest, logits, base_color, higher], axis=0)


def draw_block_counts(key, part):
    key_count, key_full = jax.random.split(key)
    counts = jax.random.randint(key_count, (NDEV, TILE_DEV), 2, MAXB + 1)
    where_full = jax.random.randint(key_full, (NDEV, 1), 0, TILE_DEV)
    counts = jnp.where(jnp.arange(TILE_DEV)[None, :] == where_full, MAXB, counts)
    return counts.reshape(NTILES).astype(jnp.int32)


def block_scale(stream_key, dims, shards, smallest, top_value):
    level, own = 1.0, jax.random.fold_in(stream_key, 6)
    for axis_at, blocks in shards:
        steps = jnp.exp(jax.random.uniform(jax.random.fold_in(own, axis_at), (blocks,), jnp.float32, smallest / len(shards), top_value / len(shards)))
        level = level * jnp.repeat(steps, dims[axis_at] // blocks).reshape([-1 if axis == axis_at else 1 for axis in range(len(dims))])
    return level


def centred(rng, dims, scale, limit, pieces=(), held_as=jnp.bfloat16):
    drawn = scale * jax.random.normal(rng, dims, jnp.float32)
    if pieces:
        drawn = drawn * block_scale(rng, dims, pieces, -0.22, 0.18)
    return jnp.clip(drawn, -limit, limit).astype(held_as)


def setup_inputs(seed: int = 0) -> dict:
    streams_of = jax.random.split(jax.random.key(seed), 12)
    params = draw_params(jax.random.fold_in(streams_of[11], 71), 0)
    adam_m = centred(streams_of[1], (PARAMS, NG), 0.005, 0.03, ((1, 128),), jnp.float32)
    adam_v = jnp.clip(jnp.exp(math.log(2.0) - 3.6888794 * jax.random.uniform(streams_of[2], (PARAMS, NG), jnp.float32) ** block_scale(streams_of[2], (PARAMS, NG), ((1, 128),), -0.2, 0.2)), 0.05, 2.0)
    cameras = draw_cameras(jax.random.fold_in(streams_of[11], 71), 0)
    exposure = jnp.clip(1.0 + 0.1 * jax.random.normal(streams_of[4], (VIEWS, 3), jnp.float32), 0.5, 1.5)
    entry_owner = draw_entry_owner(jax.random.fold_in(streams_of[11], 71), 0)
    entry_local = draw_entry_local(jax.random.fold_in(streams_of[11], 71), 0)
    block_counts = draw_block_counts(jax.random.fold_in(streams_of[11], 71), 0)
    tile_view = draw_tile_view(jax.random.fold_in(streams_of[11], 71), 0)
    tile_spot = draw_tile_spot(jax.random.fold_in(streams_of[11], 71), 0)
    d_image = centred(streams_of[10], (NTILES, 3, TPIX), 50.0, 320.0, ((0, 128),), jnp.float32)
    return dict(params=params, adam_m=adam_m, adam_v=adam_v, cameras=cameras, exposure=exposure, entry_owner=entry_owner, entry_local=entry_local, block_counts=block_counts, tile_view=tile_view, tile_spot=tile_spot, d_image=d_image)


sh_c0 = 0.28209479177387814
sh_c1 = 0.4886025119029199
sh_c2 = (1.0925484305920792, -1.0925484305920792, 0.31539156525252005, -1.0925484305920792, 0.5462742152960396)
sh_c3 = (-0.5900435899266435, 2.890611442640554, -0.4570457994644658, 0.3731763325901154, -0.4570457994644658, 1.445305721320277, -0.5900435899266435)
beta_first = 0.9
beta_second = 0.999
learn_rate = 0.01
adam_eps = 1e-08
fix_first = 1.0
fix_second = 0.632304575229036
blur_add = 0.3

def sh_color(values, unit_x, unit_y, unit_z):
    coefficients = [values[11 + 3 * index_k:14 + 3 * index_k] for index_k in range(16)]
    square_x = unit_x * unit_x
    square_y = unit_y * unit_y
    square_z = unit_z * unit_z
    basis_list = [-sh_c1 * unit_y, sh_c1 * unit_z, -sh_c1 * unit_x, sh_c2[0] * unit_x * unit_y, sh_c2[1] * unit_y * unit_z, sh_c2[2] * (2.0 * square_z - square_x - square_y), sh_c2[3] * unit_x * unit_z, sh_c2[4] * (square_x - square_y), sh_c3[0] * unit_y * (3.0 * square_x - square_y), sh_c3[1] * unit_x * unit_y * unit_z, sh_c3[2] * unit_y * (4.0 * square_z - square_x - square_y), sh_c3[3] * unit_z * (2.0 * square_z - 3.0 * square_x - 3.0 * square_y), sh_c3[4] * unit_x * (4.0 * square_z - square_x - square_y), sh_c3[5] * unit_z * (square_x - square_y), sh_c3[6] * unit_x * (square_x - 3.0 * square_y)]
    summed = 0.5 + sh_c0 * coefficients[0]
    for index_k in range(15):
        summed = summed + basis_list[index_k] * coefficients[index_k + 1]
    return jnp.maximum(summed, 0.0)

def project(values, camera):
    points = [values[0], values[1], values[2]]
    matrix = [[camera[3 * row_at + col_at] for col_at in range(3)] for row_at in range(3)]
    translation = [camera[9], camera[10], camera[11]]
    focal_len = camera[12]
    viewed = [matrix[row_at][0] * points[0] + matrix[row_at][1] * points[1] + matrix[row_at][2] * points[2] + translation[row_at] for row_at in range(3)]
    inverse_depth = 1.0 / viewed[2]
    screen_x = focal_len * viewed[0] * inverse_depth + 0.5 * IMG_W
    screen_y = focal_len * viewed[1] * inverse_depth + 0.5 * IMG_H
    slope_x = focal_len * viewed[0] * inverse_depth * inverse_depth
    slope_y = focal_len * viewed[1] * inverse_depth * inverse_depth
    jac_w = [[focal_len * inverse_depth * matrix[0][col_at] - slope_x * matrix[2][col_at] for col_at in range(3)], [focal_len * inverse_depth * matrix[1][col_at] - slope_y * matrix[2][col_at] for col_at in range(3)]]
    quat_len = jnp.sqrt(values[6] * values[6] + values[7] * values[7] + values[8] * values[8] + values[9] * values[9])
    quat_w = values[6] / quat_len
    quat_x = values[7] / quat_len
    quat_y = values[8] / quat_len
    quat_z = values[9] / quat_len
    rotation = [[1.0 - 2.0 * (quat_y * quat_y + quat_z * quat_z), 2.0 * (quat_x * quat_y - quat_w * quat_z), 2.0 * (quat_x * quat_z + quat_w * quat_y)], [2.0 * (quat_x * quat_y + quat_w * quat_z), 1.0 - 2.0 * (quat_x * quat_x + quat_z * quat_z), 2.0 * (quat_y * quat_z - quat_w * quat_x)], [2.0 * (quat_x * quat_z - quat_w * quat_y), 2.0 * (quat_y * quat_z + quat_w * quat_x), 1.0 - 2.0 * (quat_x * quat_x + quat_y * quat_y)]]
    extent = [jnp.exp(values[3]), jnp.exp(values[4]), jnp.exp(values[5])]
    spread = [[(jac_w[row_at][0] * rotation[0][col_at] + jac_w[row_at][1] * rotation[1][col_at] + jac_w[row_at][2] * rotation[2][col_at]) * extent[col_at] for col_at in range(3)] for row_at in range(2)]
    cov_a = spread[0][0] * spread[0][0] + spread[0][1] * spread[0][1] + spread[0][2] * spread[0][2] + blur_add
    cov_b = spread[0][0] * spread[1][0] + spread[0][1] * spread[1][1] + spread[0][2] * spread[1][2]
    cov_c = spread[1][0] * spread[1][0] + spread[1][1] * spread[1][1] + spread[1][2] * spread[1][2] + blur_add
    determinant = cov_a * cov_c - cov_b * cov_b
    opacity = jax.nn.sigmoid(values[10])
    center = [-(matrix[0][col_at] * translation[0] + matrix[1][col_at] * translation[1] + matrix[2][col_at] * translation[2]) for col_at in range(3)]
    offset = [points[col_at] - center[col_at] for col_at in range(3)]
    distance = jnp.sqrt(offset[0] * offset[0] + offset[1] * offset[1] + offset[2] * offset[2])
    colors = sh_color(values, offset[0] / distance, offset[1] / distance, offset[2] / distance)
    first_rows = jnp.stack([screen_x, screen_y, cov_c / determinant, -cov_b / determinant, cov_a / determinant, opacity])
    return jnp.concatenate([first_rows, colors], axis=0)

def render(proj_rows, live_mask, pix_x, pix_y):
    off_x = pix_x[None, :] - proj_rows[0][:, None]
    off_y = pix_y[None, :] - proj_rows[1][:, None]
    exponent = -0.5 * (proj_rows[2][:, None] * off_x * off_x + proj_rows[4][:, None] * off_y * off_y) - proj_rows[3][:, None] * off_x * off_y
    alpha_px = (proj_rows[5] * live_mask)[:, None] * jnp.exp(exponent)
    fade_log = jnp.log1p(-alpha_px)
    before_log = jnp.cumsum(fade_log, axis=0) - fade_log
    weights = alpha_px * jnp.exp(before_log)
    return jnp.dot(proj_rows[6:9], weights, precision=lax.Precision.HIGHEST)

def reference(params, adam_m, adam_v, cameras, exposure, entry_owner, entry_local, block_counts, tile_view, tile_spot, d_image):
    across = IMG_W // TILE
    pixel_ids = jnp.arange(TPIX, dtype=jnp.int32)
    slot_block = jnp.arange(SLOTS, dtype=jnp.int32) // BLOCK

    def tile_step(tile_idx, carried):
        gradient, expo_sum = carried
        gauss_ids = (lax.dynamic_index_in_dim(entry_owner, tile_idx, 0, keepdims=False) * G_DEV + lax.dynamic_index_in_dim(entry_local, tile_idx, 0, keepdims=False)).astype(jnp.int32)
        raw_rows = jnp.take(params, gauss_ids, axis=1)
        view_index = lax.dynamic_index_in_dim(tile_view, tile_idx, 0, keepdims=False)
        camera_col = lax.dynamic_index_in_dim(cameras, view_index, 0, keepdims=False)[:, None]
        gain_vec = lax.dynamic_index_in_dim(exposure, view_index, 0, keepdims=False)
        spot_index = lax.dynamic_index_in_dim(tile_spot, tile_idx, 0, keepdims=False)
        pix_x = (spot_index % across * TILE + pixel_ids % TILE).astype(jnp.float32) + 0.5
        pix_y = (spot_index // across * TILE + pixel_ids // TILE).astype(jnp.float32) + 0.5
        count_here = lax.dynamic_index_in_dim(block_counts, tile_idx, 0, keepdims=False)
        live_mask = (slot_block < count_here).astype(jnp.float32)

        def tile_image(rows_in, gains_in):
            return gains_in[:, None] * render(project(rows_in, camera_col), live_mask, pix_x, pix_y)
        rendered, pullback = jax.vjp(tile_image, raw_rows, gain_vec)
        grad_rows, grad_gain = pullback(lax.dynamic_index_in_dim(d_image, tile_idx, 0, keepdims=False))
        gradient = gradient.at[:, gauss_ids].add(grad_rows)
        expo_sum = expo_sum.at[view_index].add(grad_gain)
        return (gradient, expo_sum)
    initial = (jnp.zeros(params.shape, jnp.float32), jnp.zeros(exposure.shape, jnp.float32))
    gradient, expo_sum = lax.fori_loop(0, NTILES, tile_step, initial)
    new_m = beta_first * adam_m + (1.0 - beta_first) * gradient
    new_v = beta_second * adam_v + (1.0 - beta_second) * gradient * gradient
    new_params = params - learn_rate * (new_m / fix_first) / (jnp.sqrt(new_v / fix_second) + adam_eps)
    exposure_grad = expo_sum / NDEV
    return (new_params, new_m, new_v, exposure_grad)
```

```python
import jax
import jax.numpy as jnp
from jax import lax
from jax.experimental import pallas as pl
from jax.experimental.pallas import tpu as pltpu
from jax.sharding import PartitionSpec as P

AXES = ("tiles", "gauss")
DEVS = 128
CAP = 48
TILES = 4
SLOTS = 1024
BLOCK = 256
NBLK = 4
TPIX = 256
TILE = 16
ACROSS = 240
IMG_W = 3840
IMG_H = 2160
PARAMS = 59
GDEV = 16384
HALF = GDEV // 2
VALS = 9
USED = CAP * VALS
WIDE = 512
TABLES = 4
UNROLL = 16

sh_c0 = 0.28209479177387814
sh_c1 = 0.4886025119029199
sh_c2 = (
    1.0925484305920792,
    -1.0925484305920792,
    0.31539156525252005,
    -1.0925484305920792,
    0.5462742152960396,
)
sh_c3 = (
    -0.5900435899266435,
    2.890611442640554,
    -0.4570457994644658,
    0.3731763325901154,
    -0.4570457994644658,
    1.445305721320277,
    -0.5900435899266435,
)
beta_first = 0.9
beta_second = 0.999
learn_rate = 0.01
adam_eps = 1e-08
fix_first = 1.0
fix_second = 0.632304575229036
blur_add = 0.3

F32 = jnp.float32
BF16 = jnp.bfloat16


def sh_color(coefficients, unit_x, unit_y, unit_z):
    square_x = unit_x * unit_x
    square_y = unit_y * unit_y
    square_z = unit_z * unit_z
    basis_list = [
        -sh_c1 * unit_y,
        sh_c1 * unit_z,
        -sh_c1 * unit_x,
        sh_c2[0] * unit_x * unit_y,
        sh_c2[1] * unit_y * unit_z,
        sh_c2[2] * (2.0 * square_z - square_x - square_y),
        sh_c2[3] * unit_x * unit_z,
        sh_c2[4] * (square_x - square_y),
        sh_c3[0] * unit_y * (3.0 * square_x - square_y),
        sh_c3[1] * unit_x * unit_y * unit_z,
        sh_c3[2] * unit_y * (4.0 * square_z - square_x - square_y),
        sh_c3[3] * unit_z * (2.0 * square_z - 3.0 * square_x - 3.0 * square_y),
        sh_c3[4] * unit_x * (4.0 * square_z - square_x - square_y),
        sh_c3[5] * unit_z * (square_x - square_y),
        sh_c3[6] * unit_x * (square_x - 3.0 * square_y),
    ]
    colors = []
    for channel in range(3):
        summed = 0.5 + sh_c0 * coefficients[channel]
        for index_k in range(15):
            summed = summed + basis_list[index_k] * coefficients[3 * (index_k + 1) + channel]
        colors.append(jnp.maximum(summed, 0.0))
    return colors


def project(values, camera):
    points = [values[0], values[1], values[2]]
    matrix = [[camera[3 * row_at + col_at] for col_at in range(3)] for row_at in range(3)]
    translation = [camera[9], camera[10], camera[11]]
    focal_len = camera[12]
    viewed = [
        matrix[row_at][0] * points[0]
        + matrix[row_at][1] * points[1]
        + matrix[row_at][2] * points[2]
        + translation[row_at]
        for row_at in range(3)
    ]
    inverse_depth = 1.0 / viewed[2]
    screen_x = focal_len * viewed[0] * inverse_depth + 0.5 * IMG_W
    screen_y = focal_len * viewed[1] * inverse_depth + 0.5 * IMG_H
    slope_x = focal_len * viewed[0] * inverse_depth * inverse_depth
    slope_y = focal_len * viewed[1] * inverse_depth * inverse_depth
    jac_w = [
        [
            focal_len * inverse_depth * matrix[0][col_at] - slope_x * matrix[2][col_at]
            for col_at in range(3)
        ],
        [
            focal_len * inverse_depth * matrix[1][col_at] - slope_y * matrix[2][col_at]
            for col_at in range(3)
        ],
    ]
    quat_len = jnp.sqrt(
        values[6] * values[6]
        + values[7] * values[7]
        + values[8] * values[8]
        + values[9] * values[9]
    )
    quat_w = values[6] / quat_len
    quat_x = values[7] / quat_len
    quat_y = values[8] / quat_len
    quat_z = values[9] / quat_len
    rotation = [
        [
            1.0 - 2.0 * (quat_y * quat_y + quat_z * quat_z),
            2.0 * (quat_x * quat_y - quat_w * quat_z),
            2.0 * (quat_x * quat_z + quat_w * quat_y),
        ],
        [
            2.0 * (quat_x * quat_y + quat_w * quat_z),
            1.0 - 2.0 * (quat_x * quat_x + quat_z * quat_z),
            2.0 * (quat_y * quat_z - quat_w * quat_x),
        ],
        [
            2.0 * (quat_x * quat_z - quat_w * quat_y),
            2.0 * (quat_y * quat_z + quat_w * quat_x),
            1.0 - 2.0 * (quat_x * quat_x + quat_y * quat_y),
        ],
    ]
    extent = [jnp.exp(values[3]), jnp.exp(values[4]), jnp.exp(values[5])]
    spread = [
        [
            (
                jac_w[row_at][0] * rotation[0][col_at]
                + jac_w[row_at][1] * rotation[1][col_at]
                + jac_w[row_at][2] * rotation[2][col_at]
            )
            * extent[col_at]
            for col_at in range(3)
        ]
        for row_at in range(2)
    ]
    cov_a = (
        spread[0][0] * spread[0][0]
        + spread[0][1] * spread[0][1]
        + spread[0][2] * spread[0][2]
        + blur_add
    )
    cov_b = spread[0][0] * spread[1][0] + spread[0][1] * spread[1][1] + spread[0][2] * spread[1][2]
    cov_c = (
        spread[1][0] * spread[1][0]
        + spread[1][1] * spread[1][1]
        + spread[1][2] * spread[1][2]
        + blur_add
    )
    determinant = cov_a * cov_c - cov_b * cov_b
    logit = values[10]
    log_opacity = jnp.minimum(logit, 0.0) - jnp.log(1.0 + jnp.exp(-jnp.abs(logit)))
    center = [
        -(
            matrix[0][col_at] * translation[0]
            + matrix[1][col_at] * translation[1]
            + matrix[2][col_at] * translation[2]
        )
        for col_at in range(3)
    ]
    offset = [points[col_at] - center[col_at] for col_at in range(3)]
    distance = jnp.sqrt(offset[0] * offset[0] + offset[1] * offset[1] + offset[2] * offset[2])
    colors = sh_color(
        values[11:PARAMS], offset[0] / distance, offset[1] / distance, offset[2] / distance
    )
    return [
        screen_x,
        screen_y,
        cov_c / determinant,
        -cov_b / determinant,
        cov_a / determinant,
        log_opacity,
    ] + colors


def iota(shape, dim):
    return lax.broadcasted_iota(jnp.int32, shape, dim)


def mxu(left, right):
    return jnp.dot(left, right, preferred_element_type=F32)


def mxu_bt(left, right):
    return lax.dot_general(left, right, (((1,), (1,)), ((), ())), preferred_element_type=F32)


def split_two(value):
    high = value.astype(BF16)
    low = (value - high.astype(F32)).astype(BF16)
    return high, low


def split_three(value):
    high = value.astype(BF16).astype(F32)
    rest = value - high
    middle = rest.astype(BF16).astype(F32)
    low = (rest - middle).astype(BF16).astype(F32)
    return high, middle, low


def upper_strict():
    return (iota((BLOCK, BLOCK), 0) < iota((BLOCK, BLOCK), 1)).astype(F32).astype(BF16)


def route_kernel(view_ref, count_ref, owner_ref, local_ref, req_ref, entry_ref):
    tri = upper_strict()
    owners_at = iota((DEVS, BLOCK), 0)
    ranks_at = iota((DEVS, BLOCK), 0)
    before = jnp.zeros((DEVS, 1), F32)
    total_hi = jnp.zeros((DEVS, DEVS), F32)
    total_lo = jnp.zeros((DEVS, DEVS), F32)
    for tile in range(TILES):
        view = view_ref[tile]
        for block in range(NBLK):
            alive = block < count_ref[tile]
            span = slice(block * BLOCK, (block + 1) * BLOCK)
            owner = jnp.where(alive, owner_ref[tile : tile + 1, span], -1)
            local = local_ref[tile : tile + 1, span]
            hit = owners_at == owner
            one_hot = hit.astype(F32)
            one_hot_b = one_hot.astype(BF16)
            earlier = mxu(one_hot_b, tri) + before
            rank = jnp.sum(one_hot * earlier, axis=0, keepdims=True)
            before = before + jnp.sum(one_hot, axis=1, keepdims=True)
            rank = jnp.where(owner >= 0, rank.astype(jnp.int32), -1)
            code = (
                view * GDEV
                + ((local >> 7) & 1) * HALF
                + ((local >> 8) << 7)
                + (local & 127)
                + 1
            )
            at_rank = ranks_at == rank
            high = jnp.where(at_rank, (code >> 8).astype(F32), 0.0).astype(BF16)
            low = jnp.where(at_rank, (code & 255).astype(F32), 0.0).astype(BF16)
            total_hi = total_hi + mxu_bt(one_hot_b, high)
            total_lo = total_lo + mxu_bt(one_hot_b, low)
            at = tile * NBLK + block
            entry_ref[at, 0:1, :] = owner
            entry_ref[at, 1:2, :] = rank
    req_ref[...] = (total_hi * 256.0 + total_lo).astype(jnp.int32) - 1


def route(tile_view, block_counts, entry_owner, entry_local):
    return pl.pallas_call(
        route_kernel,
        name="route",
        out_shape=(
            jax.ShapeDtypeStruct((DEVS, DEVS), jnp.int32),
            jax.ShapeDtypeStruct((TILES * NBLK, 8, BLOCK), jnp.int32),
        ),
        in_specs=[
            pl.BlockSpec(memory_space=pltpu.SMEM),
            pl.BlockSpec(memory_space=pltpu.SMEM),
            pl.BlockSpec(memory_space=pltpu.VMEM),
            pl.BlockSpec(memory_space=pltpu.VMEM),
        ],
        out_specs=(pl.BlockSpec(memory_space=pltpu.VMEM), pl.BlockSpec(memory_space=pltpu.VMEM)),
        compiler_params=pltpu.CompilerParams(vmem_limit_bytes=24 << 20),
    )(tile_view, block_counts, entry_owner, entry_local)


COLS = 2048


def table_kernel(params_ref, table_ref, pad_ref):
    @pl.when(pl.program_id(0) == 0)
    def _():
        pad_ref[...] = jnp.zeros_like(pad_ref)

    for at in range(COLS // 256):
        pad_ref[at, 0:PARAMS, :] = params_ref[:, at * 256 : at * 256 + 128]
        pad_ref[at, 64 : 64 + PARAMS, :] = params_ref[:, at * 256 + 128 : at * 256 + 256]
        table_ref[at * 128 : (at + 1) * 128, :] = pad_ref[at].T


def table_of(params):
    return pl.pallas_call(
        table_kernel,
        name="table",
        grid=(GDEV // COLS,),
        out_shape=jax.ShapeDtypeStruct((HALF, 128), F32),
        in_specs=[pl.BlockSpec((PARAMS, COLS), lambda i: (0, i))],
        out_specs=pl.BlockSpec((COLS // 2, 128), lambda i: (i, 0)),
        scratch_shapes=[pltpu.VMEM((COLS // 256, 128, 128), F32)],
        compiler_params=pltpu.CompilerParams(vmem_limit_bytes=24 << 20),
        cost_estimate=pl.CostEstimate(flops=1 << 20, bytes_accessed=9 << 20, transcendentals=0),
    )(params)


def cameras_of(camera_ref, view):
    return [
        jnp.where(
            view == 0,
            camera_ref[0, at],
            jnp.where(
                view == 1,
                camera_ref[1, at],
                jnp.where(view == 2, camera_ref[2, at], camera_ref[3, at]),
            ),
        )
        for at in range(13)
    ]


def reply_kernel(
    code_ref, camera_ref, code_vec_ref, table_ref, reply_ref, rows_ref, code_t_ref, got_ref, proj_ref
):
    code_t_ref[...] = code_vec_ref[...].T
    proj_ref[USED:WIDE, :] = jnp.zeros((WIDE - USED, DEVS), F32)

    def gather(rank, carry):
        for src in range(DEVS):
            row = code_ref[src, rank] & (HALF - 1)
            got_ref[src : src + 1, :] = table_ref[pl.ds(row, 1), :]
        both = got_ref[...].T
        half = (code_t_ref[pl.ds(rank, 1), :] >> 13) & 1
        picked = jnp.where(half == 0, both[0:64], both[64:128])
        for group in range(8):
            rows_ref[pl.ds(group * 8 * CAP + rank, 8, stride=CAP), :] = picked[
                group * 8 : (group + 1) * 8
            ]
        return carry

    lax.fori_loop(0, CAP, gather, 0)

    def chunk(at, carry):
        base = pl.multiple_of(at * 8, 8)
        values = [rows_ref[pl.ds(k * CAP + base, 8), :] for k in range(PARAMS)]
        view = (code_t_ref[pl.ds(base, 8), :] >> 14) & 3
        for k, value in enumerate(project(values, cameras_of(camera_ref, view))):
            proj_ref[pl.ds(k * CAP + base, 8), :] = value
        return carry

    lax.fori_loop(0, CAP // 8, chunk, 0)
    for part in range(WIDE // 128):
        span = slice(part * 128, (part + 1) * 128)
        reply_ref[:, span] = proj_ref[span, :].T


def reply_of(codes, cameras, table):
    return pl.pallas_call(
        reply_kernel,
        name="reply",
        out_shape=(
            jax.ShapeDtypeStruct((DEVS, WIDE), F32),
            jax.ShapeDtypeStruct((64 * CAP, DEVS), F32),
        ),
        in_specs=[
            pl.BlockSpec(memory_space=pltpu.SMEM),
            pl.BlockSpec(memory_space=pltpu.SMEM),
            pl.BlockSpec(memory_space=pltpu.VMEM),
            pl.BlockSpec(memory_space=pltpu.VMEM),
        ],
        out_specs=(pl.BlockSpec(memory_space=pltpu.VMEM), pl.BlockSpec(memory_space=pltpu.VMEM)),
        scratch_shapes=[
            pltpu.VMEM((DEVS, DEVS), jnp.int32),
            pltpu.VMEM((DEVS, 128), F32),
            pltpu.VMEM((WIDE, DEVS), F32),
        ],
        compiler_params=pltpu.CompilerParams(vmem_limit_bytes=32 << 20),
    )(codes, cameras, codes, table)


def render_kernel(
    view_ref,
    spot_ref,
    count_ref,
    gain_ref,
    d_image_ref,
    entry_ref,
    arrived_ref,
    back_ref,
    split_ref,
    tri_ref,
    low_ref,
    basis_t_ref,
    basis_ref,
    vals_ref,
    alpha_ref,
    q_ref,
    color_grad_ref,
    shade_ref,
):
    for part in range(WIDE // 128):
        span = slice(part * 128, (part + 1) * 128)
        flipped = arrived_ref[:, span].T
        for piece, value in enumerate(split_three(flipped)):
            split_ref[piece, span, :] = value.astype(BF16)
    tri_ref[...] = upper_strict()
    low_ref[...] = (
        (iota((BLOCK, BLOCK), 0) > iota((BLOCK, BLOCK), 1)).astype(F32).astype(BF16)
    )

    def monomial(which, x, y):
        return jnp.where(
            which == 0,
            1.0,
            jnp.where(
                which == 1,
                x,
                jnp.where(
                    which == 2,
                    y,
                    jnp.where(
                        which == 3,
                        x * x,
                        jnp.where(which == 4, x * y, jnp.where(which == 5, y * y, 0.0)),
                    ),
                ),
            ),
        )

    pixel = iota((TPIX, 128), 0)
    lane = iota((TPIX, 128), 1)
    basis_t_ref[...] = jnp.where(
        lane < 24,
        monomial(lane & 7, (pixel & 15).astype(F32) - 7.5, (pixel >> 4).astype(F32) - 7.5),
        0.0,
    ).astype(BF16)
    pixel = iota((16, TPIX), 1)
    basis_ref[...] = monomial(
        iota((16, TPIX), 0), (pixel & 15).astype(F32) - 7.5, (pixel >> 4).astype(F32) - 7.5
    ).astype(BF16)
    back_ref[...] = jnp.zeros_like(back_ref)
    owners_at = iota((DEVS, BLOCK), 0)
    ranks_at = iota((CAP, BLOCK), 0)
    row8 = iota((8, BLOCK), 0)

    def rows8(rows):
        out = jnp.zeros((8, BLOCK), F32)
        for at, row in enumerate(rows):
            out = jnp.where(row8 == at, row, out)
        return out

    def tile_step(tile, expo):
        view = view_ref[tile]
        spot = spot_ref[tile]
        line = spot // ACROSS
        mid_x = ((spot - line * ACROSS) * TILE + TILE // 2).astype(F32)
        mid_y = (line * TILE + TILE // 2).astype(F32)
        gains = [gain_ref[view, ch] for ch in range(3)]
        d_rows = [d_image_ref[tile, ch : ch + 1, :] for ch in range(3)]
        d_raw = rows8(d_rows)
        d1, d2, d3 = split_three(d_raw)
        pixel_rows = jnp.concatenate([d1, d2, d3, jnp.zeros((8, TPIX), F32)], axis=0).astype(BF16)
        g1, g2, g3 = split_three(rows8([gains[ch] * d_rows[ch] for ch in range(3)]))
        shade_ref[...] = (
            jnp.concatenate([g1, g1, g2, g2, g1, g3, jnp.zeros((80, TPIX), F32)], axis=0)
            .T.astype(BF16)
        )
        blocks = count_ref[tile]

        def forward(block, carried):
            level, expo_rows = carried
            at = tile * NBLK + block
            owner = entry_ref[at, 0:1, :]
            rank = entry_ref[at, 1:2, :]
            one_hot = (owners_at == owner).astype(F32).astype(BF16)
            found = (
                mxu(split_ref[0, 0:USED, :], one_hot)
                + mxu(split_ref[1, 0:USED, :], one_hot)
                + mxu(split_ref[2, 0:USED, :], one_hot)
            )
            here = ranks_at == rank
            vals = [
                jnp.sum(
                    jnp.where(here, found[k * CAP : (k + 1) * CAP], 0.0), axis=0, keepdims=True
                )
                for k in range(VALS)
            ]
            shift_x = vals[0] - mid_x
            shift_y = vals[1] - mid_y
            con_a, con_b, con_c = vals[2], vals[3], vals[4]
            lin_x = con_a * shift_x + con_b * shift_y
            lin_y = con_c * shift_y + con_b * shift_x
            poly = rows8(
                [
                    vals[5] - 0.5 * (lin_x * shift_x + lin_y * shift_y),
                    lin_x,
                    lin_y,
                    -0.5 * con_a,
                    -con_b,
                    -0.5 * con_c,
                ]
            )
            vals_ref[block] = rows8([shift_x, shift_y, con_a, con_b, con_c])
            k1, k2, k3 = split_three(poly)
            poly_rows = jnp.concatenate(
                [k1, k2, k3, jnp.zeros((104, BLOCK), F32)], axis=0
            ).astype(BF16)
            color = rows8(vals[6:9])
            c1, c2, c3 = split_three(color)
            color_rows = jnp.concatenate(
                [c1, c2, c1, c2, c3, c1, jnp.zeros((80, BLOCK), F32)], axis=0
            ).astype(BF16)
            alpha = jnp.exp(mxu(basis_t_ref[...], poly_rows))
            fade = alpha * (1.0 + alpha * (0.5 + alpha * (1.0 / 3.0)))
            fade_hi, fade_lo = split_two(fade)
            summed = mxu(fade_hi, tri_ref[...]) + mxu(fade_lo, tri_ref[...]) + level
            weight = alpha * jnp.exp(-summed)
            level = summed[:, BLOCK - 1 : BLOCK] + fade[:, BLOCK - 1 : BLOCK]
            q_val = mxu(shade_ref[...], color_rows) * weight
            alpha_ref[block] = alpha
            q_ref[block] = q_val
            weight_hi, weight_lo = split_two(weight)
            seen = mxu(pixel_rows, weight_hi) + mxu(pixel_rows, weight_lo)
            seen = seen[0:8] + seen[8:16] + seen[16:24]
            color_grad_ref[block] = seen
            return level, expo_rows + color * seen

        level0 = jnp.zeros((TPIX, 1), F32)
        unused, expo_rows = lax.fori_loop(
            0, blocks, forward, (level0, jnp.zeros((8, BLOCK), F32))
        )
        expo_cols = jnp.sum(expo_rows, axis=1, keepdims=True)

        def backward(step, tail):
            block = blocks - 1 - step
            at = tile * NBLK + block
            owner = entry_ref[at, 0:1, :]
            rank = entry_ref[at, 1:2, :]
            alpha = alpha_ref[block]
            q_val = q_ref[block]
            q_hi, q_lo = split_two(q_val)
            later = mxu(q_hi, low_ref[...]) + mxu(q_lo, low_ref[...]) + tail
            d_exp = q_val - later * (alpha * (1.0 + alpha * (1.0 + alpha)))
            tail = later[:, 0:1] + q_val[:, 0:1]
            d_hi, d_lo = split_two(d_exp)
            grad = mxu(basis_ref[...], d_hi) + mxu(basis_ref[...], d_lo)
            d_poly = [grad[k : k + 1] for k in range(6)]
            held = vals_ref[block]
            shift_x, shift_y, con_a, con_b, con_c = [held[k : k + 1] for k in range(5)]
            lin_x = con_a * shift_x + con_b * shift_y
            lin_y = con_c * shift_y + con_b * shift_x
            seen = color_grad_ref[block]
            grads = [
                d_poly[1] * con_a + d_poly[2] * con_b - d_poly[0] * lin_x,
                d_poly[1] * con_b + d_poly[2] * con_c - d_poly[0] * lin_y,
                shift_x * d_poly[1] - 0.5 * (d_poly[3] + shift_x * shift_x * d_poly[0]),
                shift_y * d_poly[1]
                + shift_x * d_poly[2]
                - d_poly[4]
                - shift_x * shift_y * d_poly[0],
                shift_y * d_poly[2] - 0.5 * (d_poly[5] + shift_y * shift_y * d_poly[0]),
                d_poly[0],
                gains[0] * seen[0:1],
                gains[1] * seen[1:2],
                gains[2] * seen[2:3],
            ]
            one_hot = (owners_at == owner).astype(F32).astype(BF16)
            here = ranks_at == rank
            high_rows = []
            low_rows = []
            for value in grads:
                high = value.astype(BF16).astype(F32)
                high_rows.append(jnp.where(here, high, 0.0).astype(BF16))
                low_rows.append(jnp.where(here, value - high, 0.0).astype(BF16))
            back_ref[:, 0:USED] += mxu_bt(one_hot, jnp.concatenate(high_rows, axis=0)) + mxu_bt(
                one_hot, jnp.concatenate(low_rows, axis=0)
            )
            return tail

        lax.fori_loop(0, blocks, backward, jnp.zeros((TPIX, 1), F32))
        lane_at = iota((8, 128), 1) - (USED - 384) - 3 * view
        return expo + jnp.where(lane_at == iota((8, 128), 0), expo_cols, 0.0)

    expo = lax.fori_loop(0, TILES, tile_step, jnp.zeros((8, 128), F32))
    lane = iota((8, 128), 1)
    expo = jnp.where((lane >= USED - 384) & (lane < USED - 384 + 12), expo, 0.0)
    back_ref[:, 384:WIDE] += jnp.sum(expo, axis=0, keepdims=True)


def render_of(tile_view, tile_spot, block_counts, exposure, d_image, entries, arrived):
    smem = pl.BlockSpec(memory_space=pltpu.SMEM)
    vmem = pl.BlockSpec(memory_space=pltpu.VMEM)
    return pl.pallas_call(
        render_kernel,
        name="render",
        out_shape=jax.ShapeDtypeStruct((DEVS, WIDE), F32),
        in_specs=[smem, smem, smem, smem, vmem, vmem, vmem],
        out_specs=vmem,
        scratch_shapes=[
            pltpu.VMEM((3, WIDE, DEVS), BF16),
            pltpu.VMEM((BLOCK, BLOCK), BF16),
            pltpu.VMEM((BLOCK, BLOCK), BF16),
            pltpu.VMEM((TPIX, 128), BF16),
            pltpu.VMEM((16, TPIX), BF16),
            pltpu.VMEM((NBLK, 8, BLOCK), F32),
            pltpu.VMEM((NBLK, TPIX, BLOCK), F32),
            pltpu.VMEM((NBLK, TPIX, BLOCK), F32),
            pltpu.VMEM((NBLK, 8, BLOCK), F32),
            pltpu.VMEM((TPIX, 128), BF16),
        ],
        compiler_params=pltpu.CompilerParams(vmem_limit_bytes=32 << 20),
    )(tile_view, tile_spot, block_counts, exposure, d_image, entries, arrived)


def collect_kernel(
    code_ref,
    camera_ref,
    code_vec_ref,
    arrived_ref,
    rows_ref,
    total_ref,
    expo_ref,
    code_t_ref,
    cot_ref,
    grad_ref,
    spread_ref,
    *tables,
):
    code_t_ref[...] = code_vec_ref[...].T
    expo_ref[...] = jnp.broadcast_to(
        jnp.sum(arrived_ref[:, 384:WIDE], axis=0, keepdims=True), (8, 128)
    )
    for part in range(WIDE // 128):
        span = slice(part * 128, (part + 1) * 128)
        cot_ref[span, :] = arrived_ref[:, span].T
    for table in tables:
        table[...] = jnp.zeros_like(table)
    grad_ref[PARAMS * CAP :, :] = jnp.zeros(((64 - PARAMS) * CAP, DEVS), F32)

    def chunk(at, carry):
        base = pl.multiple_of(at * 8, 8)
        values = [rows_ref[pl.ds(k * CAP + base, 8), :] for k in range(PARAMS)]
        code = code_t_ref[pl.ds(base, 8), :]
        camera = cameras_of(camera_ref, (code >> 14) & 3)
        unused, pull = jax.vjp(lambda held: project(held, camera), values)
        (grads,) = pull([cot_ref[pl.ds(k * CAP + base, 8), :] for k in range(VALS)])
        for k in range(PARAMS):
            grad_ref[pl.ds(k * CAP + base, 8), :] = jnp.where(code >= 0, grads[k], 0.0)
        return carry

    lax.fori_loop(0, CAP // 8, chunk, 0)

    def scatter(rank, carry):
        half = (code_t_ref[pl.ds(rank, 1), :] >> 13) & 1
        mine = jnp.concatenate(
            [
                grad_ref[pl.ds(group * 8 * CAP + rank, 8, stride=CAP), :]
                for group in range(8)
            ],
            axis=0,
        )
        both = jnp.concatenate(
            [jnp.where(half == 0, mine, 0.0), jnp.where(half == 1, mine, 0.0)], axis=0
        )
        spread_ref[...] = both.T
        for src in range(DEVS):
            row = code_ref[src, rank] & (HALF - 1)
            table = tables[src % TABLES]
            table[pl.ds(row, 1), :] = table[pl.ds(row, 1), :] + spread_ref[src : src + 1, :]
        return carry

    lax.fori_loop(0, CAP, scatter, 0)

    def merge(at, carry):
        span = pl.ds(pl.multiple_of(at * 128, 128), 128)
        total = tables[0][span, :]
        for table in tables[1:]:
            total = total + table[span, :]
        total_ref[span, :] = total
        return carry

    lax.fori_loop(0, HALF // 128, merge, 0)


def collect_of(codes, cameras, arrived, rows):
    smem = pl.BlockSpec(memory_space=pltpu.SMEM)
    vmem = pl.BlockSpec(memory_space=pltpu.VMEM)
    return pl.pallas_call(
        collect_kernel,
        name="collect",
        out_shape=(
            jax.ShapeDtypeStruct((HALF, 128), F32),
            jax.ShapeDtypeStruct((8, 128), F32),
        ),
        in_specs=[smem, smem, vmem, vmem, vmem],
        out_specs=(vmem, vmem),
        scratch_shapes=[
            pltpu.VMEM((DEVS, DEVS), jnp.int32),
            pltpu.VMEM((WIDE, DEVS), F32),
            pltpu.VMEM((64 * CAP, DEVS), F32),
            pltpu.VMEM((DEVS, 128), F32),
        ]
        + [pltpu.VMEM((HALF, 128), F32)] * TABLES,
        compiler_params=pltpu.CompilerParams(vmem_limit_bytes=48 << 20),
    )(codes, cameras, codes, arrived, rows)


def adam_kernel(total_ref, params_ref, m_ref, v_ref, params_out, m_out, v_out, flip_ref):
    for at in range(COLS // 256):
        flip_ref[at] = total_ref[at * 128 : (at + 1) * 128, :].T
        for half in range(2):
            span = slice(at * 256 + half * 128, at * 256 + (half + 1) * 128)
            gradient = flip_ref[at, half * 64 : half * 64 + PARAMS, :]
            new_m = beta_first * m_ref[:, span] + (1.0 - beta_first) * gradient
            new_v = beta_second * v_ref[:, span] + (1.0 - beta_second) * gradient * gradient
            m_out[:, span] = new_m
            v_out[:, span] = new_v
            params_out[:, span] = params_ref[:, span] - learn_rate * (new_m / fix_first) / (
                jnp.sqrt(new_v / fix_second) + adam_eps
            )


def adam_of(total, params, adam_m, adam_v):
    wide = pl.BlockSpec((PARAMS, COLS), lambda i: (0, i))
    return pl.pallas_call(
        adam_kernel,
        name="adam",
        grid=(GDEV // COLS,),
        out_shape=(jax.ShapeDtypeStruct((PARAMS, GDEV), F32),) * 3,
        in_specs=[pl.BlockSpec((COLS // 2, 128), lambda i: (i, 0)), wide, wide, wide],
        out_specs=(wide, wide, wide),
        scratch_shapes=[pltpu.VMEM((COLS // 256, 128, 128), F32)],
        compiler_params=pltpu.CompilerParams(vmem_limit_bytes=32 << 20),
    )(total, params, adam_m, adam_v)


def exchange(value):
    return lax.all_to_all(value, AXES, split_axis=0, concat_axis=0, tiled=True)


def body(
    params,
    adam_m,
    adam_v,
    cameras,
    exposure,
    entry_owner,
    entry_local,
    block_counts,
    tile_view,
    tile_spot,
    d_image,
):
    requests, entries = route(tile_view, block_counts, entry_owner, entry_local)
    codes = exchange(requests)
    table = table_of(params)
    reply, rows = reply_of(codes, cameras, table)
    arrived = exchange(reply)
    back = render_of(tile_view, tile_spot, block_counts, exposure, d_image, entries, arrived)
    returned = exchange(back)
    total, expo = collect_of(codes, cameras, returned, rows)
    new_params, new_m, new_v = adam_of(total, params, adam_m, adam_v)
    first = USED - 384
    exposure_grad = expo[0, first : first + 12].reshape(4, 3) / DEVS
    return (new_params, new_m, new_v, exposure_grad)


def solution(mesh):
    both = ("tiles", "gauss")
    placed = (
        P(None, both),
        P(None, both),
        P(None, both),
        P(),
        P(),
        P(both, None),
        P(both, None),
        P(both),
        P(both),
        P(both),
        P(both, None, None),
    )
    return jax.shard_map(
        body,
        mesh=mesh,
        in_specs=placed,
        out_specs=(P(None, both), P(None, both), P(None, both), P()),
        check_vma=False,
    )
```

```python
import jax
import jax.numpy as jnp
from jax import lax
from jax.experimental import pallas as pl
from jax.experimental.pallas import tpu as pltpu
from jax.sharding import PartitionSpec as P

AXES = ("tiles", "gauss")
DEVS = 128
CAP = 48
TILES = 4
SLOTS = 1024
BLOCK = 256
NBLK = 4
TPIX = 256
TILE = 16
ACROSS = 240
IMG_W = 3840
IMG_H = 2160
PARAMS = 59
GDEV = 16384
HALF = GDEV // 2
VALS = 9
USED = CAP * VALS
WIDE = 512
TABLES = 4
UNROLL = 16

sh_c0 = 0.28209479177387814
sh_c1 = 0.4886025119029199
sh_c2 = (
    1.0925484305920792,
    -1.0925484305920792,
    0.31539156525252005,
    -1.0925484305920792,
    0.5462742152960396,
)
sh_c3 = (
    -0.5900435899266435,
    2.890611442640554,
    -0.4570457994644658,
    0.3731763325901154,
    -0.4570457994644658,
    1.445305721320277,
    -0.5900435899266435,
)
beta_first = 0.9
beta_second = 0.999
learn_rate = 0.01
adam_eps = 1e-08
fix_first = 1.0
fix_second = 0.632304575229036
blur_add = 0.3

F32 = jnp.float32
BF16 = jnp.bfloat16


def sh_color(coefficients, unit_x, unit_y, unit_z):
    square_x = unit_x * unit_x
    square_y = unit_y * unit_y
    square_z = unit_z * unit_z
    basis_list = [
        -sh_c1 * unit_y,
        sh_c1 * unit_z,
        -sh_c1 * unit_x,
        sh_c2[0] * unit_x * unit_y,
        sh_c2[1] * unit_y * unit_z,
        sh_c2[2] * (2.0 * square_z - square_x - square_y),
        sh_c2[3] * unit_x * unit_z,
        sh_c2[4] * (square_x - square_y),
        sh_c3[0] * unit_y * (3.0 * square_x - square_y),
        sh_c3[1] * unit_x * unit_y * unit_z,
        sh_c3[2] * unit_y * (4.0 * square_z - square_x - square_y),
        sh_c3[3] * unit_z * (2.0 * square_z - 3.0 * square_x - 3.0 * square_y),
        sh_c3[4] * unit_x * (4.0 * square_z - square_x - square_y),
        sh_c3[5] * unit_z * (square_x - square_y),
        sh_c3[6] * unit_x * (square_x - 3.0 * square_y),
    ]
    colors = []
    for channel in range(3):
        summed = 0.5 + sh_c0 * coefficients[channel]
        for index_k in range(15):
            summed = summed + basis_list[index_k] * coefficients[3 * (index_k + 1) + channel]
        colors.append(jnp.maximum(summed, 0.0))
    return colors


def project(values, camera):
    points = [values[0], values[1], values[2]]
    matrix = [[camera[3 * row_at + col_at] for col_at in range(3)] for row_at in range(3)]
    translation = [camera[9], camera[10], camera[11]]
    focal_len = camera[12]
    viewed = [
        matrix[row_at][0] * points[0]
        + matrix[row_at][1] * points[1]
        + matrix[row_at][2] * points[2]
        + translation[row_at]
        for row_at in range(3)
    ]
    inverse_depth = 1.0 / viewed[2]
    screen_x = focal_len * viewed[0] * inverse_depth + 0.5 * IMG_W
    screen_y = focal_len * viewed[1] * inverse_depth + 0.5 * IMG_H
    slope_x = focal_len * viewed[0] * inverse_depth * inverse_depth
    slope_y = focal_len * viewed[1] * inverse_depth * inverse_depth
    jac_w = [
        [
            focal_len * inverse_depth * matrix[0][col_at] - slope_x * matrix[2][col_at]
            for col_at in range(3)
        ],
        [
            focal_len * inverse_depth * matrix[1][col_at] - slope_y * matrix[2][col_at]
            for col_at in range(3)
        ],
    ]
    quat_len = jnp.sqrt(
        values[6] * values[6]
        + values[7] * values[7]
        + values[8] * values[8]
        + values[9] * values[9]
    )
    quat_w = values[6] / quat_len
    quat_x = values[7] / quat_len
    quat_y = values[8] / quat_len
    quat_z = values[9] / quat_len
    rotation = [
        [
            1.0 - 2.0 * (quat_y * quat_y + quat_z * quat_z),
            2.0 * (quat_x * quat_y - quat_w * quat_z),
            2.0 * (quat_x * quat_z + quat_w * quat_y),
        ],
        [
            2.0 * (quat_x * quat_y + quat_w * quat_z),
            1.0 - 2.0 * (quat_x * quat_x + quat_z * quat_z),
            2.0 * (quat_y * quat_z - quat_w * quat_x),
        ],
        [
            2.0 * (quat_x * quat_z - quat_w * quat_y),
            2.0 * (quat_y * quat_z + quat_w * quat_x),
            1.0 - 2.0 * (quat_x * quat_x + quat_y * quat_y),
        ],
    ]
    extent = [jnp.exp(values[3]), jnp.exp(values[4]), jnp.exp(values[5])]
    spread = [
        [
            (
                jac_w[row_at][0] * rotation[0][col_at]
                + jac_w[row_at][1] * rotation[1][col_at]
                + jac_w[row_at][2] * rotation[2][col_at]
            )
            * extent[col_at]
            for col_at in range(3)
        ]
        for row_at in range(2)
    ]
    cov_a = (
        spread[0][0] * spread[0][0]
        + spread[0][1] * spread[0][1]
        + spread[0][2] * spread[0][2]
        + blur_add
    )
    cov_b = spread[0][0] * spread[1][0] + spread[0][1] * spread[1][1] + spread[0][2] * spread[1][2]
    cov_c = (
        spread[1][0] * spread[1][0]
        + spread[1][1] * spread[1][1]
        + spread[1][2] * spread[1][2]
        + blur_add
    )
    determinant = cov_a * cov_c - cov_b * cov_b
    logit = values[10]
    log_opacity = jnp.minimum(logit, 0.0) - jnp.log(1.0 + jnp.exp(-jnp.abs(logit)))
    center = [
        -(
            matrix[0][col_at] * translation[0]
            + matrix[1][col_at] * translation[1]
            + matrix[2][col_at] * translation[2]
        )
        for col_at in range(3)
    ]
    offset = [points[col_at] - center[col_at] for col_at in range(3)]
    distance = jnp.sqrt(offset[0] * offset[0] + offset[1] * offset[1] + offset[2] * offset[2])
    colors = sh_color(
        values[11:PARAMS], offset[0] / distance, offset[1] / distance, offset[2] / distance
    )
    return [
        screen_x,
        screen_y,
        cov_c / determinant,
        -cov_b / determinant,
        cov_a / determinant,
        log_opacity,
    ] + colors


def iota(shape, dim):
    return lax.broadcasted_iota(jnp.int32, shape, dim)


def mxu(left, right):
    return jnp.dot(left, right, preferred_element_type=F32)


def mxu_bt(left, right):
    return lax.dot_general(left, right, (((1,), (1,)), ((), ())), preferred_element_type=F32)


def split_two(value):
    high = value.astype(BF16)
    low = (value - high.astype(F32)).astype(BF16)
    return high, low


def split_three(value):
    high = value.astype(BF16).astype(F32)
    rest = value - high
    middle = rest.astype(BF16).astype(F32)
    low = (rest - middle).astype(BF16).astype(F32)
    return high, middle, low


def upper_strict():
    return (iota((BLOCK, BLOCK), 0) < iota((BLOCK, BLOCK), 1)).astype(F32).astype(BF16)


def route_kernel(
    view_hbm,
    count_hbm,
    owner_hbm,
    local_hbm,
    req_ref,
    entry_ref,
    view_ref,
    count_ref,
    owner_ref,
    local_ref,
    sems,
):
    copies = [
        pltpu.make_async_copy(source, target, sems.at[at])
        for at, (source, target) in enumerate(
            (
                (view_hbm, view_ref),
                (count_hbm, count_ref),
                (owner_hbm, owner_ref),
                (local_hbm, local_ref),
            )
        )
    ]
    for copy in copies:
        copy.start()
    tri = upper_strict()
    for copy in copies:
        copy.wait()
    owners_at = iota((DEVS, BLOCK), 0)
    ranks_at = iota((DEVS, BLOCK), 0)
    before = jnp.zeros((DEVS, 1), F32)
    total_hi = jnp.zeros((DEVS, DEVS), F32)
    total_lo = jnp.zeros((DEVS, DEVS), F32)
    for tile in range(TILES):
        view = view_ref[tile]
        for block in range(NBLK):
            alive = block < count_ref[tile]
            span = slice(block * BLOCK, (block + 1) * BLOCK)
            owner = jnp.where(alive, owner_ref[tile : tile + 1, span], -1)
            local = local_ref[tile : tile + 1, span]
            one_hot = (owners_at == owner).astype(F32)
            one_hot_b = one_hot.astype(BF16)
            earlier = mxu(one_hot_b, tri) + before
            rank = jnp.sum(one_hot * earlier, axis=0, keepdims=True)
            before = before + jnp.sum(one_hot, axis=1, keepdims=True)
            rank = jnp.where(owner >= 0, rank.astype(jnp.int32), -1)
            code = (
                view * GDEV
                + ((local >> 7) & 1) * HALF
                + ((local >> 8) << 7)
                + (local & 127)
                + 1
            )
            at_rank = ranks_at == rank
            high = jnp.where(at_rank, (code >> 8).astype(F32), 0.0).astype(BF16)
            low = jnp.where(at_rank, (code & 255).astype(F32), 0.0).astype(BF16)
            total_hi = total_hi + mxu_bt(one_hot_b, high)
            total_lo = total_lo + mxu_bt(one_hot_b, low)
            entry_ref[0:1, tile * SLOTS + block * BLOCK : tile * SLOTS + (block + 1) * BLOCK] = owner
            entry_ref[1:2, tile * SLOTS + block * BLOCK : tile * SLOTS + (block + 1) * BLOCK] = rank
    code = (total_hi * 256.0 + total_lo).astype(jnp.int32) - 1
    req_ref[:, 0:64] = code[:, 0:64]
    req_ref[:, 64:128] = code[:, 0:64] & (HALF - 1)


def route(tile_view, block_counts, entry_owner, entry_local):
    hbm = pl.BlockSpec(memory_space=pltpu.HBM)
    vmem = pl.BlockSpec(memory_space=pltpu.VMEM)
    return pl.pallas_call(
        route_kernel,
        name="route",
        out_shape=(
            jax.ShapeDtypeStruct((DEVS, DEVS), jnp.int32),
            jax.ShapeDtypeStruct((8, TILES * SLOTS), jnp.int32),
        ),
        in_specs=[hbm, hbm, hbm, hbm],
        out_specs=(vmem, vmem),
        scratch_shapes=[
            pltpu.SMEM((TILES,), jnp.int32),
            pltpu.SMEM((TILES,), jnp.int32),
            pltpu.VMEM((TILES, SLOTS), jnp.int32),
            pltpu.VMEM((TILES, SLOTS), jnp.int32),
            pltpu.SemaphoreType.DMA((4,)),
        ],
        compiler_params=pltpu.CompilerParams(vmem_limit_bytes=16 << 20),
    )(tile_view, block_counts, entry_owner, entry_local)


COLS = 2048


def table_kernel(params_ref, table_ref, pad_ref):
    @pl.when(pl.program_id(0) == 0)
    def _():
        pad_ref[...] = jnp.zeros_like(pad_ref)

    for at in range(COLS // 256):
        pad_ref[at, 0:PARAMS, :] = params_ref[:, at * 256 : at * 256 + 128]
        pad_ref[at, 64 : 64 + PARAMS, :] = params_ref[:, at * 256 + 128 : at * 256 + 256]
        table_ref[at * 128 : (at + 1) * 128, :] = pad_ref[at].T


def table_of(params):
    return pl.pallas_call(
        table_kernel,
        name="table",
        grid=(GDEV // COLS,),
        out_shape=jax.ShapeDtypeStruct((HALF, 128), F32),
        in_specs=[pl.BlockSpec((PARAMS, COLS), lambda i: (0, i))],
        out_specs=pl.BlockSpec((COLS // 2, 128), lambda i: (i, 0)),
        scratch_shapes=[pltpu.VMEM((COLS // 256, 128, 128), F32)],
        compiler_params=pltpu.CompilerParams(vmem_limit_bytes=24 << 20),
        cost_estimate=pl.CostEstimate(flops=1 << 20, bytes_accessed=9 << 20, transcendentals=0),
    )(pltpu.with_memory_space_constraint(params, pltpu.HBM))


def cameras_of(camera_ref, view):
    return [
        jnp.where(
            view == 0,
            camera_ref[0, at],
            jnp.where(
                view == 1,
                camera_ref[1, at],
                jnp.where(view == 2, camera_ref[2, at], camera_ref[3, at]),
            ),
        )
        for at in range(13)
    ]


def reply_kernel(
    code_ref, camera_ref, code_vec_ref, table_ref, reply_ref, rows_ref, code_t_ref, got_ref, proj_ref
):
    code_t_ref[...] = code_vec_ref[...].T
    proj_ref[USED:WIDE, :] = jnp.zeros((WIDE - USED, DEVS), F32)

    def gather(rank, carry):
        for src in range(DEVS):
            row = code_ref[src, rank + 64]
            got_ref[src : src + 1, :] = table_ref[pl.ds(row, 1), :]
        both = got_ref[...].T
        half = (code_t_ref[pl.ds(rank, 1), :] >> 13) & 1
        picked = jnp.where(half == 0, both[0:64], both[64:128])
        for group in range(8):
            rows_ref[pl.ds(group * 8 * CAP + rank, 8, stride=CAP), :] = picked[
                group * 8 : (group + 1) * 8
            ]
        return carry

    lax.fori_loop(0, CAP, gather, 0)

    def chunk(at, carry):
        base = pl.multiple_of(at * 8, 8)
        values = [rows_ref[pl.ds(k * CAP + base, 8), :] for k in range(PARAMS)]
        view = (code_t_ref[pl.ds(base, 8), :] >> 14) & 3
        for k, value in enumerate(project(values, cameras_of(camera_ref, view))):
            proj_ref[pl.ds(k * CAP + base, 8), :] = value
        return carry

    lax.fori_loop(0, CAP // 8, chunk, 0)
    for part in range(WIDE // 128):
        span = slice(part * 128, (part + 1) * 128)
        reply_ref[:, span] = proj_ref[span, :].T


def reply_of(codes, cameras, table):
    return pl.pallas_call(
        reply_kernel,
        name="reply",
        out_shape=(
            jax.ShapeDtypeStruct((DEVS, WIDE), F32),
            jax.ShapeDtypeStruct((64 * CAP, DEVS), F32),
        ),
        in_specs=[
            pl.BlockSpec(memory_space=pltpu.SMEM),
            pl.BlockSpec(memory_space=pltpu.SMEM),
            pl.BlockSpec(memory_space=pltpu.VMEM),
            pl.BlockSpec(memory_space=pltpu.VMEM),
        ],
        out_specs=(pl.BlockSpec(memory_space=pltpu.VMEM), pl.BlockSpec(memory_space=pltpu.VMEM)),
        scratch_shapes=[
            pltpu.VMEM((DEVS, DEVS), jnp.int32),
            pltpu.VMEM((DEVS, 128), F32),
            pltpu.VMEM((WIDE, DEVS), F32),
        ],
        compiler_params=pltpu.CompilerParams(vmem_limit_bytes=32 << 20),
    )(codes, cameras, codes, table)


def render_kernel(
    view_ref,
    spot_ref,
    gain_ref,
    d_image_ref,
    entry_ref,
    arrived_ref,
    back_ref,
    split_ref,
    tri_ref,
    low_ref,
    basis_t_ref,
    basis_ref,
    alpha_ref,
    q_ref,
    shade_ref,
    sum_ref,
):
    for part in range(WIDE // 128):
        span = slice(part * 128, (part + 1) * 128)
        flipped = arrived_ref[:, span].T
        for piece, value in enumerate(split_three(flipped)):
            split_ref[span, piece * 128 : (piece + 1) * 128] = value.astype(BF16)
    upper = upper_strict()
    lower = (iota((BLOCK, BLOCK), 0) > iota((BLOCK, BLOCK), 1)).astype(F32).astype(BF16)
    tri_ref[0:BLOCK, :] = upper
    tri_ref[BLOCK : 2 * BLOCK, :] = upper
    low_ref[0:BLOCK, :] = lower
    low_ref[BLOCK : 2 * BLOCK, :] = lower

    def monomial(which, x, y):
        return jnp.where(
            which == 0,
            1.0,
            jnp.where(
                which == 1,
                x,
                jnp.where(
                    which == 2,
                    y,
                    jnp.where(
                        which == 3,
                        x * x,
                        jnp.where(which == 4, x * y, jnp.where(which == 5, y * y, 0.0)),
                    ),
                ),
            ),
        )

    pixel = iota((TPIX, 128), 0)
    lane = iota((TPIX, 128), 1)
    basis_t_ref[...] = jnp.where(
        lane < 24,
        monomial(lane & 7, (pixel & 15).astype(F32) - 7.5, (pixel >> 4).astype(F32) - 7.5),
        0.0,
    ).astype(BF16)
    pixel = iota((16, TPIX), 1)
    basis = monomial(
        iota((16, TPIX), 0), (pixel & 15).astype(F32) - 7.5, (pixel >> 4).astype(F32) - 7.5
    ).astype(BF16)
    basis_ref[:, 0:TPIX] = basis
    basis_ref[:, TPIX : 2 * TPIX] = basis
    sum_ref[...] = jnp.zeros_like(sum_ref)

    def rows8(rows):
        at_row = iota((8, rows[0].shape[1]), 0)
        out = jnp.zeros((8, rows[0].shape[1]), F32)
        for at, row in enumerate(rows):
            out = jnp.where(at_row == at, row, out)
        return out

    def tile_step(tile, expo):
        view = view_ref[tile]
        spot = spot_ref[tile]
        line = spot // ACROSS
        mid_x = ((spot - line * ACROSS) * TILE + TILE // 2).astype(F32)
        mid_y = (line * TILE + TILE // 2).astype(F32)
        gains = [gain_ref[view, ch] for ch in range(3)]
        d_rows = [d_image_ref[tile, ch : ch + 1, :] for ch in range(3)]
        d1, d2, d3 = split_three(rows8(d_rows))
        pixel_rows = jnp.concatenate([d1, d2, d3, jnp.zeros((8, TPIX), F32)], axis=0).astype(BF16)
        pixel_rows = jnp.concatenate([pixel_rows, pixel_rows], axis=1)
        g1, g2, g3 = split_three(rows8([gains[ch] * d_rows[ch] for ch in range(3)]))
        shade_ref[...] = (
            jnp.concatenate([g1, g1, g2, g2, g1, g3, jnp.zeros((80, TPIX), F32)], axis=0)
            .T.astype(BF16)
        )
        slots = pl.ds(pl.multiple_of(tile * SLOTS, SLOTS), SLOTS)
        owner = entry_ref[0:1, slots]
        rank = entry_ref[1:2, slots]
        one_hot = (iota((DEVS, SLOTS), 0) == owner).astype(F32).astype(BF16)
        found = mxu(
            split_ref[0:USED, :], jnp.concatenate([one_hot, one_hot, one_hot], axis=0)
        )
        here = iota((CAP, SLOTS), 0) == rank
        vals = [
            jnp.sum(jnp.where(here, found[k * CAP : (k + 1) * CAP], 0.0), axis=0, keepdims=True)
            for k in range(VALS)
        ]
        shift_x = vals[0] - mid_x
        shift_y = vals[1] - mid_y
        con_a, con_b, con_c = vals[2], vals[3], vals[4]
        lin_x = con_a * shift_x + con_b * shift_y
        lin_y = con_c * shift_y + con_b * shift_x
        level_row = vals[5] - 0.5 * (lin_x * shift_x + lin_y * shift_y)
        poly = rows8(
            [
                jnp.where(owner >= 0, level_row, -200.0),
                lin_x,
                lin_y,
                -0.5 * con_a,
                -con_b,
                -0.5 * con_c,
            ]
        )
        poly = jnp.where(owner >= 0, poly, jnp.where(iota((8, SLOTS), 0) == 0, -200.0, 0.0))
        k1, k2, k3 = split_three(poly)
        poly_rows = jnp.concatenate([k1, k2, k3, jnp.zeros((104, SLOTS), F32)], axis=0).astype(
            BF16
        )
        color = rows8(vals[6:9])
        c1, c2, c3 = split_three(color)
        color_rows = jnp.concatenate(
            [c1, c2, c1, c2, c3, c1, jnp.zeros((80, SLOTS), F32)], axis=0
        ).astype(BF16)
        level = jnp.zeros((TPIX, 1), F32)
        seen_parts = []
        for block in range(NBLK):
            span = slice(block * BLOCK, (block + 1) * BLOCK)
            alpha = jnp.exp(mxu(basis_t_ref[...], poly_rows[:, span]))
            fade = alpha * (1.0 + alpha * (0.5 + alpha * (1.0 / 3.0)))
            fade_hi, fade_lo = split_two(fade)
            summed = mxu(jnp.concatenate([fade_hi, fade_lo], axis=1), tri_ref[...]) + level
            weight = alpha * jnp.exp(-summed)
            level = summed[:, BLOCK - 1 : BLOCK] + fade[:, BLOCK - 1 : BLOCK]
            alpha_ref[block] = alpha
            q_ref[block] = mxu(shade_ref[...], color_rows[:, span]) * weight
            weight_hi, weight_lo = split_two(weight)
            seen = mxu(pixel_rows, jnp.concatenate([weight_hi, weight_lo], axis=0))
            seen_parts.append(seen[0:8] + seen[8:16] + seen[16:24])
        seen = jnp.concatenate(seen_parts, axis=1)
        expo_cols = jnp.sum(color * seen, axis=1, keepdims=True)
        tail = jnp.zeros((TPIX, 1), F32)
        grad_parts = [None] * NBLK
        for block in reversed(range(NBLK)):
            alpha = alpha_ref[block]
            q_val = q_ref[block]
            q_hi, q_lo = split_two(q_val)
            later = mxu(jnp.concatenate([q_hi, q_lo], axis=1), low_ref[...]) + tail
            d_exp = q_val - later * (alpha * (1.0 + alpha * (1.0 + alpha)))
            tail = later[:, 0:1] + q_val[:, 0:1]
            d_hi, d_lo = split_two(d_exp)
            grad_parts[block] = mxu(basis_ref[...], jnp.concatenate([d_hi, d_lo], axis=0))[0:8]
        grad = jnp.concatenate(grad_parts, axis=1)
        d_poly = [grad[k : k + 1] for k in range(6)]
        grads = [
            d_poly[1] * con_a + d_poly[2] * con_b - d_poly[0] * lin_x,
            d_poly[1] * con_b + d_poly[2] * con_c - d_poly[0] * lin_y,
            shift_x * d_poly[1] - 0.5 * (d_poly[3] + shift_x * shift_x * d_poly[0]),
            shift_y * d_poly[1] + shift_x * d_poly[2] - d_poly[4] - shift_x * shift_y * d_poly[0],
            shift_y * d_poly[2] - 0.5 * (d_poly[5] + shift_y * shift_y * d_poly[0]),
            d_poly[0],
            gains[0] * seen[0:1],
            gains[1] * seen[1:2],
            gains[2] * seen[2:3],
        ]
        high_rows = []
        low_rows = []
        for value in grads:
            high = value.astype(BF16).astype(F32)
            high_rows.append(jnp.where(here, high, 0.0).astype(BF16))
            low_rows.append(jnp.where(here, value - high, 0.0).astype(BF16))
        both = mxu_bt(jnp.concatenate(high_rows + low_rows, axis=0), one_hot)
        sum_ref[0:USED, :] += both[0:USED] + both[USED : 2 * USED]
        lane_at = iota((8, 128), 1) - (USED - 384) - 3 * view
        return expo + jnp.where(
            (lane_at == iota((8, 128), 0)) & (lane_at < 3), expo_cols, 0.0
        )

    expo = lax.fori_loop(0, TILES, tile_step, jnp.zeros((8, 128), F32))
    for part in range(WIDE // 128):
        span = slice(part * 128, (part + 1) * 128)
        back = sum_ref[span, :].T
        if part == WIDE // 128 - 1:
            back = back + jnp.sum(expo, axis=0, keepdims=True)
        back_ref[:, span] = back


def render_of(tile_view, tile_spot, exposure, d_image, entries, arrived):
    smem = pl.BlockSpec(memory_space=pltpu.SMEM)
    vmem = pl.BlockSpec(memory_space=pltpu.VMEM)
    return pl.pallas_call(
        render_kernel,
        name="render",
        out_shape=jax.ShapeDtypeStruct((DEVS, WIDE), F32),
        in_specs=[smem, smem, smem, vmem, vmem, vmem],
        out_specs=vmem,
        scratch_shapes=[
            pltpu.VMEM((WIDE, 3 * DEVS), BF16),
            pltpu.VMEM((2 * BLOCK, BLOCK), BF16),
            pltpu.VMEM((2 * BLOCK, BLOCK), BF16),
            pltpu.VMEM((TPIX, 128), BF16),
            pltpu.VMEM((16, 2 * TPIX), BF16),
            pltpu.VMEM((NBLK, TPIX, BLOCK), F32),
            pltpu.VMEM((NBLK, TPIX, BLOCK), F32),
            pltpu.VMEM((TPIX, 128), BF16),
            pltpu.VMEM((WIDE, DEVS), F32),
        ],
        compiler_params=pltpu.CompilerParams(vmem_limit_bytes=32 << 20),
    )(tile_view, tile_spot, exposure, d_image, entries, arrived)


PARTS = 8
SPAN = GDEV // PARTS


def update_kernel(
    code_ref,
    camera_ref,
    code_vec_ref,
    arrived_ref,
    rows_ref,
    params_hbm,
    m_hbm,
    v_hbm,
    params_out,
    m_out,
    v_out,
    expo_ref,
    code_t_ref,
    cot_ref,
    grad_ref,
    spread_ref,
    flip_ref,
    params_ref,
    m_ref,
    v_ref,
    in_sems,
    out_sems,
    *tables,
):
    held = ((params_hbm, params_ref, params_out), (m_hbm, m_ref, m_out), (v_hbm, v_ref, v_out))

    def fetch(part):
        span = pl.ds(part * SPAN, SPAN)
        return [
            pltpu.make_async_copy(source.at[:, span], kept.at[:, span], in_sems.at[at, part])
            for at, (source, kept, unused) in enumerate(held)
        ]

    def give(part):
        span = pl.ds(part * SPAN, SPAN)
        return [
            pltpu.make_async_copy(kept.at[:, span], target.at[:, span], out_sems.at[at, part])
            for at, (unused, kept, target) in enumerate(held)
        ]

    for part in range(PARTS):
        for copy in fetch(part):
            copy.start()
    code_t_ref[...] = code_vec_ref[...].T
    expo_ref[...] = jnp.broadcast_to(
        jnp.sum(arrived_ref[:, 384:WIDE], axis=0, keepdims=True), (8, 128)
    )
    for part in range(WIDE // 128):
        span = slice(part * 128, (part + 1) * 128)
        cot_ref[span, :] = arrived_ref[:, span].T
    for table in tables:
        table[...] = jnp.zeros_like(table)
    grad_ref[PARAMS * CAP :, :] = jnp.zeros(((64 - PARAMS) * CAP, DEVS), F32)

    def chunk(at, carry):
        base = pl.multiple_of(at * 8, 8)
        values = [rows_ref[pl.ds(k * CAP + base, 8), :] for k in range(PARAMS)]
        code = code_t_ref[pl.ds(base, 8), :]
        camera = cameras_of(camera_ref, (code >> 14) & 3)
        unused, pull = jax.vjp(lambda given: project(given, camera), values)
        (grads,) = pull([cot_ref[pl.ds(k * CAP + base, 8), :] for k in range(VALS)])
        for k in range(PARAMS):
            grad_ref[pl.ds(k * CAP + base, 8), :] = jnp.where(code >= 0, grads[k], 0.0)
        return carry

    lax.fori_loop(0, CAP // 8, chunk, 0)

    def scatter(rank, carry):
        half = (code_t_ref[pl.ds(rank, 1), :] >> 13) & 1
        mine = jnp.concatenate(
            [grad_ref[pl.ds(group * 8 * CAP + rank, 8, stride=CAP), :] for group in range(8)],
            axis=0,
        )
        both = jnp.concatenate(
            [jnp.where(half == 0, mine, 0.0), jnp.where(half == 1, mine, 0.0)], axis=0
        )
        spread_ref[...] = both.T
        for src in range(DEVS):
            row = code_ref[src, rank + 64]
            table = tables[src % TABLES]
            table[pl.ds(row, 1), :] = table[pl.ds(row, 1), :] + spread_ref[src : src + 1, :]
        return carry

    lax.fori_loop(0, CAP, scatter, 0)

    for part in range(PARTS):
        for copy in fetch(part):
            copy.wait()

        def step(at, carry):
            rows = pl.ds(pl.multiple_of(part * (SPAN // 2) + at * 128, 128), 128)
            total = tables[0][rows, :]
            for table in tables[1:]:
                total = total + table[rows, :]
            flip_ref[...] = total.T
            for half in range(2):
                span = pl.ds(pl.multiple_of(part * SPAN + at * 256 + half * 128, 128), 128)
                gradient = flip_ref[half * 64 : half * 64 + PARAMS, :]
                new_m = beta_first * m_ref[:, span] + (1.0 - beta_first) * gradient
                new_v = beta_second * v_ref[:, span] + (1.0 - beta_second) * gradient * gradient
                m_ref[:, span] = new_m
                v_ref[:, span] = new_v
                params_ref[:, span] = params_ref[:, span] - learn_rate * (new_m / fix_first) / (
                    jnp.sqrt(new_v / fix_second) + adam_eps
                )
            return carry

        lax.fori_loop(0, SPAN // 256, step, 0)
        for copy in give(part):
            copy.start()
    for part in range(PARTS):
        for copy in give(part):
            copy.wait()


def update_of(codes, cameras, arrived, rows, params, adam_m, adam_v):
    smem = pl.BlockSpec(memory_space=pltpu.SMEM)
    vmem = pl.BlockSpec(memory_space=pltpu.VMEM)
    hbm = pl.BlockSpec(memory_space=pltpu.HBM)
    whole = jax.ShapeDtypeStruct((PARAMS, GDEV), F32)
    return pl.pallas_call(
        update_kernel,
        name="update",
        out_shape=(whole, whole, whole, jax.ShapeDtypeStruct((8, 128), F32)),
        in_specs=[smem, smem, vmem, vmem, vmem, hbm, hbm, hbm],
        out_specs=(hbm, hbm, hbm, vmem),
        scratch_shapes=[
            pltpu.VMEM((DEVS, DEVS), jnp.int32),
            pltpu.VMEM((WIDE, DEVS), F32),
            pltpu.VMEM((64 * CAP, DEVS), F32),
            pltpu.VMEM((DEVS, 128), F32),
            pltpu.VMEM((128, 128), F32),
        ]
        + [pltpu.VMEM((PARAMS, GDEV), F32)] * 3
        + [pltpu.SemaphoreType.DMA((3, PARTS))] * 2
        + [pltpu.VMEM((HALF, 128), F32)] * TABLES,
        compiler_params=pltpu.CompilerParams(vmem_limit_bytes=48 << 20),
    )(codes, cameras, codes, arrived, rows, params, adam_m, adam_v)


def exchange(value):
    return lax.all_to_all(value, AXES, split_axis=0, concat_axis=0, tiled=True)


def body(
    params,
    adam_m,
    adam_v,
    cameras,
    exposure,
    entry_owner,
    entry_local,
    block_counts,
    tile_view,
    tile_spot,
    d_image,
):
    requests, entries = route(tile_view, block_counts, entry_owner, entry_local)
    codes = exchange(requests)
    table = table_of(params)
    reply, rows = reply_of(codes, cameras, table)
    arrived = exchange(reply)
    back = render_of(tile_view, tile_spot, exposure, d_image, entries, arrived)
    returned = exchange(back)
    new_params, new_m, new_v, expo = update_of(
        codes, cameras, returned, rows, params, adam_m, adam_v
    )
    first = USED - 384
    exposure_grad = expo[0, first : first + 12].reshape(4, 3) / DEVS
    return (new_params, new_m, new_v, exposure_grad)


def solution(mesh):
    both = ("tiles", "gauss")
    placed = (
        P(None, both),
        P(None, both),
        P(None, both),
        P(),
        P(),
        P(both, None),
        P(both, None),
        P(both),
        P(both),
        P(both),
        P(both, None, None),
    )
    return jax.shard_map(
        body,
        mesh=mesh,
        in_specs=placed,
        out_specs=(P(None, both), P(None, both), P(None, both), P()),
        check_vma=False,
    )
```

```python
import jax
import jax.numpy as jnp
from jax import lax
from jax.experimental import pallas as pl
from jax.experimental.pallas import tpu as pltpu
from jax.sharding import PartitionSpec as P

AXES = ("tiles", "gauss")
DEVS = 128
CAP = 48
TILES = 4
SLOTS = 1024
BLOCK = 256
NBLK = 4
TPIX = 256
TILE = 16
ACROSS = 240
IMG_W = 3840
IMG_H = 2160
PARAMS = 59
GDEV = 16384
HALF = GDEV // 2
VALS = 9
USED = CAP * VALS
WIDE = 512
TABLES = 4
UNROLL = 16

sh_c0 = 0.28209479177387814
sh_c1 = 0.4886025119029199
sh_c2 = (
    1.0925484305920792,
    -1.0925484305920792,
    0.31539156525252005,
    -1.0925484305920792,
    0.5462742152960396,
)
sh_c3 = (
    -0.5900435899266435,
    2.890611442640554,
    -0.4570457994644658,
    0.3731763325901154,
    -0.4570457994644658,
    1.445305721320277,
    -0.5900435899266435,
)
beta_first = 0.9
beta_second = 0.999
learn_rate = 0.01
adam_eps = 1e-08
fix_first = 1.0
fix_second = 0.632304575229036
blur_add = 0.3

F32 = jnp.float32
BF16 = jnp.bfloat16


def sh_color(coefficients, unit_x, unit_y, unit_z):
    square_x = unit_x * unit_x
    square_y = unit_y * unit_y
    square_z = unit_z * unit_z
    basis_list = [
        -sh_c1 * unit_y,
        sh_c1 * unit_z,
        -sh_c1 * unit_x,
        sh_c2[0] * unit_x * unit_y,
        sh_c2[1] * unit_y * unit_z,
        sh_c2[2] * (2.0 * square_z - square_x - square_y),
        sh_c2[3] * unit_x * unit_z,
        sh_c2[4] * (square_x - square_y),
        sh_c3[0] * unit_y * (3.0 * square_x - square_y),
        sh_c3[1] * unit_x * unit_y * unit_z,
        sh_c3[2] * unit_y * (4.0 * square_z - square_x - square_y),
        sh_c3[3] * unit_z * (2.0 * square_z - 3.0 * square_x - 3.0 * square_y),
        sh_c3[4] * unit_x * (4.0 * square_z - square_x - square_y),
        sh_c3[5] * unit_z * (square_x - square_y),
        sh_c3[6] * unit_x * (square_x - 3.0 * square_y),
    ]
    colors = []
    for channel in range(3):
        summed = 0.5 + sh_c0 * coefficients[channel]
        for index_k in range(15):
            summed = summed + basis_list[index_k] * coefficients[3 * (index_k + 1) + channel]
        colors.append(jnp.maximum(summed, 0.0))
    return colors


def project(values, camera):
    points = [values[0], values[1], values[2]]
    matrix = [[camera[3 * row_at + col_at] for col_at in range(3)] for row_at in range(3)]
    translation = [camera[9], camera[10], camera[11]]
    focal_len = camera[12]
    viewed = [
        matrix[row_at][0] * points[0]
        + matrix[row_at][1] * points[1]
        + matrix[row_at][2] * points[2]
        + translation[row_at]
        for row_at in range(3)
    ]
    inverse_depth = 1.0 / viewed[2]
    screen_x = focal_len * viewed[0] * inverse_depth + 0.5 * IMG_W
    screen_y = focal_len * viewed[1] * inverse_depth + 0.5 * IMG_H
    slope_x = focal_len * viewed[0] * inverse_depth * inverse_depth
    slope_y = focal_len * viewed[1] * inverse_depth * inverse_depth
    jac_w = [
        [
            focal_len * inverse_depth * matrix[0][col_at] - slope_x * matrix[2][col_at]
            for col_at in range(3)
        ],
        [
            focal_len * inverse_depth * matrix[1][col_at] - slope_y * matrix[2][col_at]
            for col_at in range(3)
        ],
    ]
    quat_len = jnp.sqrt(
        values[6] * values[6]
        + values[7] * values[7]
        + values[8] * values[8]
        + values[9] * values[9]
    )
    quat_w = values[6] / quat_len
    quat_x = values[7] / quat_len
    quat_y = values[8] / quat_len
    quat_z = values[9] / quat_len
    rotation = [
        [
            1.0 - 2.0 * (quat_y * quat_y + quat_z * quat_z),
            2.0 * (quat_x * quat_y - quat_w * quat_z),
            2.0 * (quat_x * quat_z + quat_w * quat_y),
        ],
        [
            2.0 * (quat_x * quat_y + quat_w * quat_z),
            1.0 - 2.0 * (quat_x * quat_x + quat_z * quat_z),
            2.0 * (quat_y * quat_z - quat_w * quat_x),
        ],
        [
            2.0 * (quat_x * quat_z - quat_w * quat_y),
            2.0 * (quat_y * quat_z + quat_w * quat_x),
            1.0 - 2.0 * (quat_x * quat_x + quat_y * quat_y),
        ],
    ]
    extent = [jnp.exp(values[3]), jnp.exp(values[4]), jnp.exp(values[5])]
    spread = [
        [
            (
                jac_w[row_at][0] * rotation[0][col_at]
                + jac_w[row_at][1] * rotation[1][col_at]
                + jac_w[row_at][2] * rotation[2][col_at]
            )
            * extent[col_at]
            for col_at in range(3)
        ]
        for row_at in range(2)
    ]
    cov_a = (
        spread[0][0] * spread[0][0]
        + spread[0][1] * spread[0][1]
        + spread[0][2] * spread[0][2]
        + blur_add
    )
    cov_b = spread[0][0] * spread[1][0] + spread[0][1] * spread[1][1] + spread[0][2] * spread[1][2]
    cov_c = (
        spread[1][0] * spread[1][0]
        + spread[1][1] * spread[1][1]
        + spread[1][2] * spread[1][2]
        + blur_add
    )
    determinant = cov_a * cov_c - cov_b * cov_b
    logit = values[10]
    log_opacity = jnp.minimum(logit, 0.0) - jnp.log(1.0 + jnp.exp(-jnp.abs(logit)))
    center = [
        -(
            matrix[0][col_at] * translation[0]
            + matrix[1][col_at] * translation[1]
            + matrix[2][col_at] * translation[2]
        )
        for col_at in range(3)
    ]
    offset = [points[col_at] - center[col_at] for col_at in range(3)]
    distance = jnp.sqrt(offset[0] * offset[0] + offset[1] * offset[1] + offset[2] * offset[2])
    colors = sh_color(
        values[11:PARAMS], offset[0] / distance, offset[1] / distance, offset[2] / distance
    )
    return [
        screen_x,
        screen_y,
        cov_c / determinant,
        -cov_b / determinant,
        cov_a / determinant,
        log_opacity,
    ] + colors


def in_hbm(value):
    return pltpu.with_memory_space_constraint(value, pltpu.HBM)


def iota(shape, dim):
    return lax.broadcasted_iota(jnp.int32, shape, dim)


def mxu(left, right):
    return jnp.dot(left, right, preferred_element_type=F32)


def mxu_bt(left, right):
    return lax.dot_general(left, right, (((1,), (1,)), ((), ())), preferred_element_type=F32)


def split_two(value):
    high = value.astype(BF16)
    low = (value - high.astype(F32)).astype(BF16)
    return high, low


def split_three(value):
    high = value.astype(BF16).astype(F32)
    rest = value - high
    middle = rest.astype(BF16).astype(F32)
    low = (rest - middle).astype(BF16).astype(F32)
    return high, middle, low


def upper_strict():
    return (iota((BLOCK, BLOCK), 0) < iota((BLOCK, BLOCK), 1)).astype(F32).astype(BF16)


def route_kernel(
    view_hbm,
    count_hbm,
    owner_hbm,
    local_hbm,
    req_ref,
    entry_ref,
    view_ref,
    count_ref,
    owner_ref,
    local_ref,
    flip_ref,
    sems,
):
    copies = [
        pltpu.make_async_copy(source, target, sems.at[at])
        for at, (source, target) in enumerate(
            (
                (view_hbm, view_ref),
                (count_hbm, count_ref),
                (owner_hbm, owner_ref),
                (local_hbm, local_ref),
            )
        )
    ]
    for copy in copies:
        copy.start()
    tri = upper_strict()
    for copy in copies:
        copy.wait()
    before = jnp.zeros((DEVS, 1), F32)
    total = jnp.zeros((2 * CAP, DEVS), F32)
    for tile in range(TILES):
        view = view_ref[tile]
        slots = slice(tile * SLOTS, (tile + 1) * SLOTS)
        alive = (iota((1, SLOTS), 1) >> 8) < count_ref[tile]
        owner = jnp.where(alive, owner_ref[tile : tile + 1, :], -1)
        local = local_ref[tile : tile + 1, :]
        one_hot = (iota((DEVS, SLOTS), 0) == owner).astype(F32)
        one_hot_b = one_hot.astype(BF16)
        ranks = []
        for block in range(NBLK):
            span = slice(block * BLOCK, (block + 1) * BLOCK)
            earlier = mxu(one_hot_b[:, span], tri) + before
            ranks.append(jnp.sum(one_hot[:, span] * earlier, axis=0, keepdims=True))
            last = (block + 1) * BLOCK
            before = earlier[:, BLOCK - 1 : BLOCK] + one_hot[:, last - 1 : last]
        rank = jnp.where(owner >= 0, jnp.concatenate(ranks, axis=1).astype(jnp.int32), -1)
        code = (
            view * GDEV + ((local >> 7) & 1) * HALF + ((local >> 8) << 7) + (local & 127) + 1
        )
        here = iota((CAP, SLOTS), 0) == rank
        high = jnp.where(here, (code >> 8).astype(F32), 0.0).astype(BF16)
        low = jnp.where(here, (code & 255).astype(F32), 0.0).astype(BF16)
        total = total + mxu_bt(jnp.concatenate([high, low], axis=0), one_hot_b)
        entry_ref[0:1, slots] = owner
        entry_ref[1:2, slots] = rank
    flip_ref[...] = jnp.zeros_like(flip_ref)
    flip_ref[0:CAP, :] = total[0:CAP] * 256.0 + total[CAP : 2 * CAP]
    req_ref[...] = flip_ref[...].T.astype(jnp.int32) - 1


def route(tile_view, block_counts, entry_owner, entry_local):
    hbm = pl.BlockSpec(memory_space=pltpu.HBM)
    vmem = pl.BlockSpec(memory_space=pltpu.VMEM)
    return pl.pallas_call(
        route_kernel,
        name="route",
        out_shape=(
            jax.ShapeDtypeStruct((DEVS, DEVS), jnp.int32),
            jax.ShapeDtypeStruct((8, TILES * SLOTS), jnp.int32),
        ),
        in_specs=[hbm, hbm, hbm, hbm],
        out_specs=(vmem, vmem),
        scratch_shapes=[
            pltpu.SMEM((TILES,), jnp.int32),
            pltpu.SMEM((TILES,), jnp.int32),
            pltpu.VMEM((TILES, SLOTS), jnp.int32),
            pltpu.VMEM((TILES, SLOTS), jnp.int32),
            pltpu.VMEM((DEVS, DEVS), F32),
            pltpu.SemaphoreType.DMA((4,)),
        ],
        compiler_params=pltpu.CompilerParams(vmem_limit_bytes=16 << 20),
    )(*[in_hbm(given) for given in (tile_view, block_counts, entry_owner, entry_local)])


COLS = 2048


def table_kernel(params_ref, table_ref, pad_ref):
    @pl.when(pl.program_id(0) == 0)
    def _():
        pad_ref[...] = jnp.zeros_like(pad_ref)

    for at in range(COLS // 256):
        pad_ref[at, 0:PARAMS, :] = params_ref[:, at * 256 : at * 256 + 128]
        pad_ref[at, 64 : 64 + PARAMS, :] = params_ref[:, at * 256 + 128 : at * 256 + 256]
        table_ref[at * 128 : (at + 1) * 128, :] = pad_ref[at].T


def table_of(params):
    return pl.pallas_call(
        table_kernel,
        name="table",
        grid=(GDEV // COLS,),
        out_shape=pltpu.HBM((HALF, 128), F32),
        in_specs=[pl.BlockSpec((PARAMS, COLS), lambda i: (0, i))],
        out_specs=pl.BlockSpec((COLS // 2, 128), lambda i: (i, 0)),
        scratch_shapes=[pltpu.VMEM((COLS // 256, 128, 128), F32)],
        compiler_params=pltpu.CompilerParams(vmem_limit_bytes=24 << 20),
        cost_estimate=pl.CostEstimate(flops=1 << 20, bytes_accessed=9 << 20, transcendentals=0),
    )(in_hbm(params))


def cameras_of(camera_ref, view):
    return [
        jnp.where(
            view == 0,
            camera_ref[0, at],
            jnp.where(
                view == 1,
                camera_ref[1, at],
                jnp.where(view == 2, camera_ref[2, at], camera_ref[3, at]),
            ),
        )
        for at in range(13)
    ]


PIECES = 8


def reply_kernel(
    camera_ref,
    code_ref,
    table_hbm,
    reply_ref,
    rows_ref,
    code_t_ref,
    row_t_ref,
    row_smem,
    table_ref,
    got_ref,
    proj_ref,
    table_sems,
    row_sem,
):
    copies = []
    for piece in range(PIECES):
        span = pl.ds(piece * (HALF // PIECES), HALF // PIECES)
        copies.append(
            pltpu.make_async_copy(table_hbm.at[span], table_ref.at[span], table_sems.at[piece])
        )
    for copy in copies:
        copy.start()
    code_t_ref[...] = code_ref[...].T
    row_t_ref[...] = code_t_ref[0:CAP, :] & (HALF - 1)
    send_rows = pltpu.make_async_copy(row_t_ref, row_smem, row_sem)
    send_rows.start()
    proj_ref[USED:WIDE, :] = jnp.zeros((WIDE - USED, DEVS), F32)
    send_rows.wait()
    for copy in copies:
        copy.wait()

    def gather(step, carry):
        for odd in range(2):
            rank = step * 2 + odd
            for src in range(DEVS):
                got_ref[odd, src : src + 1, :] = table_ref[pl.ds(row_smem[rank, src], 1), :]
            both = got_ref[odd].T
            half = (code_t_ref[pl.ds(rank, 1), :] >> 13) & 1
            picked = jnp.where(half == 0, both[0:64], both[64:128])
            for group in range(8):
                rows_ref[pl.ds(group * 8 * CAP + rank, 8, stride=CAP), :] = picked[
                    group * 8 : (group + 1) * 8
                ]
        return carry

    lax.fori_loop(0, CAP // 2, gather, 0)

    def chunk(at, carry):
        base = pl.multiple_of(at * 8, 8)
        values = [rows_ref[pl.ds(k * CAP + base, 8), :] for k in range(PARAMS)]
        view = (code_t_ref[pl.ds(base, 8), :] >> 14) & 3
        for k, value in enumerate(project(values, cameras_of(camera_ref, view))):
            proj_ref[pl.ds(k * CAP + base, 8), :] = value
        return carry

    lax.fori_loop(0, CAP // 8, chunk, 0)
    for part in range(WIDE // 128):
        reply_ref[:, part, :] = proj_ref[part * 128 : (part + 1) * 128, :].T


def reply_of(codes, cameras, table):
    smem = pl.BlockSpec(memory_space=pltpu.SMEM)
    vmem = pl.BlockSpec(memory_space=pltpu.VMEM)
    hbm = pl.BlockSpec(memory_space=pltpu.HBM)
    return pl.pallas_call(
        reply_kernel,
        name="reply",
        out_shape=(
            jax.ShapeDtypeStruct((DEVS, WIDE // 128, 128), F32),
            jax.ShapeDtypeStruct((64 * CAP, DEVS), F32),
        ),
        in_specs=[smem, vmem, hbm],
        out_specs=(vmem, vmem),
        scratch_shapes=[
            pltpu.VMEM((DEVS, DEVS), jnp.int32),
            pltpu.VMEM((CAP, DEVS), jnp.int32),
            pltpu.SMEM((CAP, DEVS), jnp.int32),
            pltpu.VMEM((HALF, 128), F32),
            pltpu.VMEM((2, DEVS, 128), F32),
            pltpu.VMEM((WIDE, DEVS), F32),
            pltpu.SemaphoreType.DMA((PIECES,)),
            pltpu.SemaphoreType.DMA,
        ],
        compiler_params=pltpu.CompilerParams(vmem_limit_bytes=48 << 20),
    )(cameras, codes, in_hbm(table))


def render_kernel(
    view_ref,
    spot_ref,
    gain_ref,
    d_image_ref,
    entry_ref,
    arrived_ref,
    back_ref,
    split_ref,
    tri_ref,
    low_ref,
    basis_t_ref,
    basis_ref,
    alpha_ref,
    q_ref,
    shade_ref,
    sum_ref,
):
    for part in range(WIDE // 128):
        span = slice(part * 128, (part + 1) * 128)
        flipped = arrived_ref[:, part, :].T
        for piece, value in enumerate(split_three(flipped)):
            split_ref[span, piece * 128 : (piece + 1) * 128] = value.astype(BF16)
    upper = upper_strict()
    lower = (iota((BLOCK, BLOCK), 0) > iota((BLOCK, BLOCK), 1)).astype(F32).astype(BF16)
    tri_ref[0:BLOCK, :] = upper
    tri_ref[BLOCK : 2 * BLOCK, :] = upper
    low_ref[0:BLOCK, :] = lower
    low_ref[BLOCK : 2 * BLOCK, :] = lower

    def monomial(which, x, y):
        return jnp.where(
            which == 0,
            1.0,
            jnp.where(
                which == 1,
                x,
                jnp.where(
                    which == 2,
                    y,
                    jnp.where(
                        which == 3,
                        x * x,
                        jnp.where(which == 4, x * y, jnp.where(which == 5, y * y, 0.0)),
                    ),
                ),
            ),
        )

    pixel = iota((TPIX, 128), 0)
    lane = iota((TPIX, 128), 1)
    basis_t_ref[...] = jnp.where(
        lane < 24,
        monomial(lane & 7, (pixel & 15).astype(F32) - 7.5, (pixel >> 4).astype(F32) - 7.5),
        0.0,
    ).astype(BF16)
    pixel = iota((16, TPIX), 1)
    basis = monomial(
        iota((16, TPIX), 0), (pixel & 15).astype(F32) - 7.5, (pixel >> 4).astype(F32) - 7.5
    ).astype(BF16)
    basis_ref[:, 0:TPIX] = basis
    basis_ref[:, TPIX : 2 * TPIX] = basis
    sum_ref[...] = jnp.zeros_like(sum_ref)

    def rows8(rows):
        at_row = iota((8, rows[0].shape[1]), 0)
        out = jnp.zeros((8, rows[0].shape[1]), F32)
        for at, row in enumerate(rows):
            out = jnp.where(at_row == at, row, out)
        return out

    def tile_step(tile, expo):
        view = view_ref[tile]
        spot = spot_ref[tile]
        line = spot // ACROSS
        mid_x = ((spot - line * ACROSS) * TILE + TILE // 2).astype(F32)
        mid_y = (line * TILE + TILE // 2).astype(F32)
        gains = [gain_ref[view, ch] for ch in range(3)]
        d_rows = [d_image_ref[tile, ch : ch + 1, :] for ch in range(3)]
        d1, d2, d3 = split_three(rows8(d_rows))
        pixel_rows = jnp.concatenate([d1, d2, d3, jnp.zeros((8, TPIX), F32)], axis=0).astype(BF16)
        pixel_rows = jnp.concatenate([pixel_rows, pixel_rows], axis=1)
        g1, g2, g3 = split_three(rows8([gains[ch] * d_rows[ch] for ch in range(3)]))
        shade_ref[...] = (
            jnp.concatenate([g1, g1, g2, g2, g1, g3, jnp.zeros((80, TPIX), F32)], axis=0)
            .T.astype(BF16)
        )
        slots = pl.ds(pl.multiple_of(tile * SLOTS, SLOTS), SLOTS)
        owner = entry_ref[0:1, slots]
        rank = entry_ref[1:2, slots]
        one_hot = (iota((DEVS, SLOTS), 0) == owner).astype(F32).astype(BF16)
        found = mxu(
            split_ref[0:USED, :], jnp.concatenate([one_hot, one_hot, one_hot], axis=0)
        )
        here = iota((CAP, SLOTS), 0) == rank
        vals = [
            jnp.sum(jnp.where(here, found[k * CAP : (k + 1) * CAP], 0.0), axis=0, keepdims=True)
            for k in range(VALS)
        ]
        shift_x = vals[0] - mid_x
        shift_y = vals[1] - mid_y
        con_a, con_b, con_c = vals[2], vals[3], vals[4]
        lin_x = con_a * shift_x + con_b * shift_y
        lin_y = con_c * shift_y + con_b * shift_x
        level_row = vals[5] - 0.5 * (lin_x * shift_x + lin_y * shift_y)
        poly = rows8(
            [
                jnp.where(owner >= 0, level_row, -200.0),
                lin_x,
                lin_y,
                -0.5 * con_a,
                -con_b,
                -0.5 * con_c,
            ]
        )
        poly = jnp.where(owner >= 0, poly, jnp.where(iota((8, SLOTS), 0) == 0, -200.0, 0.0))
        k1, k2, k3 = split_three(poly)
        poly_rows = jnp.concatenate([k1, k2, k3, jnp.zeros((104, SLOTS), F32)], axis=0).astype(
            BF16
        )
        color = rows8(vals[6:9])
        c1, c2, c3 = split_three(color)
        color_rows = jnp.concatenate(
            [c1, c2, c1, c2, c3, c1, jnp.zeros((80, SLOTS), F32)], axis=0
        ).astype(BF16)
        level = jnp.zeros((TPIX, 1), F32)
        seen_parts = []
        for block in range(NBLK):
            span = slice(block * BLOCK, (block + 1) * BLOCK)
            alpha = jnp.exp(mxu(basis_t_ref[...], poly_rows[:, span]))
            fade = alpha * (1.0 + alpha * (0.5 + alpha * (1.0 / 3.0)))
            fade_hi, fade_lo = split_two(fade)
            summed = mxu(jnp.concatenate([fade_hi, fade_lo], axis=1), tri_ref[...]) + level
            weight = alpha * jnp.exp(-summed)
            level = summed[:, BLOCK - 1 : BLOCK] + fade[:, BLOCK - 1 : BLOCK]
            alpha_ref[block] = alpha
            q_ref[block] = mxu(shade_ref[...], color_rows[:, span]) * weight
            weight_hi, weight_lo = split_two(weight)
            seen = mxu(pixel_rows, jnp.concatenate([weight_hi, weight_lo], axis=0))
            seen_parts.append(seen[0:8] + seen[8:16] + seen[16:24])
        seen = jnp.concatenate(seen_parts, axis=1)
        expo_cols = jnp.sum(color * seen, axis=1, keepdims=True)
        tail = jnp.zeros((TPIX, 1), F32)
        grad_parts = [None] * NBLK
        for block in reversed(range(NBLK)):
            alpha = alpha_ref[block]
            q_val = q_ref[block]
            q_hi, q_lo = split_two(q_val)
            later = mxu(jnp.concatenate([q_hi, q_lo], axis=1), low_ref[...]) + tail
            d_exp = q_val - later * (alpha * (1.0 + alpha * (1.0 + alpha)))
            tail = later[:, 0:1] + q_val[:, 0:1]
            d_hi, d_lo = split_two(d_exp)
            grad_parts[block] = mxu(basis_ref[...], jnp.concatenate([d_hi, d_lo], axis=0))[0:8]
        grad = jnp.concatenate(grad_parts, axis=1)
        d_poly = [grad[k : k + 1] for k in range(6)]
        grads = [
            d_poly[1] * con_a + d_poly[2] * con_b - d_poly[0] * lin_x,
            d_poly[1] * con_b + d_poly[2] * con_c - d_poly[0] * lin_y,
            shift_x * d_poly[1] - 0.5 * (d_poly[3] + shift_x * shift_x * d_poly[0]),
            shift_y * d_poly[1] + shift_x * d_poly[2] - d_poly[4] - shift_x * shift_y * d_poly[0],
            shift_y * d_poly[2] - 0.5 * (d_poly[5] + shift_y * shift_y * d_poly[0]),
            d_poly[0],
            gains[0] * seen[0:1],
            gains[1] * seen[1:2],
            gains[2] * seen[2:3],
        ]
        high_rows = []
        low_rows = []
        for value in grads:
            high = value.astype(BF16).astype(F32)
            high_rows.append(jnp.where(here, high, 0.0).astype(BF16))
            low_rows.append(jnp.where(here, value - high, 0.0).astype(BF16))
        both = mxu_bt(jnp.concatenate(high_rows + low_rows, axis=0), one_hot)
        sum_ref[0:USED, :] += both[0:USED] + both[USED : 2 * USED]
        lane_at = iota((8, 128), 1) - (USED - 384) - 3 * view
        return expo + jnp.where(
            (lane_at == iota((8, 128), 0)) & (lane_at < 3), expo_cols, 0.0
        )

    expo = lax.fori_loop(0, TILES, tile_step, jnp.zeros((8, 128), F32))
    for part in range(WIDE // 128):
        span = slice(part * 128, (part + 1) * 128)
        back = sum_ref[span, :].T
        if part == WIDE // 128 - 1:
            back = back + jnp.sum(expo, axis=0, keepdims=True)
        back_ref[:, part, :] = back


def render_of(tile_view, tile_spot, exposure, d_image, entries, arrived):
    smem = pl.BlockSpec(memory_space=pltpu.SMEM)
    vmem = pl.BlockSpec(memory_space=pltpu.VMEM)
    return pl.pallas_call(
        render_kernel,
        name="render",
        out_shape=jax.ShapeDtypeStruct((DEVS, WIDE // 128, 128), F32),
        in_specs=[smem, smem, smem, vmem, vmem, vmem],
        out_specs=vmem,
        scratch_shapes=[
            pltpu.VMEM((WIDE, 3 * DEVS), BF16),
            pltpu.VMEM((2 * BLOCK, BLOCK), BF16),
            pltpu.VMEM((2 * BLOCK, BLOCK), BF16),
            pltpu.VMEM((TPIX, 128), BF16),
            pltpu.VMEM((16, 2 * TPIX), BF16),
            pltpu.VMEM((NBLK, TPIX, BLOCK), F32),
            pltpu.VMEM((NBLK, TPIX, BLOCK), F32),
            pltpu.VMEM((TPIX, 128), BF16),
            pltpu.VMEM((WIDE, DEVS), F32),
        ],
        compiler_params=pltpu.CompilerParams(vmem_limit_bytes=32 << 20),
    )(tile_view, tile_spot, exposure, d_image, entries, arrived)


PARTS = 8
SPAN = GDEV // PARTS


def update_kernel(
    camera_ref,
    code_ref,
    arrived_ref,
    rows_ref,
    params_hbm,
    m_hbm,
    v_hbm,
    params_out,
    m_out,
    v_out,
    expo_ref,
    code_t_ref,
    row_t_ref,
    row_smem,
    cot_ref,
    grad_ref,
    spread_ref,
    flip_ref,
    params_ref,
    m_ref,
    v_ref,
    in_sems,
    out_sems,
    row_sem,
    *tables,
):
    held = ((params_hbm, params_ref, params_out), (m_hbm, m_ref, m_out), (v_hbm, v_ref, v_out))

    def fetch(part):
        span = pl.ds(pl.multiple_of(part * SPAN, SPAN), SPAN)
        return [
            pltpu.make_async_copy(source.at[:, span], kept.at[:, span], in_sems.at[at, part])
            for at, (source, kept, unused) in enumerate(held)
        ]

    def give(part):
        span = pl.ds(pl.multiple_of(part * SPAN, SPAN), SPAN)
        return [
            pltpu.make_async_copy(kept.at[:, span], target.at[:, span], out_sems.at[at, part])
            for at, (unused, kept, target) in enumerate(held)
        ]

    code_t_ref[...] = code_ref[...].T
    row_t_ref[...] = code_t_ref[0:CAP, :] & (HALF - 1)
    send_rows = pltpu.make_async_copy(row_t_ref, row_smem, row_sem)
    send_rows.start()
    for part in range(PARTS):
        for copy in fetch(part):
            copy.start()
    shares = jnp.sum(arrived_ref[:, 3, :], axis=0, keepdims=True) * (1.0 / DEVS)
    for view in range(TILES):
        first = USED - 384 + 3 * view
        expo_ref[view : view + 1, :] = shares[:, first : first + 3]
    for part in range(WIDE // 128):
        cot_ref[part * 128 : (part + 1) * 128, :] = arrived_ref[:, part, :].T
    for table in tables:
        table[...] = jnp.zeros_like(table)
    grad_ref[PARAMS * CAP :, :] = jnp.zeros(((64 - PARAMS) * CAP, DEVS), F32)

    def chunk(at, carry):
        base = pl.multiple_of(at * 8, 8)
        values = [rows_ref[pl.ds(k * CAP + base, 8), :] for k in range(PARAMS)]
        code = code_t_ref[pl.ds(base, 8), :]
        camera = cameras_of(camera_ref, (code >> 14) & 3)
        unused, pull = jax.vjp(lambda given: project(given, camera), values)
        (grads,) = pull([cot_ref[pl.ds(k * CAP + base, 8), :] for k in range(VALS)])
        for k in range(PARAMS):
            grad_ref[pl.ds(k * CAP + base, 8), :] = jnp.where(code >= 0, grads[k], 0.0)
        return carry

    lax.fori_loop(0, CAP // 8, chunk, 0)
    send_rows.wait()

    def scatter(step, carry):
        for odd in range(2):
            rank = step * 2 + odd
            half = (code_t_ref[pl.ds(rank, 1), :] >> 13) & 1
            mine = jnp.concatenate(
                [grad_ref[pl.ds(group * 8 * CAP + rank, 8, stride=CAP), :] for group in range(8)],
                axis=0,
            )
            both = jnp.concatenate(
                [jnp.where(half == 0, mine, 0.0), jnp.where(half == 1, mine, 0.0)], axis=0
            )
            spread_ref[odd] = both.T
            for first in range(0, DEVS, 2 * TABLES):
                rows = [row_smem[rank, first + at] for at in range(2 * TABLES)]
                olds = [
                    tables[at % TABLES][pl.ds(rows[at], 1), :] for at in range(2 * TABLES)
                ]
                news = [
                    olds[at] + spread_ref[odd, first + at : first + at + 1, :]
                    for at in range(TABLES)
                ]
                for at in range(TABLES, 2 * TABLES):
                    old = jnp.where(rows[at] == rows[at - TABLES], news[at - TABLES], olds[at])
                    news.append(old + spread_ref[odd, first + at : first + at + 1, :])
                for at in range(2 * TABLES):
                    tables[at % TABLES][pl.ds(rows[at], 1), :] = news[at]
        return carry

    lax.fori_loop(0, CAP // 2, scatter, 0)

    def finish(part, carry):
        for copy in fetch(part):
            copy.wait()
        for at in range(SPAN // 256):
            rows = pl.ds(pl.multiple_of(part * (SPAN // 2) + at * 128, 128), 128)
            total = tables[0][rows, :]
            for table in tables[1:]:
                total = total + table[rows, :]
            flip_ref[at] = total.T
            for half in range(2):
                span = pl.ds(pl.multiple_of(part * SPAN + at * 256 + half * 128, 128), 128)
                gradient = flip_ref[at, half * 64 : half * 64 + PARAMS, :]
                new_m = beta_first * m_ref[:, span] + (1.0 - beta_first) * gradient
                new_v = beta_second * v_ref[:, span] + (1.0 - beta_second) * gradient * gradient
                m_ref[:, span] = new_m
                v_ref[:, span] = new_v
                params_ref[:, span] = params_ref[:, span] - learn_rate * (new_m / fix_first) / (
                    jnp.sqrt(new_v / fix_second) + adam_eps
                )
        for copy in give(part):
            copy.start()
        return carry

    lax.fori_loop(0, PARTS, finish, 0)
    for part in range(PARTS):
        for copy in give(part):
            copy.wait()


def update_of(codes, cameras, arrived, rows, params, adam_m, adam_v):
    smem = pl.BlockSpec(memory_space=pltpu.SMEM)
    vmem = pl.BlockSpec(memory_space=pltpu.VMEM)
    hbm = pl.BlockSpec(memory_space=pltpu.HBM)
    whole = jax.ShapeDtypeStruct((PARAMS, GDEV), F32)
    return pl.pallas_call(
        update_kernel,
        name="update",
        out_shape=(whole, whole, whole, jax.ShapeDtypeStruct((4, 3), F32)),
        in_specs=[smem, vmem, vmem, vmem, hbm, hbm, hbm],
        out_specs=(hbm, hbm, hbm, vmem),
        scratch_shapes=[
            pltpu.VMEM((DEVS, DEVS), jnp.int32),
            pltpu.VMEM((CAP, DEVS), jnp.int32),
            pltpu.SMEM((CAP, DEVS), jnp.int32),
            pltpu.VMEM((WIDE, DEVS), F32),
            pltpu.VMEM((64 * CAP, DEVS), F32),
            pltpu.VMEM((2, DEVS, 128), F32),
            pltpu.VMEM((SPAN // 256, 128, 128), F32),
        ]
        + [pltpu.VMEM((PARAMS, GDEV), F32)] * 3
        + [pltpu.SemaphoreType.DMA((3, PARTS))] * 2
        + [pltpu.SemaphoreType.DMA]
        + [pltpu.VMEM((HALF, 128), F32)] * TABLES,
        compiler_params=pltpu.CompilerParams(vmem_limit_bytes=48 << 20),
    )(cameras, codes, arrived, rows, in_hbm(params), in_hbm(adam_m), in_hbm(adam_v))


def exchange(value):
    return lax.all_to_all(value, AXES, split_axis=0, concat_axis=0, tiled=True)


def body(
    params,
    adam_m,
    adam_v,
    cameras,
    exposure,
    entry_owner,
    entry_local,
    block_counts,
    tile_view,
    tile_spot,
    d_image,
):
    requests, entries = route(tile_view, block_counts, entry_owner, entry_local)
    codes = exchange(requests)
    table = table_of(params)
    reply, rows = reply_of(codes, cameras, table)
    arrived = exchange(reply)
    back = render_of(tile_view, tile_spot, exposure, d_image, entries, arrived)
    returned = exchange(back)
    new_params, new_m, new_v, exposure_grad = update_of(
        codes, cameras, returned, rows, params, adam_m, adam_v
    )
    return (new_params, new_m, new_v, exposure_grad)


def solution(mesh):
    both = ("tiles", "gauss")
    placed = (
        P(None, both),
        P(None, both),
        P(None, both),
        P(),
        P(),
        P(both, None),
        P(both, None),
        P(both),
        P(both),
        P(both),
        P(both, None, None),
    )
    return jax.shard_map(
        body,
        mesh=mesh,
        in_specs=placed,
        out_specs=(P(None, both), P(None, both), P(None, both), P()),
        check_vma=False,
    )
```

```python
import jax
import jax.numpy as jnp
from jax import lax
from jax.experimental import pallas as pl
from jax.experimental.pallas import tpu as pltpu
from jax.sharding import PartitionSpec as P

AXES = ("tiles", "gauss")
DEVS = 128
CAP = 48
TILES = 4
SLOTS = 1024
BLOCK = 256
NBLK = 4
TPIX = 256
TILE = 16
ACROSS = 240
IMG_W = 3840
IMG_H = 2160
PARAMS = 59
GDEV = 16384
HALF = GDEV // 2
VALS = 9
USED = CAP * VALS
WIDE = 512
TABLES = 4
UNROLL = 16

sh_c0 = 0.28209479177387814
sh_c1 = 0.4886025119029199
sh_c2 = (
    1.0925484305920792,
    -1.0925484305920792,
    0.31539156525252005,
    -1.0925484305920792,
    0.5462742152960396,
)
sh_c3 = (
    -0.5900435899266435,
    2.890611442640554,
    -0.4570457994644658,
    0.3731763325901154,
    -0.4570457994644658,
    1.445305721320277,
    -0.5900435899266435,
)
beta_first = 0.9
beta_second = 0.999
learn_rate = 0.01
adam_eps = 1e-08
fix_first = 1.0
fix_second = 0.632304575229036
blur_add = 0.3

F32 = jnp.float32
BF16 = jnp.bfloat16


def sh_color(coefficients, unit_x, unit_y, unit_z):
    square_x = unit_x * unit_x
    square_y = unit_y * unit_y
    square_z = unit_z * unit_z
    basis_list = [
        -sh_c1 * unit_y,
        sh_c1 * unit_z,
        -sh_c1 * unit_x,
        sh_c2[0] * unit_x * unit_y,
        sh_c2[1] * unit_y * unit_z,
        sh_c2[2] * (2.0 * square_z - square_x - square_y),
        sh_c2[3] * unit_x * unit_z,
        sh_c2[4] * (square_x - square_y),
        sh_c3[0] * unit_y * (3.0 * square_x - square_y),
        sh_c3[1] * unit_x * unit_y * unit_z,
        sh_c3[2] * unit_y * (4.0 * square_z - square_x - square_y),
        sh_c3[3] * unit_z * (2.0 * square_z - 3.0 * square_x - 3.0 * square_y),
        sh_c3[4] * unit_x * (4.0 * square_z - square_x - square_y),
        sh_c3[5] * unit_z * (square_x - square_y),
        sh_c3[6] * unit_x * (square_x - 3.0 * square_y),
    ]
    colors = []
    for channel in range(3):
        summed = 0.5 + sh_c0 * coefficients[channel]
        for index_k in range(15):
            summed = summed + basis_list[index_k] * coefficients[3 * (index_k + 1) + channel]
        colors.append(jnp.maximum(summed, 0.0))
    return colors


def project(values, camera):
    points = [values[0], values[1], values[2]]
    matrix = [[camera[3 * row_at + col_at] for col_at in range(3)] for row_at in range(3)]
    translation = [camera[9], camera[10], camera[11]]
    focal_len = camera[12]
    viewed = [
        matrix[row_at][0] * points[0]
        + matrix[row_at][1] * points[1]
        + matrix[row_at][2] * points[2]
        + translation[row_at]
        for row_at in range(3)
    ]
    inverse_depth = 1.0 / viewed[2]
    screen_x = focal_len * viewed[0] * inverse_depth + 0.5 * IMG_W
    screen_y = focal_len * viewed[1] * inverse_depth + 0.5 * IMG_H
    slope_x = focal_len * viewed[0] * inverse_depth * inverse_depth
    slope_y = focal_len * viewed[1] * inverse_depth * inverse_depth
    jac_w = [
        [
            focal_len * inverse_depth * matrix[0][col_at] - slope_x * matrix[2][col_at]
            for col_at in range(3)
        ],
        [
            focal_len * inverse_depth * matrix[1][col_at] - slope_y * matrix[2][col_at]
            for col_at in range(3)
        ],
    ]
    quat_len = jnp.sqrt(
        values[6] * values[6]
        + values[7] * values[7]
        + values[8] * values[8]
        + values[9] * values[9]
    )
    quat_w = values[6] / quat_len
    quat_x = values[7] / quat_len
    quat_y = values[8] / quat_len
    quat_z = values[9] / quat_len
    rotation = [
        [
            1.0 - 2.0 * (quat_y * quat_y + quat_z * quat_z),
            2.0 * (quat_x * quat_y - quat_w * quat_z),
            2.0 * (quat_x * quat_z + quat_w * quat_y),
        ],
        [
            2.0 * (quat_x * quat_y + quat_w * quat_z),
            1.0 - 2.0 * (quat_x * quat_x + quat_z * quat_z),
            2.0 * (quat_y * quat_z - quat_w * quat_x),
        ],
        [
            2.0 * (quat_x * quat_z - quat_w * quat_y),
            2.0 * (quat_y * quat_z + quat_w * quat_x),
            1.0 - 2.0 * (quat_x * quat_x + quat_y * quat_y),
        ],
    ]
    extent = [jnp.exp(values[3]), jnp.exp(values[4]), jnp.exp(values[5])]
    spread = [
        [
            (
                jac_w[row_at][0] * rotation[0][col_at]
                + jac_w[row_at][1] * rotation[1][col_at]
                + jac_w[row_at][2] * rotation[2][col_at]
            )
            * extent[col_at]
            for col_at in range(3)
        ]
        for row_at in range(2)
    ]
    cov_a = (
        spread[0][0] * spread[0][0]
        + spread[0][1] * spread[0][1]
        + spread[0][2] * spread[0][2]
        + blur_add
    )
    cov_b = spread[0][0] * spread[1][0] + spread[0][1] * spread[1][1] + spread[0][2] * spread[1][2]
    cov_c = (
        spread[1][0] * spread[1][0]
        + spread[1][1] * spread[1][1]
        + spread[1][2] * spread[1][2]
        + blur_add
    )
    determinant = cov_a * cov_c - cov_b * cov_b
    logit = values[10]
    log_opacity = jnp.minimum(logit, 0.0) - jnp.log(1.0 + jnp.exp(-jnp.abs(logit)))
    center = [
        -(
            matrix[0][col_at] * translation[0]
            + matrix[1][col_at] * translation[1]
            + matrix[2][col_at] * translation[2]
        )
        for col_at in range(3)
    ]
    offset = [points[col_at] - center[col_at] for col_at in range(3)]
    distance = jnp.sqrt(offset[0] * offset[0] + offset[1] * offset[1] + offset[2] * offset[2])
    colors = sh_color(
        values[11:PARAMS], offset[0] / distance, offset[1] / distance, offset[2] / distance
    )
    return [
        screen_x,
        screen_y,
        cov_c / determinant,
        -cov_b / determinant,
        cov_a / determinant,
        log_opacity,
    ] + colors


def in_hbm(value):
    return pltpu.with_memory_space_constraint(value, pltpu.HBM)


def iota(shape, dim):
    return lax.broadcasted_iota(jnp.int32, shape, dim)


def mxu(left, right):
    return jnp.dot(left, right, preferred_element_type=F32)


def mxu_bt(left, right):
    return lax.dot_general(left, right, (((1,), (1,)), ((), ())), preferred_element_type=F32)


def split_two(value):
    high = value.astype(BF16)
    low = (value - high.astype(F32)).astype(BF16)
    return high, low


def split_three(value):
    high = value.astype(BF16).astype(F32)
    rest = value - high
    middle = rest.astype(BF16).astype(F32)
    low = (rest - middle).astype(BF16).astype(F32)
    return high, middle, low


def upper_strict():
    return (iota((BLOCK, BLOCK), 0) < iota((BLOCK, BLOCK), 1)).astype(F32).astype(BF16)


def route_kernel(
    view_hbm,
    count_hbm,
    owner_hbm,
    local_hbm,
    req_ref,
    entry_ref,
    view_ref,
    count_ref,
    owner_ref,
    local_ref,
    flip_ref,
    sems,
):
    copies = [
        pltpu.make_async_copy(source, target, sems.at[at])
        for at, (source, target) in enumerate(
            (
                (view_hbm, view_ref),
                (count_hbm, count_ref),
                (owner_hbm, owner_ref),
                (local_hbm, local_ref),
            )
        )
    ]
    for copy in copies:
        copy.start()
    tri = upper_strict()
    for copy in copies:
        copy.wait()
    before = jnp.zeros((DEVS, 1), F32)
    total = jnp.zeros((2 * CAP, DEVS), F32)
    for tile in range(TILES):
        view = view_ref[tile]
        slots = slice(tile * SLOTS, (tile + 1) * SLOTS)
        alive = (iota((1, SLOTS), 1) >> 8) < count_ref[tile]
        owner = jnp.where(alive, owner_ref[tile : tile + 1, :], -1)
        local = local_ref[tile : tile + 1, :]
        one_hot = (iota((DEVS, SLOTS), 0) == owner).astype(F32)
        one_hot_b = one_hot.astype(BF16)
        ranks = []
        for block in range(NBLK):
            span = slice(block * BLOCK, (block + 1) * BLOCK)
            earlier = mxu(one_hot_b[:, span], tri) + before
            ranks.append(jnp.sum(one_hot[:, span] * earlier, axis=0, keepdims=True))
            last = (block + 1) * BLOCK
            before = earlier[:, BLOCK - 1 : BLOCK] + one_hot[:, last - 1 : last]
        rank = jnp.where(owner >= 0, jnp.concatenate(ranks, axis=1).astype(jnp.int32), -1)
        code = (
            view * GDEV + ((local >> 7) & 1) * HALF + ((local >> 8) << 7) + (local & 127) + 1
        )
        here = iota((CAP, SLOTS), 0) == rank
        high = jnp.where(here, (code >> 8).astype(F32), 0.0).astype(BF16)
        low = jnp.where(here, (code & 255).astype(F32), 0.0).astype(BF16)
        total = total + mxu_bt(jnp.concatenate([high, low], axis=0), one_hot_b)
        entry_ref[0:1, slots] = owner
        entry_ref[1:2, slots] = rank
    flip_ref[...] = jnp.zeros_like(flip_ref)
    flip_ref[0:CAP, :] = total[0:CAP] * 256.0 + total[CAP : 2 * CAP]
    req_ref[...] = flip_ref[...].T.astype(jnp.int32) - 1


def route(tile_view, block_counts, entry_owner, entry_local):
    hbm = pl.BlockSpec(memory_space=pltpu.HBM)
    vmem = pl.BlockSpec(memory_space=pltpu.VMEM)
    return pl.pallas_call(
        route_kernel,
        name="route",
        out_shape=(
            jax.ShapeDtypeStruct((DEVS, DEVS), jnp.int32),
            jax.ShapeDtypeStruct((8, TILES * SLOTS), jnp.int32),
        ),
        in_specs=[hbm, hbm, hbm, hbm],
        out_specs=(vmem, vmem),
        scratch_shapes=[
            pltpu.SMEM((TILES,), jnp.int32),
            pltpu.SMEM((TILES,), jnp.int32),
            pltpu.VMEM((TILES, SLOTS), jnp.int32),
            pltpu.VMEM((TILES, SLOTS), jnp.int32),
            pltpu.VMEM((DEVS, DEVS), F32),
            pltpu.SemaphoreType.DMA((4,)),
        ],
        compiler_params=pltpu.CompilerParams(vmem_limit_bytes=16 << 20),
    )(*[in_hbm(given) for given in (tile_view, block_counts, entry_owner, entry_local)])


PIECES = 8
PIECE = HALF // PIECES


def table_kernel(params_hbm, table_hbm, params_ref, table_ref, in_sems, out_sems):
    takes = []
    gives = []
    for piece in range(PIECES):
        cols = pl.ds(piece * 2 * PIECE, 2 * PIECE)
        takes.append(
            pltpu.make_async_copy(params_hbm.at[:, cols], params_ref.at[:, cols], in_sems.at[piece])
        )
        rows = pl.ds(piece * PIECE, PIECE)
        gives.append(
            pltpu.make_async_copy(table_ref.at[rows], table_hbm.at[rows], out_sems.at[piece])
        )
    for copy in takes:
        copy.start()
    gap = jnp.zeros((64 - PARAMS, 128), F32)
    for piece in range(PIECES):
        takes[piece].wait()
        for at in range(piece * (PIECE // 128), (piece + 1) * (PIECE // 128)):
            both = jnp.concatenate(
                [
                    params_ref[:, at * 256 : at * 256 + 128],
                    gap,
                    params_ref[:, at * 256 + 128 : at * 256 + 256],
                    gap,
                ],
                axis=0,
            )
            table_ref[at * 128 : (at + 1) * 128, :] = both.T
        gives[piece].start()
    for copy in gives:
        copy.wait()


def table_of(params):
    hbm = pl.BlockSpec(memory_space=pltpu.HBM)
    return pl.pallas_call(
        table_kernel,
        name="table",
        out_shape=pltpu.HBM((HALF, 128), F32),
        in_specs=[hbm],
        out_specs=hbm,
        scratch_shapes=[
            pltpu.VMEM((PARAMS, GDEV), F32),
            pltpu.VMEM((HALF, 128), F32),
            pltpu.SemaphoreType.DMA((PIECES,)),
            pltpu.SemaphoreType.DMA((PIECES,)),
        ],
        compiler_params=pltpu.CompilerParams(vmem_limit_bytes=24 << 20),
        cost_estimate=pl.CostEstimate(flops=1 << 20, bytes_accessed=9 << 20, transcendentals=0),
    )(in_hbm(params))


def cameras_of(camera_ref, view):
    return [
        jnp.where(
            view == 0,
            camera_ref[0, at],
            jnp.where(
                view == 1,
                camera_ref[1, at],
                jnp.where(view == 2, camera_ref[2, at], camera_ref[3, at]),
            ),
        )
        for at in range(13)
    ]


def reply_kernel(
    camera_ref,
    code_ref,
    table_hbm,
    reply_ref,
    rows_ref,
    code_t_ref,
    row_t_ref,
    row_smem,
    table_ref,
    got_ref,
    proj_ref,
    table_sems,
    row_sem,
):
    copies = []
    for piece in range(PIECES):
        span = pl.ds(piece * (HALF // PIECES), HALF // PIECES)
        copies.append(
            pltpu.make_async_copy(table_hbm.at[span], table_ref.at[span], table_sems.at[piece])
        )
    for copy in copies:
        copy.start()
    code_t_ref[...] = code_ref[...].T
    row_t_ref[...] = code_t_ref[0:CAP, :] & (HALF - 1)
    send_rows = pltpu.make_async_copy(row_t_ref, row_smem, row_sem)
    send_rows.start()
    proj_ref[USED:WIDE, :] = jnp.zeros((WIDE - USED, DEVS), F32)
    send_rows.wait()
    for copy in copies:
        copy.wait()

    def gather(step, carry):
        for odd in range(2):
            rank = step * 2 + odd
            for src in range(DEVS):
                got_ref[odd, src : src + 1, :] = table_ref[pl.ds(row_smem[rank, src], 1), :]
            both = got_ref[odd].T
            half = (code_t_ref[pl.ds(rank, 1), :] >> 13) & 1
            picked = jnp.where(half == 0, both[0:64], both[64:128])
            for group in range(8):
                rows_ref[pl.ds(group * 8 * CAP + rank, 8, stride=CAP), :] = picked[
                    group * 8 : (group + 1) * 8
                ]
        return carry

    lax.fori_loop(0, CAP // 2, gather, 0)

    def chunk(at, carry):
        base = pl.multiple_of(at * 8, 8)
        values = [rows_ref[pl.ds(k * CAP + base, 8), :] for k in range(PARAMS)]
        view = (code_t_ref[pl.ds(base, 8), :] >> 14) & 3
        for k, value in enumerate(project(values, cameras_of(camera_ref, view))):
            proj_ref[pl.ds(k * CAP + base, 8), :] = value
        return carry

    lax.fori_loop(0, CAP // 8, chunk, 0)
    for part in range(WIDE // 128):
        reply_ref[:, part, :] = proj_ref[part * 128 : (part + 1) * 128, :].T


def reply_of(codes, cameras, table):
    smem = pl.BlockSpec(memory_space=pltpu.SMEM)
    vmem = pl.BlockSpec(memory_space=pltpu.VMEM)
    hbm = pl.BlockSpec(memory_space=pltpu.HBM)
    return pl.pallas_call(
        reply_kernel,
        name="reply",
        out_shape=(
            jax.ShapeDtypeStruct((DEVS, WIDE // 128, 128), F32),
            jax.ShapeDtypeStruct((64 * CAP, DEVS), F32),
        ),
        in_specs=[smem, vmem, hbm],
        out_specs=(vmem, vmem),
        scratch_shapes=[
            pltpu.VMEM((DEVS, DEVS), jnp.int32),
            pltpu.VMEM((CAP, DEVS), jnp.int32),
            pltpu.SMEM((CAP, DEVS), jnp.int32),
            pltpu.VMEM((HALF, 128), F32),
            pltpu.VMEM((2, DEVS, 128), F32),
            pltpu.VMEM((WIDE, DEVS), F32),
            pltpu.SemaphoreType.DMA((PIECES,)),
            pltpu.SemaphoreType.DMA,
        ],
        compiler_params=pltpu.CompilerParams(vmem_limit_bytes=48 << 20),
    )(cameras, codes, in_hbm(table))


def render_kernel(
    view_hbm,
    spot_hbm,
    gain_hbm,
    d_image_hbm,
    entry_ref,
    arrived_ref,
    back_ref,
    view_ref,
    spot_ref,
    gain_ref,
    d_image_ref,
    sems,
    split_ref,
    tri_ref,
    low_ref,
    basis_t_ref,
    basis_ref,
    alpha_ref,
    q_ref,
    shade_ref,
    sum_ref,
):
    copies = [
        pltpu.make_async_copy(source, target, sems.at[at])
        for at, (source, target) in enumerate(
            (
                (view_hbm, view_ref),
                (spot_hbm, spot_ref),
                (gain_hbm, gain_ref),
                (d_image_hbm, d_image_ref),
            )
        )
    ]
    for copy in copies:
        copy.start()
    for part in range(WIDE // 128):
        span = slice(part * 128, (part + 1) * 128)
        flipped = arrived_ref[:, part, :].T
        for piece, value in enumerate(split_three(flipped)):
            split_ref[span, piece * 128 : (piece + 1) * 128] = value.astype(BF16)
    upper = upper_strict()
    lower = (iota((BLOCK, BLOCK), 0) > iota((BLOCK, BLOCK), 1)).astype(F32).astype(BF16)
    tri_ref[0:BLOCK, :] = upper
    tri_ref[BLOCK : 2 * BLOCK, :] = upper
    low_ref[0:BLOCK, :] = lower
    low_ref[BLOCK : 2 * BLOCK, :] = lower

    def monomial(which, x, y):
        return jnp.where(
            which == 0,
            1.0,
            jnp.where(
                which == 1,
                x,
                jnp.where(
                    which == 2,
                    y,
                    jnp.where(
                        which == 3,
                        x * x,
                        jnp.where(which == 4, x * y, jnp.where(which == 5, y * y, 0.0)),
                    ),
                ),
            ),
        )

    pixel = iota((TPIX, 128), 0)
    lane = iota((TPIX, 128), 1)
    basis_t_ref[...] = jnp.where(
        lane < 24,
        monomial(lane & 7, (pixel & 15).astype(F32) - 7.5, (pixel >> 4).astype(F32) - 7.5),
        0.0,
    ).astype(BF16)
    pixel = iota((16, TPIX), 1)
    basis = monomial(
        iota((16, TPIX), 0), (pixel & 15).astype(F32) - 7.5, (pixel >> 4).astype(F32) - 7.5
    ).astype(BF16)
    basis_ref[:, 0:TPIX] = basis
    basis_ref[:, TPIX : 2 * TPIX] = basis
    sum_ref[...] = jnp.zeros_like(sum_ref)

    def rows8(rows):
        at_row = iota((8, rows[0].shape[1]), 0)
        out = jnp.zeros((8, rows[0].shape[1]), F32)
        for at, row in enumerate(rows):
            out = jnp.where(at_row == at, row, out)
        return out

    def tile_step(tile, expo):
        view = view_ref[tile]
        spot = spot_ref[tile]
        line = spot // ACROSS
        mid_x = ((spot - line * ACROSS) * TILE + TILE // 2).astype(F32)
        mid_y = (line * TILE + TILE // 2).astype(F32)
        gains = [gain_ref[view, ch] for ch in range(3)]
        d_rows = [d_image_ref[ch, pl.ds(tile, 1), :] for ch in range(3)]
        d1, d2, d3 = split_three(rows8(d_rows))
        pixel_rows = jnp.concatenate([d1, d2, d3, jnp.zeros((8, TPIX), F32)], axis=0).astype(BF16)
        pixel_rows = jnp.concatenate([pixel_rows, pixel_rows], axis=1)
        g1, g2, g3 = split_three(rows8([gains[ch] * d_rows[ch] for ch in range(3)]))
        shade_ref[...] = (
            jnp.concatenate([g1, g1, g2, g2, g1, g3, jnp.zeros((80, TPIX), F32)], axis=0)
            .T.astype(BF16)
        )
        slots = pl.ds(pl.multiple_of(tile * SLOTS, SLOTS), SLOTS)
        owner = entry_ref[0:1, slots]
        rank = entry_ref[1:2, slots]
        one_hot = (iota((DEVS, SLOTS), 0) == owner).astype(F32).astype(BF16)
        found = mxu(
            split_ref[0:USED, :], jnp.concatenate([one_hot, one_hot, one_hot], axis=0)
        )
        here = iota((CAP, SLOTS), 0) == rank
        vals = [
            jnp.sum(jnp.where(here, found[k * CAP : (k + 1) * CAP], 0.0), axis=0, keepdims=True)
            for k in range(VALS)
        ]
        shift_x = vals[0] - mid_x
        shift_y = vals[1] - mid_y
        con_a, con_b, con_c = vals[2], vals[3], vals[4]
        lin_x = con_a * shift_x + con_b * shift_y
        lin_y = con_c * shift_y + con_b * shift_x
        level_row = vals[5] - 0.5 * (lin_x * shift_x + lin_y * shift_y)
        poly = rows8(
            [
                jnp.where(owner >= 0, level_row, -200.0),
                lin_x,
                lin_y,
                -0.5 * con_a,
                -con_b,
                -0.5 * con_c,
            ]
        )
        poly = jnp.where(owner >= 0, poly, jnp.where(iota((8, SLOTS), 0) == 0, -200.0, 0.0))
        k1, k2, k3 = split_three(poly)
        poly_rows = jnp.concatenate([k1, k2, k3, jnp.zeros((104, SLOTS), F32)], axis=0).astype(
            BF16
        )
        color = rows8(vals[6:9])
        c1, c2, c3 = split_three(color)
        color_rows = jnp.concatenate(
            [c1, c2, c1, c2, c3, c1, jnp.zeros((80, SLOTS), F32)], axis=0
        ).astype(BF16)
        level = jnp.zeros((TPIX, 1), F32)
        seen_parts = []
        for block in range(NBLK):
            span = slice(block * BLOCK, (block + 1) * BLOCK)
            alpha = jnp.exp(mxu(basis_t_ref[...], poly_rows[:, span]))
            fade = alpha * (1.0 + alpha * (0.5 + alpha * (1.0 / 3.0)))
            fade_hi, fade_lo = split_two(fade)
            summed = mxu(jnp.concatenate([fade_hi, fade_lo], axis=1), tri_ref[...]) + level
            weight = alpha * jnp.exp(-summed)
            level = summed[:, BLOCK - 1 : BLOCK] + fade[:, BLOCK - 1 : BLOCK]
            alpha_ref[block] = alpha
            q_ref[block] = mxu(shade_ref[...], color_rows[:, span]) * weight
            weight_hi, weight_lo = split_two(weight)
            seen = mxu(pixel_rows, jnp.concatenate([weight_hi, weight_lo], axis=0))
            seen_parts.append(seen[0:8] + seen[8:16] + seen[16:24])
        seen = jnp.concatenate(seen_parts, axis=1)
        expo_cols = jnp.sum(color * seen, axis=1, keepdims=True)
        tail = jnp.zeros((TPIX, 1), F32)
        grad_parts = [None] * NBLK
        for block in reversed(range(NBLK)):
            alpha = alpha_ref[block]
            q_val = q_ref[block]
            q_hi, q_lo = split_two(q_val)
            later = mxu(jnp.concatenate([q_hi, q_lo], axis=1), low_ref[...]) + tail
            d_exp = q_val - later * (alpha * (1.0 + alpha * (1.0 + alpha)))
            tail = later[:, 0:1] + q_val[:, 0:1]
            d_hi, d_lo = split_two(d_exp)
            grad_parts[block] = mxu(basis_ref[...], jnp.concatenate([d_hi, d_lo], axis=0))[0:8]
        grad = jnp.concatenate(grad_parts, axis=1)
        d_poly = [grad[k : k + 1] for k in range(6)]
        grads = [
            d_poly[1] * con_a + d_poly[2] * con_b - d_poly[0] * lin_x,
            d_poly[1] * con_b + d_poly[2] * con_c - d_poly[0] * lin_y,
            shift_x * d_poly[1] - 0.5 * (d_poly[3] + shift_x * shift_x * d_poly[0]),
            shift_y * d_poly[1] + shift_x * d_poly[2] - d_poly[4] - shift_x * shift_y * d_poly[0],
            shift_y * d_poly[2] - 0.5 * (d_poly[5] + shift_y * shift_y * d_poly[0]),
            d_poly[0],
            gains[0] * seen[0:1],
            gains[1] * seen[1:2],
            gains[2] * seen[2:3],
        ]
        high_rows = []
        low_rows = []
        for value in grads:
            high = value.astype(BF16).astype(F32)
            high_rows.append(jnp.where(here, high, 0.0).astype(BF16))
            low_rows.append(jnp.where(here, value - high, 0.0).astype(BF16))
        both = mxu_bt(jnp.concatenate(high_rows + low_rows, axis=0), one_hot)
        sum_ref[0:USED, :] += both[0:USED] + both[USED : 2 * USED]
        lane_at = iota((8, 128), 1) - (USED - 384) - 3 * view
        return expo + jnp.where(
            (lane_at == iota((8, 128), 0)) & (lane_at < 3), expo_cols, 0.0
        )

    for copy in copies:
        copy.wait()
    expo = lax.fori_loop(0, TILES, tile_step, jnp.zeros((8, 128), F32))
    for part in range(WIDE // 128):
        span = slice(part * 128, (part + 1) * 128)
        back = sum_ref[span, :].T
        if part == WIDE // 128 - 1:
            back = back + jnp.sum(expo, axis=0, keepdims=True)
        back_ref[:, part, :] = back


def render_of(tile_view, tile_spot, exposure, d_image, entries, arrived):
    hbm = pl.BlockSpec(memory_space=pltpu.HBM)
    vmem = pl.BlockSpec(memory_space=pltpu.VMEM)
    given = (tile_view, tile_spot, exposure, jnp.transpose(d_image, (1, 0, 2)))
    return pl.pallas_call(
        render_kernel,
        name="render",
        out_shape=jax.ShapeDtypeStruct((DEVS, WIDE // 128, 128), F32),
        in_specs=[hbm, hbm, hbm, hbm, vmem, vmem],
        out_specs=vmem,
        scratch_shapes=[
            pltpu.SMEM((TILES,), jnp.int32),
            pltpu.SMEM((TILES,), jnp.int32),
            pltpu.SMEM((4, 3), F32),
            pltpu.VMEM((3, TILES, TPIX), F32),
            pltpu.SemaphoreType.DMA((4,)),
            pltpu.VMEM((WIDE, 3 * DEVS), BF16),
            pltpu.VMEM((2 * BLOCK, BLOCK), BF16),
            pltpu.VMEM((2 * BLOCK, BLOCK), BF16),
            pltpu.VMEM((TPIX, 128), BF16),
            pltpu.VMEM((16, 2 * TPIX), BF16),
            pltpu.VMEM((NBLK, TPIX, BLOCK), F32),
            pltpu.VMEM((NBLK, TPIX, BLOCK), F32),
            pltpu.VMEM((TPIX, 128), BF16),
            pltpu.VMEM((WIDE, DEVS), F32),
        ],
        compiler_params=pltpu.CompilerParams(vmem_limit_bytes=32 << 20),
    )(*[in_hbm(value) for value in given], entries, arrived)


PARTS = 8
SPAN = GDEV // PARTS


def update_kernel(
    camera_ref,
    code_ref,
    arrived_ref,
    rows_ref,
    params_hbm,
    m_hbm,
    v_hbm,
    params_out,
    m_out,
    v_out,
    expo_ref,
    code_t_ref,
    row_t_ref,
    row_smem,
    cot_ref,
    grad_ref,
    spread_ref,
    flip_ref,
    params_ref,
    m_ref,
    v_ref,
    in_sems,
    out_sems,
    row_sem,
    *tables,
):
    held = ((params_hbm, params_ref, params_out), (m_hbm, m_ref, m_out), (v_hbm, v_ref, v_out))

    def fetch(part):
        span = pl.ds(pl.multiple_of(part * SPAN, SPAN), SPAN)
        return [
            pltpu.make_async_copy(source.at[:, span], kept.at[:, span], in_sems.at[at, part])
            for at, (source, kept, unused) in enumerate(held)
        ]

    def give(part):
        span = pl.ds(pl.multiple_of(part * SPAN, SPAN), SPAN)
        return [
            pltpu.make_async_copy(kept.at[:, span], target.at[:, span], out_sems.at[at, part])
            for at, (unused, kept, target) in enumerate(held)
        ]

    code_t_ref[...] = code_ref[...].T
    row_t_ref[...] = code_t_ref[0:CAP, :] & (HALF - 1)
    send_rows = pltpu.make_async_copy(row_t_ref, row_smem, row_sem)
    send_rows.start()
    for part in range(PARTS):
        for copy in fetch(part):
            copy.start()
    shares = jnp.sum(arrived_ref[:, 3, :], axis=0, keepdims=True) * (1.0 / DEVS)
    for view in range(TILES):
        first = USED - 384 + 3 * view
        expo_ref[view : view + 1, :] = shares[:, first : first + 3]
    for part in range(WIDE // 128):
        cot_ref[part * 128 : (part + 1) * 128, :] = arrived_ref[:, part, :].T
    for table in tables:
        table[...] = jnp.zeros_like(table)
    grad_ref[PARAMS * CAP :, :] = jnp.zeros(((64 - PARAMS) * CAP, DEVS), F32)

    def chunk(at, carry):
        base = pl.multiple_of(at * 8, 8)
        values = [rows_ref[pl.ds(k * CAP + base, 8), :] for k in range(PARAMS)]
        code = code_t_ref[pl.ds(base, 8), :]
        camera = cameras_of(camera_ref, (code >> 14) & 3)
        unused, pull = jax.vjp(lambda given: project(given, camera), values)
        (grads,) = pull([cot_ref[pl.ds(k * CAP + base, 8), :] for k in range(VALS)])
        for k in range(PARAMS):
            grad_ref[pl.ds(k * CAP + base, 8), :] = jnp.where(code >= 0, grads[k], 0.0)
        return carry

    lax.fori_loop(0, CAP // 8, chunk, 0)
    send_rows.wait()

    def scatter(step, carry):
        for odd in range(2):
            rank = step * 2 + odd
            half = (code_t_ref[pl.ds(rank, 1), :] >> 13) & 1
            mine = jnp.concatenate(
                [grad_ref[pl.ds(group * 8 * CAP + rank, 8, stride=CAP), :] for group in range(8)],
                axis=0,
            )
            both = jnp.concatenate(
                [jnp.where(half == 0, mine, 0.0), jnp.where(half == 1, mine, 0.0)], axis=0
            )
            spread_ref[odd] = both.T
            for first in range(0, DEVS, 2 * TABLES):
                rows = [row_smem[rank, first + at] for at in range(2 * TABLES)]
                olds = [
                    tables[at % TABLES][pl.ds(rows[at], 1), :] for at in range(2 * TABLES)
                ]
                news = [
                    olds[at] + spread_ref[odd, first + at : first + at + 1, :]
                    for at in range(TABLES)
                ]
                for at in range(TABLES, 2 * TABLES):
                    old = jnp.where(rows[at] == rows[at - TABLES], news[at - TABLES], olds[at])
                    news.append(old + spread_ref[odd, first + at : first + at + 1, :])
                for at in range(2 * TABLES):
                    tables[at % TABLES][pl.ds(rows[at], 1), :] = news[at]
        return carry

    lax.fori_loop(0, CAP // 2, scatter, 0)

    def finish(part, carry):
        for copy in fetch(part):
            copy.wait()
        for at in range(SPAN // 256):
            rows = pl.ds(pl.multiple_of(part * (SPAN // 2) + at * 128, 128), 128)
            total = tables[0][rows, :]
            for table in tables[1:]:
                total = total + table[rows, :]
            flip_ref[at] = total.T
            for half in range(2):
                span = pl.ds(pl.multiple_of(part * SPAN + at * 256 + half * 128, 128), 128)
                gradient = flip_ref[at, half * 64 : half * 64 + PARAMS, :]
                new_m = beta_first * m_ref[:, span] + (1.0 - beta_first) * gradient
                new_v = beta_second * v_ref[:, span] + (1.0 - beta_second) * gradient * gradient
                m_ref[:, span] = new_m
                v_ref[:, span] = new_v
                params_ref[:, span] = params_ref[:, span] - learn_rate * (new_m / fix_first) / (
                    jnp.sqrt(new_v / fix_second) + adam_eps
                )
        for copy in give(part):
            copy.start()
        return carry

    lax.fori_loop(0, PARTS, finish, 0)
    for part in range(PARTS):
        for copy in give(part):
            copy.wait()


def update_of(codes, cameras, arrived, rows, params, adam_m, adam_v):
    smem = pl.BlockSpec(memory_space=pltpu.SMEM)
    vmem = pl.BlockSpec(memory_space=pltpu.VMEM)
    hbm = pl.BlockSpec(memory_space=pltpu.HBM)
    whole = jax.ShapeDtypeStruct((PARAMS, GDEV), F32)
    return pl.pallas_call(
        update_kernel,
        name="update",
        out_shape=(whole, whole, whole, jax.ShapeDtypeStruct((4, 3), F32)),
        in_specs=[smem, vmem, vmem, vmem, hbm, hbm, hbm],
        out_specs=(hbm, hbm, hbm, vmem),
        scratch_shapes=[
            pltpu.VMEM((DEVS, DEVS), jnp.int32),
            pltpu.VMEM((CAP, DEVS), jnp.int32),
            pltpu.SMEM((CAP, DEVS), jnp.int32),
            pltpu.VMEM((WIDE, DEVS), F32),
            pltpu.VMEM((64 * CAP, DEVS), F32),
            pltpu.VMEM((2, DEVS, 128), F32),
            pltpu.VMEM((SPAN // 256, 128, 128), F32),
        ]
        + [pltpu.VMEM((PARAMS, GDEV), F32)] * 3
        + [pltpu.SemaphoreType.DMA((3, PARTS))] * 2
        + [pltpu.SemaphoreType.DMA]
        + [pltpu.VMEM((HALF, 128), F32)] * TABLES,
        compiler_params=pltpu.CompilerParams(vmem_limit_bytes=48 << 20),
    )(cameras, codes, arrived, rows, in_hbm(params), in_hbm(adam_m), in_hbm(adam_v))


def exchange(value):
    return lax.all_to_all(value, AXES, split_axis=0, concat_axis=0, tiled=True)


def body(
    params,
    adam_m,
    adam_v,
    cameras,
    exposure,
    entry_owner,
    entry_local,
    block_counts,
    tile_view,
    tile_spot,
    d_image,
):
    requests, entries = route(tile_view, block_counts, entry_owner, entry_local)
    codes = exchange(requests)
    table = table_of(params)
    reply, rows = reply_of(codes, cameras, table)
    arrived = exchange(reply)
    back = render_of(tile_view, tile_spot, exposure, d_image, entries, arrived)
    returned = exchange(back)
    new_params, new_m, new_v, exposure_grad = update_of(
        codes, cameras, returned, rows, params, adam_m, adam_v
    )
    return (new_params, new_m, new_v, exposure_grad)


def solution(mesh):
    both = ("tiles", "gauss")
    placed = (
        P(None, both),
        P(None, both),
        P(None, both),
        P(),
        P(),
        P(both, None),
        P(both, None),
        P(both),
        P(both),
        P(both),
        P(both, None, None),
    )
    return jax.shard_map(
        body,
        mesh=mesh,
        in_specs=placed,
        out_specs=(P(None, both), P(None, both), P(None, both), P()),
        check_vma=False,
    )
```

```python
import jax
import jax.numpy as jnp
from jax import lax
from jax.experimental import pallas as pl
from jax.experimental.pallas import tpu as pltpu
from jax.sharding import PartitionSpec as P

AXES = ("tiles", "gauss")
DEVS = 128
CAP = 48
TILES = 4
SLOTS = 1024
BLOCK = 256
NBLK = 4
TPIX = 256
TILE = 16
ACROSS = 240
IMG_W = 3840
IMG_H = 2160
PARAMS = 59
GDEV = 16384
HALF = GDEV // 2
VALS = 9
USED = CAP * VALS
DEEP = CAP // 2
ROWS = DEEP * VALS
WIDE = 512
TABLES = 4
UNROLL = 16

sh_c0 = 0.28209479177387814
sh_c1 = 0.4886025119029199
sh_c2 = (
    1.0925484305920792,
    -1.0925484305920792,
    0.31539156525252005,
    -1.0925484305920792,
    0.5462742152960396,
)
sh_c3 = (
    -0.5900435899266435,
    2.890611442640554,
    -0.4570457994644658,
    0.3731763325901154,
    -0.4570457994644658,
    1.445305721320277,
    -0.5900435899266435,
)
beta_first = 0.9
beta_second = 0.999
learn_rate = 0.01
adam_eps = 1e-08
fix_first = 1.0
fix_second = 0.632304575229036
blur_add = 0.3

F32 = jnp.float32
BF16 = jnp.bfloat16


def sh_color(coefficients, unit_x, unit_y, unit_z):
    square_x = unit_x * unit_x
    square_y = unit_y * unit_y
    square_z = unit_z * unit_z
    basis_list = [
        -sh_c1 * unit_y,
        sh_c1 * unit_z,
        -sh_c1 * unit_x,
        sh_c2[0] * unit_x * unit_y,
        sh_c2[1] * unit_y * unit_z,
        sh_c2[2] * (2.0 * square_z - square_x - square_y),
        sh_c2[3] * unit_x * unit_z,
        sh_c2[4] * (square_x - square_y),
        sh_c3[0] * unit_y * (3.0 * square_x - square_y),
        sh_c3[1] * unit_x * unit_y * unit_z,
        sh_c3[2] * unit_y * (4.0 * square_z - square_x - square_y),
        sh_c3[3] * unit_z * (2.0 * square_z - 3.0 * square_x - 3.0 * square_y),
        sh_c3[4] * unit_x * (4.0 * square_z - square_x - square_y),
        sh_c3[5] * unit_z * (square_x - square_y),
        sh_c3[6] * unit_x * (square_x - 3.0 * square_y),
    ]
    colors = []
    for channel in range(3):
        summed = 0.5 + sh_c0 * coefficients[channel]
        for index_k in range(15):
            summed = summed + basis_list[index_k] * coefficients[3 * (index_k + 1) + channel]
        colors.append(jnp.maximum(summed, 0.0))
    return colors


def project(values, camera):
    points = [values[0], values[1], values[2]]
    matrix = [[camera[3 * row_at + col_at] for col_at in range(3)] for row_at in range(3)]
    translation = [camera[9], camera[10], camera[11]]
    focal_len = camera[12]
    viewed = [
        matrix[row_at][0] * points[0]
        + matrix[row_at][1] * points[1]
        + matrix[row_at][2] * points[2]
        + translation[row_at]
        for row_at in range(3)
    ]
    inverse_depth = 1.0 / viewed[2]
    screen_x = focal_len * viewed[0] * inverse_depth + 0.5 * IMG_W
    screen_y = focal_len * viewed[1] * inverse_depth + 0.5 * IMG_H
    slope_x = focal_len * viewed[0] * inverse_depth * inverse_depth
    slope_y = focal_len * viewed[1] * inverse_depth * inverse_depth
    jac_w = [
        [
            focal_len * inverse_depth * matrix[0][col_at] - slope_x * matrix[2][col_at]
            for col_at in range(3)
        ],
        [
            focal_len * inverse_depth * matrix[1][col_at] - slope_y * matrix[2][col_at]
            for col_at in range(3)
        ],
    ]
    quat_len = jnp.sqrt(
        values[6] * values[6]
        + values[7] * values[7]
        + values[8] * values[8]
        + values[9] * values[9]
    )
    quat_w = values[6] / quat_len
    quat_x = values[7] / quat_len
    quat_y = values[8] / quat_len
    quat_z = values[9] / quat_len
    rotation = [
        [
            1.0 - 2.0 * (quat_y * quat_y + quat_z * quat_z),
            2.0 * (quat_x * quat_y - quat_w * quat_z),
            2.0 * (quat_x * quat_z + quat_w * quat_y),
        ],
        [
            2.0 * (quat_x * quat_y + quat_w * quat_z),
            1.0 - 2.0 * (quat_x * quat_x + quat_z * quat_z),
            2.0 * (quat_y * quat_z - quat_w * quat_x),
        ],
        [
            2.0 * (quat_x * quat_z - quat_w * quat_y),
            2.0 * (quat_y * quat_z + quat_w * quat_x),
            1.0 - 2.0 * (quat_x * quat_x + quat_y * quat_y),
        ],
    ]
    extent = [jnp.exp(values[3]), jnp.exp(values[4]), jnp.exp(values[5])]
    spread = [
        [
            (
                jac_w[row_at][0] * rotation[0][col_at]
                + jac_w[row_at][1] * rotation[1][col_at]
                + jac_w[row_at][2] * rotation[2][col_at]
            )
            * extent[col_at]
            for col_at in range(3)
        ]
        for row_at in range(2)
    ]
    cov_a = (
        spread[0][0] * spread[0][0]
        + spread[0][1] * spread[0][1]
        + spread[0][2] * spread[0][2]
        + blur_add
    )
    cov_b = spread[0][0] * spread[1][0] + spread[0][1] * spread[1][1] + spread[0][2] * spread[1][2]
    cov_c = (
        spread[1][0] * spread[1][0]
        + spread[1][1] * spread[1][1]
        + spread[1][2] * spread[1][2]
        + blur_add
    )
    determinant = cov_a * cov_c - cov_b * cov_b
    logit = values[10]
    log_opacity = jnp.minimum(logit, 0.0) - jnp.log(1.0 + jnp.exp(-jnp.abs(logit)))
    center = [
        -(
            matrix[0][col_at] * translation[0]
            + matrix[1][col_at] * translation[1]
            + matrix[2][col_at] * translation[2]
        )
        for col_at in range(3)
    ]
    offset = [points[col_at] - center[col_at] for col_at in range(3)]
    distance = jnp.sqrt(offset[0] * offset[0] + offset[1] * offset[1] + offset[2] * offset[2])
    colors = sh_color(
        values[11:PARAMS], offset[0] / distance, offset[1] / distance, offset[2] / distance
    )
    return [
        screen_x,
        screen_y,
        cov_c / determinant,
        -cov_b / determinant,
        cov_a / determinant,
        log_opacity,
    ] + colors


def in_hbm(value):
    return pltpu.with_memory_space_constraint(value, pltpu.HBM)


def iota(shape, dim):
    return lax.broadcasted_iota(jnp.int32, shape, dim)


def mxu(left, right):
    return jnp.dot(left, right, preferred_element_type=F32)


def mxu_bt(left, right):
    return lax.dot_general(left, right, (((1,), (1,)), ((), ())), preferred_element_type=F32)


def split_two(value):
    high = value.astype(BF16)
    low = (value - high.astype(F32)).astype(BF16)
    return high, low


def split_three(value):
    high = value.astype(BF16).astype(F32)
    rest = value - high
    middle = rest.astype(BF16).astype(F32)
    low = (rest - middle).astype(BF16).astype(F32)
    return high, middle, low


def upper_strict():
    return (iota((BLOCK, BLOCK), 0) < iota((BLOCK, BLOCK), 1)).astype(F32).astype(BF16)


def route_kernel(
    view_hbm,
    count_hbm,
    owner_hbm,
    local_hbm,
    req_ref,
    entry_ref,
    view_ref,
    count_ref,
    owner_ref,
    local_ref,
    flip_ref,
    sems,
):
    copies = [
        pltpu.make_async_copy(source, target, sems.at[at])
        for at, (source, target) in enumerate(
            (
                (view_hbm, view_ref),
                (count_hbm, count_ref),
                (owner_hbm, owner_ref),
                (local_hbm, local_ref),
            )
        )
    ]
    for copy in copies:
        copy.start()
    tri = upper_strict()
    for copy in copies:
        copy.wait()
    before = jnp.zeros((DEVS, 1), F32)
    total = jnp.zeros((2 * CAP, DEVS), F32)
    for tile in range(TILES):
        view = view_ref[tile]
        slots = slice(tile * SLOTS, (tile + 1) * SLOTS)
        alive = (iota((1, SLOTS), 1) >> 8) < count_ref[tile]
        owner = jnp.where(alive, owner_ref[tile : tile + 1, :], -1)
        local = local_ref[tile : tile + 1, :]
        one_hot = (iota((DEVS, SLOTS), 0) == owner).astype(F32)
        one_hot_b = one_hot.astype(BF16)
        ranks = []
        for block in range(NBLK):
            span = slice(block * BLOCK, (block + 1) * BLOCK)
            earlier = mxu(one_hot_b[:, span], tri) + before
            ranks.append(jnp.sum(one_hot[:, span] * earlier, axis=0, keepdims=True))
            last = (block + 1) * BLOCK
            before = earlier[:, BLOCK - 1 : BLOCK] + one_hot[:, last - 1 : last]
        rank = jnp.where(owner >= 0, jnp.concatenate(ranks, axis=1).astype(jnp.int32), -1)
        code = (
            view * GDEV + ((local >> 7) & 1) * HALF + ((local >> 8) << 7) + (local & 127) + 1
        )
        here = iota((CAP, SLOTS), 0) == rank
        high = jnp.where(here, (code >> 8).astype(F32), 0.0).astype(BF16)
        low = jnp.where(here, (code & 255).astype(F32), 0.0).astype(BF16)
        total = total + mxu_bt(jnp.concatenate([high, low], axis=0), one_hot_b)
        entry_ref[0:1, slots] = owner
        entry_ref[1:2, slots] = rank
    flip_ref[...] = jnp.zeros_like(flip_ref)
    flip_ref[0:CAP, :] = total[0:CAP] * 256.0 + total[CAP : 2 * CAP]
    req_ref[...] = flip_ref[...].T.astype(jnp.int32) - 1


def route(tile_view, block_counts, entry_owner, entry_local):
    hbm = pl.BlockSpec(memory_space=pltpu.HBM)
    vmem = pl.BlockSpec(memory_space=pltpu.VMEM)
    return pl.pallas_call(
        route_kernel,
        name="route",
        out_shape=(
            jax.ShapeDtypeStruct((DEVS, DEVS), jnp.int32),
            jax.ShapeDtypeStruct((8, TILES * SLOTS), jnp.int32),
        ),
        in_specs=[hbm, hbm, hbm, hbm],
        out_specs=(vmem, vmem),
        scratch_shapes=[
            pltpu.SMEM((TILES,), jnp.int32),
            pltpu.SMEM((TILES,), jnp.int32),
            pltpu.VMEM((TILES, SLOTS), jnp.int32),
            pltpu.VMEM((TILES, SLOTS), jnp.int32),
            pltpu.VMEM((DEVS, DEVS), F32),
            pltpu.SemaphoreType.DMA((4,)),
        ],
        compiler_params=pltpu.CompilerParams(vmem_limit_bytes=16 << 20),
    )(*[in_hbm(given) for given in (tile_view, block_counts, entry_owner, entry_local)])


PIECES = 8
PIECE = HALF // PIECES


def table_kernel(params_hbm, table_hbm, params_ref, table_ref, in_sems, out_sems):
    takes = []
    gives = []
    for piece in range(PIECES):
        cols = pl.ds(piece * 2 * PIECE, 2 * PIECE)
        takes.append(
            pltpu.make_async_copy(params_hbm.at[:, cols], params_ref.at[:, cols], in_sems.at[piece])
        )
        rows = pl.ds(piece * PIECE, PIECE)
        gives.append(
            pltpu.make_async_copy(table_ref.at[rows], table_hbm.at[rows], out_sems.at[piece])
        )
    for copy in takes:
        copy.start()
    gap = jnp.zeros((64 - PARAMS, 128), F32)
    for piece in range(PIECES):
        takes[piece].wait()
        for at in range(piece * (PIECE // 128), (piece + 1) * (PIECE // 128)):
            both = jnp.concatenate(
                [
                    params_ref[:, at * 256 : at * 256 + 128],
                    gap,
                    params_ref[:, at * 256 + 128 : at * 256 + 256],
                    gap,
                ],
                axis=0,
            )
            table_ref[at * 128 : (at + 1) * 128, :] = both.T
        gives[piece].start()
    for copy in gives:
        copy.wait()


def table_of(params):
    hbm = pl.BlockSpec(memory_space=pltpu.HBM)
    return pl.pallas_call(
        table_kernel,
        name="table",
        out_shape=pltpu.HBM((HALF, 128), F32),
        in_specs=[hbm],
        out_specs=hbm,
        scratch_shapes=[
            pltpu.VMEM((PARAMS, GDEV), F32),
            pltpu.VMEM((HALF, 128), F32),
            pltpu.SemaphoreType.DMA((PIECES,)),
            pltpu.SemaphoreType.DMA((PIECES,)),
        ],
        compiler_params=pltpu.CompilerParams(vmem_limit_bytes=24 << 20),
        cost_estimate=pl.CostEstimate(flops=1 << 20, bytes_accessed=9 << 20, transcendentals=0),
    )(in_hbm(params))


def cameras_of(camera_ref, view):
    return [
        jnp.where(
            view == 0,
            camera_ref[0, at],
            jnp.where(
                view == 1,
                camera_ref[1, at],
                jnp.where(view == 2, camera_ref[2, at], camera_ref[3, at]),
            ),
        )
        for at in range(13)
    ]


def reply_kernel(
    camera_ref,
    code_ref,
    table_hbm,
    reply_ref,
    rows_ref,
    code_t_ref,
    row_t_ref,
    row_smem,
    table_ref,
    got_ref,
    proj_ref,
    table_sems,
    row_sem,
):
    copies = []
    for piece in range(PIECES):
        span = pl.ds(piece * (HALF // PIECES), HALF // PIECES)
        copies.append(
            pltpu.make_async_copy(table_hbm.at[span], table_ref.at[span], table_sems.at[piece])
        )
    for copy in copies:
        copy.start()
    code_t_ref[...] = code_ref[...].T
    row_t_ref[...] = code_t_ref[0:CAP, :] & (HALF - 1)
    send_rows = pltpu.make_async_copy(row_t_ref, row_smem, row_sem)
    send_rows.start()
    proj_ref[USED:WIDE, :] = jnp.zeros((WIDE - USED, DEVS), F32)
    send_rows.wait()
    for copy in copies:
        copy.wait()

    def gather(step, carry):
        for odd in range(2):
            rank = step * 2 + odd
            for src in range(DEVS):
                got_ref[odd, src : src + 1, :] = table_ref[pl.ds(row_smem[rank, src], 1), :]
            both = got_ref[odd].T
            half = (code_t_ref[pl.ds(rank, 1), :] >> 13) & 1
            picked = jnp.where(half == 0, both[0:64], both[64:128])
            for group in range(8):
                rows_ref[pl.ds(group * 8 * CAP + rank, 8, stride=CAP), :] = picked[
                    group * 8 : (group + 1) * 8
                ]
        return carry

    lax.fori_loop(0, CAP // 2, gather, 0)

    def chunk(at, carry):
        base = pl.multiple_of(at * 8, 8)
        values = [rows_ref[pl.ds(k * CAP + base, 8), :] for k in range(PARAMS)]
        view = (code_t_ref[pl.ds(base, 8), :] >> 14) & 3
        for k, value in enumerate(project(values, cameras_of(camera_ref, view))):
            proj_ref[pl.ds(k * CAP + base, 8), :] = value
        return carry

    lax.fori_loop(0, CAP // 8, chunk, 0)
    for part in range(WIDE // 128):
        reply_ref[:, part, :] = proj_ref[part * 128 : (part + 1) * 128, :].T


def reply_of(codes, cameras, table):
    smem = pl.BlockSpec(memory_space=pltpu.SMEM)
    vmem = pl.BlockSpec(memory_space=pltpu.VMEM)
    hbm = pl.BlockSpec(memory_space=pltpu.HBM)
    return pl.pallas_call(
        reply_kernel,
        name="reply",
        out_shape=(
            jax.ShapeDtypeStruct((DEVS, WIDE // 128, 128), F32),
            jax.ShapeDtypeStruct((64 * CAP, DEVS), F32),
        ),
        in_specs=[smem, vmem, hbm],
        out_specs=(vmem, vmem),
        scratch_shapes=[
            pltpu.VMEM((DEVS, DEVS), jnp.int32),
            pltpu.VMEM((CAP, DEVS), jnp.int32),
            pltpu.SMEM((CAP, DEVS), jnp.int32),
            pltpu.VMEM((HALF, 128), F32),
            pltpu.VMEM((2, DEVS, 128), F32),
            pltpu.VMEM((WIDE, DEVS), F32),
            pltpu.SemaphoreType.DMA((PIECES,)),
            pltpu.SemaphoreType.DMA,
        ],
        compiler_params=pltpu.CompilerParams(vmem_limit_bytes=48 << 20),
    )(cameras, codes, in_hbm(table))


def render_kernel(
    view_hbm,
    spot_hbm,
    gain_hbm,
    d_image_hbm,
    entry_ref,
    arrived_ref,
    back_ref,
    view_ref,
    spot_ref,
    gain_ref,
    d_image_ref,
    sems,
    split_ref,
    tri_ref,
    low_ref,
    basis_t_ref,
    basis_ref,
    alpha_ref,
    q_ref,
    shade_ref,
    sum_ref,
    high_ref,
    low_part_ref,
    fold_ref,
):
    copies = [
        pltpu.make_async_copy(source, target, sems.at[at])
        for at, (source, target) in enumerate(
            (
                (view_hbm, view_ref),
                (spot_hbm, spot_ref),
                (gain_hbm, gain_ref),
                (d_image_hbm, d_image_ref),
            )
        )
    ]
    for copy in copies:
        copy.start()
    for part in range(WIDE // 128):
        sum_ref[part * 128 : (part + 1) * 128, 0:128] = arrived_ref[:, part, :].T
    for k in range(VALS):
        for deep in range(2):
            fold_ref[k * DEEP : (k + 1) * DEEP, deep * 128 : (deep + 1) * 128] = sum_ref[
                k * CAP + deep * DEEP : k * CAP + (deep + 1) * DEEP, 0:128
            ]
    for piece, value in enumerate(split_three(fold_ref[...])):
        split_ref[:, piece * 256 : (piece + 1) * 256] = value.astype(BF16)
    upper = upper_strict()
    lower = (iota((BLOCK, BLOCK), 0) > iota((BLOCK, BLOCK), 1)).astype(F32).astype(BF16)
    tri_ref[0:BLOCK, :] = upper
    tri_ref[BLOCK : 2 * BLOCK, :] = upper
    low_ref[0:BLOCK, :] = lower
    low_ref[BLOCK : 2 * BLOCK, :] = lower

    def monomial(which, x, y):
        return jnp.where(
            which == 0,
            1.0,
            jnp.where(
                which == 1,
                x,
                jnp.where(
                    which == 2,
                    y,
                    jnp.where(
                        which == 3,
                        x * x,
                        jnp.where(which == 4, x * y, jnp.where(which == 5, y * y, 0.0)),
                    ),
                ),
            ),
        )

    pixel = iota((TPIX, 128), 0)
    lane = iota((TPIX, 128), 1)
    basis_t_ref[...] = jnp.where(
        lane < 24,
        monomial(lane & 7, (pixel & 15).astype(F32) - 7.5, (pixel >> 4).astype(F32) - 7.5),
        0.0,
    ).astype(BF16)
    pixel = iota((16, TPIX), 1)
    basis = monomial(
        iota((16, TPIX), 0), (pixel & 15).astype(F32) - 7.5, (pixel >> 4).astype(F32) - 7.5
    ).astype(BF16)
    basis_ref[:, 0:TPIX] = basis
    basis_ref[:, TPIX : 2 * TPIX] = basis
    fold_ref[...] = jnp.zeros_like(fold_ref)

    def rows8(rows):
        at_row = iota((8, rows[0].shape[1]), 0)
        out = jnp.zeros((8, rows[0].shape[1]), F32)
        for at, row in enumerate(rows):
            out = jnp.where(at_row == at, row, out)
        return out

    def tile_step(tile, expo):
        view = view_ref[tile]
        spot = spot_ref[tile]
        line = spot // ACROSS
        mid_x = ((spot - line * ACROSS) * TILE + TILE // 2).astype(F32)
        mid_y = (line * TILE + TILE // 2).astype(F32)
        gains = [gain_ref[view, ch] for ch in range(3)]
        d_rows = [d_image_ref[ch, pl.ds(tile, 1), :] for ch in range(3)]
        d1, d2, d3 = split_three(rows8(d_rows))
        pixel_rows = jnp.concatenate([d1, d2, d3, jnp.zeros((8, TPIX), F32)], axis=0).astype(BF16)
        pixel_rows = jnp.concatenate([pixel_rows, pixel_rows], axis=1)
        g1, g2, g3 = split_three(rows8([gains[ch] * d_rows[ch] for ch in range(3)]))
        shade_ref[...] = (
            jnp.concatenate([g1, g1, g2, g2, g1, g3, jnp.zeros((80, TPIX), F32)], axis=0)
            .T.astype(BF16)
        )
        slots = pl.ds(pl.multiple_of(tile * SLOTS, SLOTS), SLOTS)
        owner = entry_ref[0:1, slots]
        rank = entry_ref[1:2, slots]
        deep = (rank >= DEEP).astype(jnp.int32)
        one_hot = (iota((2 * DEVS, SLOTS), 0) == owner + DEVS * deep).astype(F32).astype(BF16)
        found = mxu(split_ref[...], jnp.concatenate([one_hot, one_hot, one_hot], axis=0))
        here = iota((DEEP, SLOTS), 0) == rank - DEEP * deep
        vals = [
            jnp.sum(jnp.where(here, found[k * DEEP : (k + 1) * DEEP], 0.0), axis=0, keepdims=True)
            for k in range(VALS)
        ]
        shift_x = vals[0] - mid_x
        shift_y = vals[1] - mid_y
        con_a, con_b, con_c = vals[2], vals[3], vals[4]
        lin_x = con_a * shift_x + con_b * shift_y
        lin_y = con_c * shift_y + con_b * shift_x
        level_row = vals[5] - 0.5 * (lin_x * shift_x + lin_y * shift_y)
        poly = rows8(
            [
                jnp.where(owner >= 0, level_row, -200.0),
                lin_x,
                lin_y,
                -0.5 * con_a,
                -con_b,
                -0.5 * con_c,
            ]
        )
        poly = jnp.where(owner >= 0, poly, jnp.where(iota((8, SLOTS), 0) == 0, -200.0, 0.0))
        k1, k2, k3 = split_three(poly)
        poly_rows = jnp.concatenate([k1, k2, k3, jnp.zeros((104, SLOTS), F32)], axis=0).astype(
            BF16
        )
        color = rows8(vals[6:9])
        c1, c2, c3 = split_three(color)
        color_rows = jnp.concatenate(
            [c1, c2, c1, c2, c3, c1, jnp.zeros((80, SLOTS), F32)], axis=0
        ).astype(BF16)
        spans = [slice(block * BLOCK, (block + 1) * BLOCK) for block in range(NBLK)]
        for block, span in enumerate(spans):
            alpha = jnp.exp(mxu(basis_t_ref[...], poly_rows[:, span]))
            alpha_ref[block] = alpha
            fade = alpha * (1.0 + alpha * (0.5 + alpha * (1.0 / 3.0)))
            fade_hi, fade_lo = split_two(fade)
            high_ref[block] = fade_hi
            low_part_ref[block] = fade_lo
        summed = mxu(
            jnp.concatenate(
                [
                    high_ref[...].reshape(NBLK * TPIX, BLOCK),
                    low_part_ref[...].reshape(NBLK * TPIX, BLOCK),
                ],
                axis=1,
            ),
            tri_ref[...],
        )
        level = jnp.zeros((TPIX, 1), F32)
        seen_parts = []
        for block, span in enumerate(spans):
            alpha = alpha_ref[block]
            here_sum = summed[block * TPIX : (block + 1) * TPIX] + level
            weight = alpha * jnp.exp(-here_sum)
            edge = alpha[:, BLOCK - 1 : BLOCK]
            level = here_sum[:, BLOCK - 1 : BLOCK] + edge * (
                1.0 + edge * (0.5 + edge * (1.0 / 3.0))
            )
            q_val = mxu(shade_ref[...], color_rows[:, span]) * weight
            q_ref[block] = q_val
            q_hi, q_lo = split_two(q_val)
            high_ref[block] = q_hi
            low_part_ref[block] = q_lo
            weight_hi, weight_lo = split_two(weight)
            seen = mxu(pixel_rows, jnp.concatenate([weight_hi, weight_lo], axis=0))
            seen_parts.append(seen[0:8] + seen[8:16] + seen[16:24])
        seen = jnp.concatenate(seen_parts, axis=1)
        expo_cols = jnp.sum(color * seen, axis=1, keepdims=True)
        later = mxu(
            jnp.concatenate(
                [
                    high_ref[...].reshape(NBLK * TPIX, BLOCK),
                    low_part_ref[...].reshape(NBLK * TPIX, BLOCK),
                ],
                axis=1,
            ),
            low_ref[...],
        )
        tail = jnp.zeros((TPIX, 1), F32)
        grad_parts = [None] * NBLK
        for block in reversed(range(NBLK)):
            alpha = alpha_ref[block]
            q_val = q_ref[block]
            here_sum = later[block * TPIX : (block + 1) * TPIX] + tail
            d_exp = q_val - here_sum * (alpha * (1.0 + alpha * (1.0 + alpha)))
            tail = here_sum[:, 0:1] + q_val[:, 0:1]
            d_hi, d_lo = split_two(d_exp)
            grad_parts[block] = mxu(basis_ref[...], jnp.concatenate([d_hi, d_lo], axis=0))[0:8]
        grad = jnp.concatenate(grad_parts, axis=1)
        d_poly = [grad[k : k + 1] for k in range(6)]
        grads = [
            d_poly[1] * con_a + d_poly[2] * con_b - d_poly[0] * lin_x,
            d_poly[1] * con_b + d_poly[2] * con_c - d_poly[0] * lin_y,
            shift_x * d_poly[1] - 0.5 * (d_poly[3] + shift_x * shift_x * d_poly[0]),
            shift_y * d_poly[1] + shift_x * d_poly[2] - d_poly[4] - shift_x * shift_y * d_poly[0],
            shift_y * d_poly[2] - 0.5 * (d_poly[5] + shift_y * shift_y * d_poly[0]),
            d_poly[0],
            gains[0] * seen[0:1],
            gains[1] * seen[1:2],
            gains[2] * seen[2:3],
        ]
        high_rows = []
        low_rows = []
        for value in grads:
            high = value.astype(BF16).astype(F32)
            high_rows.append(jnp.where(here, high, 0.0))
            low_rows.append(jnp.where(here, value - high, 0.0))
        both = mxu_bt(jnp.concatenate(high_rows + low_rows, axis=0).astype(BF16), one_hot)
        fold_ref[...] += both[0:ROWS] + both[ROWS : 2 * ROWS]
        lane_at = iota((8, 128), 1) - (USED - 384) - 3 * view
        return expo + jnp.where(
            (lane_at == iota((8, 128), 0)) & (lane_at < 3), expo_cols, 0.0
        )

    for copy in copies:
        copy.wait()
    expo = lax.fori_loop(0, TILES, tile_step, jnp.zeros((8, 128), F32))
    sum_ref[USED:WIDE, :] = jnp.zeros((WIDE - USED, DEVS), F32)
    for k in range(VALS):
        for deep in range(2):
            sum_ref[k * CAP + deep * DEEP : k * CAP + (deep + 1) * DEEP, :] = fold_ref[
                k * DEEP : (k + 1) * DEEP, deep * 128 : (deep + 1) * 128
            ]
    for part in range(WIDE // 128):
        span = slice(part * 128, (part + 1) * 128)
        back = sum_ref[span, :].T
        if part == WIDE // 128 - 1:
            back = back + jnp.sum(expo, axis=0, keepdims=True)
        back_ref[:, part, :] = back


def render_of(tile_view, tile_spot, exposure, d_image, entries, arrived):
    hbm = pl.BlockSpec(memory_space=pltpu.HBM)
    vmem = pl.BlockSpec(memory_space=pltpu.VMEM)
    given = (tile_view, tile_spot, exposure, jnp.transpose(d_image, (1, 0, 2)))
    return pl.pallas_call(
        render_kernel,
        name="render",
        out_shape=jax.ShapeDtypeStruct((DEVS, WIDE // 128, 128), F32),
        in_specs=[hbm, hbm, hbm, hbm, vmem, vmem],
        out_specs=vmem,
        scratch_shapes=[
            pltpu.SMEM((TILES,), jnp.int32),
            pltpu.SMEM((TILES,), jnp.int32),
            pltpu.SMEM((4, 3), F32),
            pltpu.VMEM((3, TILES, TPIX), F32),
            pltpu.SemaphoreType.DMA((4,)),
            pltpu.VMEM((ROWS, 6 * DEVS), BF16),
            pltpu.VMEM((2 * BLOCK, BLOCK), BF16),
            pltpu.VMEM((2 * BLOCK, BLOCK), BF16),
            pltpu.VMEM((TPIX, 128), BF16),
            pltpu.VMEM((16, 2 * TPIX), BF16),
            pltpu.VMEM((NBLK, TPIX, BLOCK), F32),
            pltpu.VMEM((NBLK, TPIX, BLOCK), F32),
            pltpu.VMEM((TPIX, 128), BF16),
            pltpu.VMEM((WIDE, DEVS), F32),
            pltpu.VMEM((NBLK, TPIX, BLOCK), BF16),
            pltpu.VMEM((NBLK, TPIX, BLOCK), BF16),
            pltpu.VMEM((ROWS, 2 * DEVS), F32),
        ],
        compiler_params=pltpu.CompilerParams(vmem_limit_bytes=32 << 20),
    )(*[in_hbm(value) for value in given], entries, arrived)


PARTS = 8
SPAN = GDEV // PARTS


def update_kernel(
    camera_ref,
    code_ref,
    arrived_ref,
    rows_ref,
    params_hbm,
    m_hbm,
    v_hbm,
    params_out,
    m_out,
    v_out,
    expo_ref,
    code_t_ref,
    row_t_ref,
    row_smem,
    cot_ref,
    grad_ref,
    spread_ref,
    flip_ref,
    params_ref,
    m_ref,
    v_ref,
    in_sems,
    out_sems,
    row_sem,
    *tables,
):
    held = ((params_hbm, params_ref, params_out), (m_hbm, m_ref, m_out), (v_hbm, v_ref, v_out))

    def fetch(part):
        span = pl.ds(pl.multiple_of(part * SPAN, SPAN), SPAN)
        return [
            pltpu.make_async_copy(source.at[:, span], kept.at[:, span], in_sems.at[at, part])
            for at, (source, kept, unused) in enumerate(held)
        ]

    def give(part):
        span = pl.ds(pl.multiple_of(part * SPAN, SPAN), SPAN)
        return [
            pltpu.make_async_copy(kept.at[:, span], target.at[:, span], out_sems.at[at, part])
            for at, (unused, kept, target) in enumerate(held)
        ]

    code_t_ref[...] = code_ref[...].T
    row_t_ref[...] = code_t_ref[0:CAP, :] & (HALF - 1)
    send_rows = pltpu.make_async_copy(row_t_ref, row_smem, row_sem)
    send_rows.start()
    for part in range(PARTS):
        for copy in fetch(part):
            copy.start()
    shares = jnp.sum(arrived_ref[:, 3, :], axis=0, keepdims=True) * (1.0 / DEVS)
    for view in range(TILES):
        first = USED - 384 + 3 * view
        expo_ref[view : view + 1, :] = shares[:, first : first + 3]
    for part in range(WIDE // 128):
        cot_ref[part * 128 : (part + 1) * 128, :] = arrived_ref[:, part, :].T
    for table in tables:
        table[...] = jnp.zeros_like(table)
    grad_ref[PARAMS * CAP :, :] = jnp.zeros(((64 - PARAMS) * CAP, DEVS), F32)

    def chunk(at, carry):
        base = pl.multiple_of(at * 8, 8)
        values = [rows_ref[pl.ds(k * CAP + base, 8), :] for k in range(PARAMS)]
        code = code_t_ref[pl.ds(base, 8), :]
        camera = cameras_of(camera_ref, (code >> 14) & 3)
        unused, pull = jax.vjp(lambda given: project(given, camera), values)
        (grads,) = pull([cot_ref[pl.ds(k * CAP + base, 8), :] for k in range(VALS)])
        for k in range(PARAMS):
            grad_ref[pl.ds(k * CAP + base, 8), :] = jnp.where(code >= 0, grads[k], 0.0)
        return carry

    lax.fori_loop(0, CAP // 8, chunk, 0)
    send_rows.wait()

    def scatter(step, carry):
        for odd in range(2):
            rank = step * 2 + odd
            half = (code_t_ref[pl.ds(rank, 1), :] >> 13) & 1
            mine = jnp.concatenate(
                [grad_ref[pl.ds(group * 8 * CAP + rank, 8, stride=CAP), :] for group in range(8)],
                axis=0,
            )
            both = jnp.concatenate(
                [jnp.where(half == 0, mine, 0.0), jnp.where(half == 1, mine, 0.0)], axis=0
            )
            spread_ref[odd] = both.T
            for first in range(0, DEVS, 2 * TABLES):
                rows = [row_smem[rank, first + at] for at in range(2 * TABLES)]
                olds = [
                    tables[at % TABLES][pl.ds(rows[at], 1), :] for at in range(2 * TABLES)
                ]
                news = [
                    olds[at] + spread_ref[odd, first + at : first + at + 1, :]
                    for at in range(TABLES)
                ]
                for at in range(TABLES, 2 * TABLES):
                    old = jnp.where(rows[at] == rows[at - TABLES], news[at - TABLES], olds[at])
                    news.append(old + spread_ref[odd, first + at : first + at + 1, :])
                for at in range(2 * TABLES):
                    tables[at % TABLES][pl.ds(rows[at], 1), :] = news[at]
        return carry

    lax.fori_loop(0, CAP // 2, scatter, 0)

    def finish(part, carry):
        for copy in fetch(part):
            copy.wait()
        for at in range(SPAN // 256):
            rows = pl.ds(pl.multiple_of(part * (SPAN // 2) + at * 128, 128), 128)
            total = tables[0][rows, :]
            for table in tables[1:]:
                total = total + table[rows, :]
            flip_ref[at] = total.T
            for half in range(2):
                span = pl.ds(pl.multiple_of(part * SPAN + at * 256 + half * 128, 128), 128)
                gradient = flip_ref[at, half * 64 : half * 64 + PARAMS, :]
                new_m = beta_first * m_ref[:, span] + (1.0 - beta_first) * gradient
                new_v = beta_second * v_ref[:, span] + (1.0 - beta_second) * gradient * gradient
                m_ref[:, span] = new_m
                v_ref[:, span] = new_v
                params_ref[:, span] = params_ref[:, span] - learn_rate * (new_m / fix_first) / (
                    jnp.sqrt(new_v / fix_second) + adam_eps
                )
        for copy in give(part):
            copy.start()
        return carry

    lax.fori_loop(0, PARTS, finish, 0)
    for part in range(PARTS):
        for copy in give(part):
            copy.wait()


def update_of(codes, cameras, arrived, rows, params, adam_m, adam_v):
    smem = pl.BlockSpec(memory_space=pltpu.SMEM)
    vmem = pl.BlockSpec(memory_space=pltpu.VMEM)
    hbm = pl.BlockSpec(memory_space=pltpu.HBM)
    whole = jax.ShapeDtypeStruct((PARAMS, GDEV), F32)
    return pl.pallas_call(
        update_kernel,
        name="update",
        out_shape=(whole, whole, whole, jax.ShapeDtypeStruct((4, 3), F32)),
        in_specs=[smem, vmem, vmem, vmem, hbm, hbm, hbm],
        out_specs=(hbm, hbm, hbm, vmem),
        scratch_shapes=[
            pltpu.VMEM((DEVS, DEVS), jnp.int32),
            pltpu.VMEM((CAP, DEVS), jnp.int32),
            pltpu.SMEM((CAP, DEVS), jnp.int32),
            pltpu.VMEM((WIDE, DEVS), F32),
            pltpu.VMEM((64 * CAP, DEVS), F32),
            pltpu.VMEM((2, DEVS, 128), F32),
            pltpu.VMEM((SPAN // 256, 128, 128), F32),
        ]
        + [pltpu.VMEM((PARAMS, GDEV), F32)] * 3
        + [pltpu.SemaphoreType.DMA((3, PARTS))] * 2
        + [pltpu.SemaphoreType.DMA]
        + [pltpu.VMEM((HALF, 128), F32)] * TABLES,
        compiler_params=pltpu.CompilerParams(vmem_limit_bytes=48 << 20),
    )(cameras, codes, arrived, rows, in_hbm(params), in_hbm(adam_m), in_hbm(adam_v))


def exchange(value):
    return lax.all_to_all(value, AXES, split_axis=0, concat_axis=0, tiled=True)


def body(
    params,
    adam_m,
    adam_v,
    cameras,
    exposure,
    entry_owner,
    entry_local,
    block_counts,
    tile_view,
    tile_spot,
    d_image,
):
    requests, entries = route(tile_view, block_counts, entry_owner, entry_local)
    codes = exchange(requests)
    table = table_of(params)
    reply, rows = reply_of(codes, cameras, table)
    arrived = exchange(reply)
    back = render_of(tile_view, tile_spot, exposure, d_image, entries, arrived)
    returned = exchange(back)
    new_params, new_m, new_v, exposure_grad = update_of(
        codes, cameras, returned, rows, params, adam_m, adam_v
    )
    return (new_params, new_m, new_v, exposure_grad)


def solution(mesh):
    both = ("tiles", "gauss")
    placed = (
        P(None, both),
        P(None, both),
        P(None, both),
        P(),
        P(),
        P(both, None),
        P(both, None),
        P(both),
        P(both),
        P(both),
        P(both, None, None),
    )
    return jax.shard_map(
        body,
        mesh=mesh,
        in_specs=placed,
        out_specs=(P(None, both), P(None, both), P(None, both), P()),
        check_vma=False,
    )
```

```python
import jax
import jax.numpy as jnp
from jax import lax
from jax.experimental import pallas as pl
from jax.experimental.pallas import tpu as pltpu
from jax.sharding import PartitionSpec as P

AXES = ("tiles", "gauss")
DEVS = 128
CAP = 48
TILES = 4
SLOTS = 1024
BLOCK = 256
NBLK = 4
TPIX = 256
TILE = 16
ACROSS = 240
IMG_W = 3840
IMG_H = 2160
PARAMS = 59
GDEV = 16384
HALF = GDEV // 2
VALS = 9
USED = CAP * VALS
DEEP = CAP // 2
ROWS = DEEP * VALS
WIDE = 512
TABLES = 4
UNROLL = 16

sh_c0 = 0.28209479177387814
sh_c1 = 0.4886025119029199
sh_c2 = (
    1.0925484305920792,
    -1.0925484305920792,
    0.31539156525252005,
    -1.0925484305920792,
    0.5462742152960396,
)
sh_c3 = (
    -0.5900435899266435,
    2.890611442640554,
    -0.4570457994644658,
    0.3731763325901154,
    -0.4570457994644658,
    1.445305721320277,
    -0.5900435899266435,
)
beta_first = 0.9
beta_second = 0.999
learn_rate = 0.01
adam_eps = 1e-08
fix_first = 1.0
fix_second = 0.632304575229036
blur_add = 0.3

F32 = jnp.float32
BF16 = jnp.bfloat16


def sh_color(coefficients, unit_x, unit_y, unit_z):
    square_x = unit_x * unit_x
    square_y = unit_y * unit_y
    square_z = unit_z * unit_z
    basis_list = [
        -sh_c1 * unit_y,
        sh_c1 * unit_z,
        -sh_c1 * unit_x,
        sh_c2[0] * unit_x * unit_y,
        sh_c2[1] * unit_y * unit_z,
        sh_c2[2] * (2.0 * square_z - square_x - square_y),
        sh_c2[3] * unit_x * unit_z,
        sh_c2[4] * (square_x - square_y),
        sh_c3[0] * unit_y * (3.0 * square_x - square_y),
        sh_c3[1] * unit_x * unit_y * unit_z,
        sh_c3[2] * unit_y * (4.0 * square_z - square_x - square_y),
        sh_c3[3] * unit_z * (2.0 * square_z - 3.0 * square_x - 3.0 * square_y),
        sh_c3[4] * unit_x * (4.0 * square_z - square_x - square_y),
        sh_c3[5] * unit_z * (square_x - square_y),
        sh_c3[6] * unit_x * (square_x - 3.0 * square_y),
    ]
    colors = []
    for channel in range(3):
        summed = 0.5 + sh_c0 * coefficients[channel]
        for index_k in range(15):
            summed = summed + basis_list[index_k] * coefficients[3 * (index_k + 1) + channel]
        colors.append(jnp.maximum(summed, 0.0))
    return colors


def project(values, camera):
    points = [values[0], values[1], values[2]]
    matrix = [[camera[3 * row_at + col_at] for col_at in range(3)] for row_at in range(3)]
    translation = [camera[9], camera[10], camera[11]]
    focal_len = camera[12]
    viewed = [
        matrix[row_at][0] * points[0]
        + matrix[row_at][1] * points[1]
        + matrix[row_at][2] * points[2]
        + translation[row_at]
        for row_at in range(3)
    ]
    inverse_depth = 1.0 / viewed[2]
    screen_x = focal_len * viewed[0] * inverse_depth + 0.5 * IMG_W
    screen_y = focal_len * viewed[1] * inverse_depth + 0.5 * IMG_H
    slope_x = focal_len * viewed[0] * inverse_depth * inverse_depth
    slope_y = focal_len * viewed[1] * inverse_depth * inverse_depth
    jac_w = [
        [
            focal_len * inverse_depth * matrix[0][col_at] - slope_x * matrix[2][col_at]
            for col_at in range(3)
        ],
        [
            focal_len * inverse_depth * matrix[1][col_at] - slope_y * matrix[2][col_at]
            for col_at in range(3)
        ],
    ]
    quat_len = jnp.sqrt(
        values[6] * values[6]
        + values[7] * values[7]
        + values[8] * values[8]
        + values[9] * values[9]
    )
    quat_w = values[6] / quat_len
    quat_x = values[7] / quat_len
    quat_y = values[8] / quat_len
    quat_z = values[9] / quat_len
    rotation = [
        [
            1.0 - 2.0 * (quat_y * quat_y + quat_z * quat_z),
            2.0 * (quat_x * quat_y - quat_w * quat_z),
            2.0 * (quat_x * quat_z + quat_w * quat_y),
        ],
        [
            2.0 * (quat_x * quat_y + quat_w * quat_z),
            1.0 - 2.0 * (quat_x * quat_x + quat_z * quat_z),
            2.0 * (quat_y * quat_z - quat_w * quat_x),
        ],
        [
            2.0 * (quat_x * quat_z - quat_w * quat_y),
            2.0 * (quat_y * quat_z + quat_w * quat_x),
            1.0 - 2.0 * (quat_x * quat_x + quat_y * quat_y),
        ],
    ]
    extent = [jnp.exp(values[3]), jnp.exp(values[4]), jnp.exp(values[5])]
    spread = [
        [
            (
                jac_w[row_at][0] * rotation[0][col_at]
                + jac_w[row_at][1] * rotation[1][col_at]
                + jac_w[row_at][2] * rotation[2][col_at]
            )
            * extent[col_at]
            for col_at in range(3)
        ]
        for row_at in range(2)
    ]
    cov_a = (
        spread[0][0] * spread[0][0]
        + spread[0][1] * spread[0][1]
        + spread[0][2] * spread[0][2]
        + blur_add
    )
    cov_b = spread[0][0] * spread[1][0] + spread[0][1] * spread[1][1] + spread[0][2] * spread[1][2]
    cov_c = (
        spread[1][0] * spread[1][0]
        + spread[1][1] * spread[1][1]
        + spread[1][2] * spread[1][2]
        + blur_add
    )
    determinant = cov_a * cov_c - cov_b * cov_b
    logit = values[10]
    log_opacity = jnp.minimum(logit, 0.0) - jnp.log(1.0 + jnp.exp(-jnp.abs(logit)))
    center = [
        -(
            matrix[0][col_at] * translation[0]
            + matrix[1][col_at] * translation[1]
            + matrix[2][col_at] * translation[2]
        )
        for col_at in range(3)
    ]
    offset = [points[col_at] - center[col_at] for col_at in range(3)]
    distance = jnp.sqrt(offset[0] * offset[0] + offset[1] * offset[1] + offset[2] * offset[2])
    colors = sh_color(
        values[11:PARAMS], offset[0] / distance, offset[1] / distance, offset[2] / distance
    )
    return [
        screen_x,
        screen_y,
        cov_c / determinant,
        -cov_b / determinant,
        cov_a / determinant,
        log_opacity,
    ] + colors


def in_hbm(value):
    return pltpu.with_memory_space_constraint(value, pltpu.HBM)


def iota(shape, dim):
    return lax.broadcasted_iota(jnp.int32, shape, dim)


def mxu(left, right):
    return jnp.dot(left, right, preferred_element_type=F32)


def mxu_bt(left, right):
    return lax.dot_general(left, right, (((1,), (1,)), ((), ())), preferred_element_type=F32)


def split_two(value):
    high = value.astype(BF16)
    low = (value - high.astype(F32)).astype(BF16)
    return high, low


def split_three(value):
    high = value.astype(BF16).astype(F32)
    rest = value - high
    middle = rest.astype(BF16).astype(F32)
    low = (rest - middle).astype(BF16).astype(F32)
    return high, middle, low


def upper_strict():
    return (iota((BLOCK, BLOCK), 0) < iota((BLOCK, BLOCK), 1)).astype(F32).astype(BF16)


def route_kernel(
    view_hbm,
    count_hbm,
    owner_hbm,
    local_hbm,
    req_ref,
    entry_ref,
    view_ref,
    count_ref,
    owner_ref,
    local_ref,
    flip_ref,
    sems,
):
    copies = [
        pltpu.make_async_copy(source, target, sems.at[at])
        for at, (source, target) in enumerate(
            (
                (view_hbm, view_ref),
                (count_hbm, count_ref),
                (owner_hbm, owner_ref),
                (local_hbm, local_ref),
            )
        )
    ]
    for copy in copies:
        copy.start()
    tri = upper_strict()
    for copy in copies:
        copy.wait()
    before = jnp.zeros((DEVS, 1), F32)
    total = jnp.zeros((2 * CAP, DEVS), F32)
    for tile in range(TILES):
        view = view_ref[tile]
        slots = slice(tile * SLOTS, (tile + 1) * SLOTS)
        alive = (iota((1, SLOTS), 1) >> 8) < count_ref[tile]
        owner = jnp.where(alive, owner_ref[tile : tile + 1, :], -1)
        local = local_ref[tile : tile + 1, :]
        one_hot = (iota((DEVS, SLOTS), 0) == owner).astype(F32)
        one_hot_b = one_hot.astype(BF16)
        ranks = []
        for block in range(NBLK):
            span = slice(block * BLOCK, (block + 1) * BLOCK)
            earlier = mxu(one_hot_b[:, span], tri) + before
            ranks.append(jnp.sum(one_hot[:, span] * earlier, axis=0, keepdims=True))
            last = (block + 1) * BLOCK
            before = earlier[:, BLOCK - 1 : BLOCK] + one_hot[:, last - 1 : last]
        rank = jnp.where(owner >= 0, jnp.concatenate(ranks, axis=1).astype(jnp.int32), -1)
        code = (
            view * GDEV + ((local >> 7) & 1) * HALF + ((local >> 8) << 7) + (local & 127) + 1
        )
        here = iota((CAP, SLOTS), 0) == rank
        high = jnp.where(here, (code >> 8).astype(F32), 0.0).astype(BF16)
        low = jnp.where(here, (code & 255).astype(F32), 0.0).astype(BF16)
        total = total + mxu_bt(jnp.concatenate([high, low], axis=0), one_hot_b)
        entry_ref[0:1, slots] = owner
        entry_ref[1:2, slots] = rank
    flip_ref[...] = jnp.zeros_like(flip_ref)
    flip_ref[0:CAP, :] = total[0:CAP] * 256.0 + total[CAP : 2 * CAP]
    req_ref[...] = flip_ref[...].T.astype(jnp.int32) - 1


def route(tile_view, block_counts, entry_owner, entry_local):
    hbm = pl.BlockSpec(memory_space=pltpu.HBM)
    vmem = pl.BlockSpec(memory_space=pltpu.VMEM)
    return pl.pallas_call(
        route_kernel,
        name="route",
        out_shape=(
            jax.ShapeDtypeStruct((DEVS, DEVS), jnp.int32),
            jax.ShapeDtypeStruct((8, TILES * SLOTS), jnp.int32),
        ),
        in_specs=[hbm, hbm, hbm, hbm],
        out_specs=(vmem, vmem),
        scratch_shapes=[
            pltpu.SMEM((TILES,), jnp.int32),
            pltpu.SMEM((TILES,), jnp.int32),
            pltpu.VMEM((TILES, SLOTS), jnp.int32),
            pltpu.VMEM((TILES, SLOTS), jnp.int32),
            pltpu.VMEM((DEVS, DEVS), F32),
            pltpu.SemaphoreType.DMA((4,)),
        ],
        compiler_params=pltpu.CompilerParams(vmem_limit_bytes=16 << 20),
    )(*[in_hbm(given) for given in (tile_view, block_counts, entry_owner, entry_local)])


PIECES = 8
PIECE = HALF // PIECES


def table_kernel(params_hbm, table_hbm, params_ref, table_ref, in_sems, out_sems):
    takes = []
    gives = []
    for piece in range(PIECES):
        cols = pl.ds(piece * 2 * PIECE, 2 * PIECE)
        takes.append(
            pltpu.make_async_copy(params_hbm.at[:, cols], params_ref.at[:, cols], in_sems.at[piece])
        )
        rows = pl.ds(piece * PIECE, PIECE)
        gives.append(
            pltpu.make_async_copy(table_ref.at[rows], table_hbm.at[rows], out_sems.at[piece])
        )
    for copy in takes:
        copy.start()
    gap = jnp.zeros((64 - PARAMS, 128), F32)
    for piece in range(PIECES):
        takes[piece].wait()
        for at in range(piece * (PIECE // 128), (piece + 1) * (PIECE // 128)):
            both = jnp.concatenate(
                [
                    params_ref[:, at * 256 : at * 256 + 128],
                    gap,
                    params_ref[:, at * 256 + 128 : at * 256 + 256],
                    gap,
                ],
                axis=0,
            )
            table_ref[at * 128 : (at + 1) * 128, :] = both.T
        gives[piece].start()
    for copy in gives:
        copy.wait()


def table_of(params):
    hbm = pl.BlockSpec(memory_space=pltpu.HBM)
    return pl.pallas_call(
        table_kernel,
        name="table",
        out_shape=pltpu.HBM((HALF, 128), F32),
        in_specs=[hbm],
        out_specs=hbm,
        scratch_shapes=[
            pltpu.VMEM((PARAMS, GDEV), F32),
            pltpu.VMEM((HALF, 128), F32),
            pltpu.SemaphoreType.DMA((PIECES,)),
            pltpu.SemaphoreType.DMA((PIECES,)),
        ],
        compiler_params=pltpu.CompilerParams(vmem_limit_bytes=24 << 20),
        cost_estimate=pl.CostEstimate(flops=1 << 20, bytes_accessed=9 << 20, transcendentals=0),
    )(in_hbm(params))


def cameras_of(camera_ref, view):
    return [
        jnp.where(
            view == 0,
            camera_ref[0, at],
            jnp.where(
                view == 1,
                camera_ref[1, at],
                jnp.where(view == 2, camera_ref[2, at], camera_ref[3, at]),
            ),
        )
        for at in range(13)
    ]


def reply_kernel(
    camera_ref,
    code_ref,
    table_hbm,
    reply_ref,
    rows_ref,
    code_t_ref,
    row_t_ref,
    row_smem,
    table_ref,
    got_ref,
    proj_ref,
    table_sem,
    row_sem,
):
    take_table = pltpu.make_async_copy(table_hbm, table_ref, table_sem)
    take_table.start()
    code_t_ref[...] = code_ref[...].T
    row_t_ref[...] = code_t_ref[0:CAP, :] & (HALF - 1)
    send_rows = pltpu.make_async_copy(row_t_ref, row_smem, row_sem)
    send_rows.start()
    proj_ref[USED:WIDE, :] = jnp.zeros((WIDE - USED, DEVS), F32)
    send_rows.wait()
    take_table.wait()

    def gather(step, carry):
        for odd in range(12):
            rank = step * 12 + odd
            for src in range(DEVS):
                got_ref[odd, src : src + 1, :] = table_ref[pl.ds(row_smem[rank, src], 1), :]
            both = got_ref[odd].T
            half = (code_t_ref[pl.ds(rank, 1), :] >> 13) & 1
            picked = jnp.where(half == 0, both[0:64], both[64:128])
            for group in range(8):
                rows_ref[pl.ds(group * 8 * CAP + rank, 8, stride=CAP), :] = picked[
                    group * 8 : (group + 1) * 8
                ]
        return carry

    lax.fori_loop(0, CAP // 12, gather, 0)

    def chunk(at, carry):
        base = pl.multiple_of(at * 8, 8)
        values = [rows_ref[pl.ds(k * CAP + base, 8), :] for k in range(PARAMS)]
        view = (code_t_ref[pl.ds(base, 8), :] >> 14) & 3
        for k, value in enumerate(project(values, cameras_of(camera_ref, view))):
            proj_ref[pl.ds(k * CAP + base, 8), :] = value
        return carry

    lax.fori_loop(0, CAP // 8, chunk, 0)
    for part in range(WIDE // 128):
        reply_ref[:, part, :] = proj_ref[part * 128 : (part + 1) * 128, :].T


def reply_of(codes, cameras, table):
    smem = pl.BlockSpec(memory_space=pltpu.SMEM)
    vmem = pl.BlockSpec(memory_space=pltpu.VMEM)
    hbm = pl.BlockSpec(memory_space=pltpu.HBM)
    return pl.pallas_call(
        reply_kernel,
        name="reply",
        out_shape=(
            jax.ShapeDtypeStruct((DEVS, WIDE // 128, 128), F32),
            jax.ShapeDtypeStruct((64 * CAP, DEVS), F32),
        ),
        in_specs=[smem, vmem, hbm],
        out_specs=(vmem, vmem),
        scratch_shapes=[
            pltpu.VMEM((DEVS, DEVS), jnp.int32),
            pltpu.VMEM((CAP, DEVS), jnp.int32),
            pltpu.SMEM((CAP, DEVS), jnp.int32),
            pltpu.VMEM((HALF, 128), F32),
            pltpu.VMEM((12, DEVS, 128), F32),
            pltpu.VMEM((WIDE, DEVS), F32),
            pltpu.SemaphoreType.DMA,
            pltpu.SemaphoreType.DMA,
        ],
        compiler_params=pltpu.CompilerParams(vmem_limit_bytes=48 << 20),
    )(cameras, codes, in_hbm(table))


def render_kernel(
    view_hbm,
    spot_hbm,
    gain_hbm,
    d_image_hbm,
    entry_ref,
    arrived_ref,
    back_ref,
    view_ref,
    spot_ref,
    gain_ref,
    d_image_ref,
    sems,
    split_ref,
    tri_ref,
    low_ref,
    basis_t_ref,
    basis_ref,
    alpha_ref,
    q_ref,
    shade_ref,
    sum_ref,
    high_ref,
    low_part_ref,
    fold_ref,
):
    copies = [
        pltpu.make_async_copy(source, target, sems.at[at])
        for at, (source, target) in enumerate(
            (
                (view_hbm, view_ref),
                (spot_hbm, spot_ref),
                (gain_hbm, gain_ref),
                (d_image_hbm, d_image_ref),
            )
        )
    ]
    for copy in copies:
        copy.start()
    for part in range(WIDE // 128):
        sum_ref[part * 128 : (part + 1) * 128, 0:128] = arrived_ref[:, part, :].T
    for k in range(VALS):
        for deep in range(2):
            fold_ref[k * DEEP : (k + 1) * DEEP, deep * 128 : (deep + 1) * 128] = sum_ref[
                k * CAP + deep * DEEP : k * CAP + (deep + 1) * DEEP, 0:128
            ]
    for piece, value in enumerate(split_three(fold_ref[...])):
        split_ref[:, piece * 256 : (piece + 1) * 256] = value.astype(BF16)
    upper = upper_strict()
    lower = (iota((BLOCK, BLOCK), 0) > iota((BLOCK, BLOCK), 1)).astype(F32).astype(BF16)
    tri_ref[0:BLOCK, :] = upper
    tri_ref[BLOCK : 2 * BLOCK, :] = upper
    low_ref[0:BLOCK, :] = lower
    low_ref[BLOCK : 2 * BLOCK, :] = lower

    def monomial(which, x, y):
        return jnp.where(
            which == 0,
            1.0,
            jnp.where(
                which == 1,
                x,
                jnp.where(
                    which == 2,
                    y,
                    jnp.where(
                        which == 3,
                        x * x,
                        jnp.where(which == 4, x * y, jnp.where(which == 5, y * y, 0.0)),
                    ),
                ),
            ),
        )

    pixel = iota((TPIX, 128), 0)
    lane = iota((TPIX, 128), 1)
    basis_t_ref[...] = jnp.where(
        lane < 24,
        monomial(lane & 7, (pixel & 15).astype(F32) - 7.5, (pixel >> 4).astype(F32) - 7.5),
        0.0,
    ).astype(BF16)
    pixel = iota((16, TPIX), 1)
    basis = monomial(
        iota((16, TPIX), 0), (pixel & 15).astype(F32) - 7.5, (pixel >> 4).astype(F32) - 7.5
    ).astype(BF16)
    basis_ref[:, 0:TPIX] = basis
    basis_ref[:, TPIX : 2 * TPIX] = basis
    fold_ref[...] = jnp.zeros_like(fold_ref)

    def rows8(rows):
        at_row = iota((8, rows[0].shape[1]), 0)
        out = jnp.zeros((8, rows[0].shape[1]), F32)
        for at, row in enumerate(rows):
            out = jnp.where(at_row == at, row, out)
        return out

    def tile_step(tile, expo):
        view = view_ref[tile]
        spot = spot_ref[tile]
        line = spot // ACROSS
        mid_x = ((spot - line * ACROSS) * TILE + TILE // 2).astype(F32)
        mid_y = (line * TILE + TILE // 2).astype(F32)
        gains = [gain_ref[view, ch] for ch in range(3)]
        d_rows = [d_image_ref[ch, pl.ds(tile, 1), :] for ch in range(3)]
        d1, d2, d3 = split_three(rows8(d_rows))
        pixel_rows = jnp.concatenate([d1, d2, d3, jnp.zeros((8, TPIX), F32)], axis=0).astype(BF16)
        pixel_rows = jnp.concatenate([pixel_rows, pixel_rows], axis=1)
        g1, g2, g3 = split_three(rows8([gains[ch] * d_rows[ch] for ch in range(3)]))
        shade_ref[...] = (
            jnp.concatenate([g1, g1, g2, g2, g1, g3, jnp.zeros((80, TPIX), F32)], axis=0)
            .T.astype(BF16)
        )
        slots = pl.ds(pl.multiple_of(tile * SLOTS, SLOTS), SLOTS)
        owner = entry_ref[0:1, slots]
        rank = entry_ref[1:2, slots]
        deep = (rank >= DEEP).astype(jnp.int32)
        one_hot = (iota((2 * DEVS, SLOTS), 0) == owner + DEVS * deep).astype(F32).astype(BF16)
        found = mxu(split_ref[...], jnp.concatenate([one_hot, one_hot, one_hot], axis=0))
        here = iota((DEEP, SLOTS), 0) == rank - DEEP * deep
        vals = [
            jnp.sum(jnp.where(here, found[k * DEEP : (k + 1) * DEEP], 0.0), axis=0, keepdims=True)
            for k in range(VALS)
        ]
        shift_x = vals[0] - mid_x
        shift_y = vals[1] - mid_y
        con_a, con_b, con_c = vals[2], vals[3], vals[4]
        lin_x = con_a * shift_x + con_b * shift_y
        lin_y = con_c * shift_y + con_b * shift_x
        level_row = vals[5] - 0.5 * (lin_x * shift_x + lin_y * shift_y)
        poly = rows8(
            [
                jnp.where(owner >= 0, level_row, -200.0),
                lin_x,
                lin_y,
                -0.5 * con_a,
                -con_b,
                -0.5 * con_c,
            ]
        )
        poly = jnp.where(owner >= 0, poly, jnp.where(iota((8, SLOTS), 0) == 0, -200.0, 0.0))
        k1, k2, k3 = split_three(poly)
        poly_rows = jnp.concatenate([k1, k2, k3, jnp.zeros((104, SLOTS), F32)], axis=0).astype(
            BF16
        )
        color = rows8(vals[6:9])
        c1, c2, c3 = split_three(color)
        color_rows = jnp.concatenate(
            [c1, c2, c1, c2, c3, c1, jnp.zeros((80, SLOTS), F32)], axis=0
        ).astype(BF16)
        spans = [slice(block * BLOCK, (block + 1) * BLOCK) for block in range(NBLK)]
        for block, span in enumerate(spans):
            alpha = jnp.exp(mxu(basis_t_ref[...], poly_rows[:, span]))
            alpha_ref[block] = alpha
            fade = alpha * (1.0 + alpha * (0.5 + alpha * (1.0 / 3.0)))
            fade_hi, fade_lo = split_two(fade)
            high_ref[block] = fade_hi
            low_part_ref[block] = fade_lo
        summed = mxu(
            jnp.concatenate(
                [
                    high_ref[...].reshape(NBLK * TPIX, BLOCK),
                    low_part_ref[...].reshape(NBLK * TPIX, BLOCK),
                ],
                axis=1,
            ),
            tri_ref[...],
        )
        level = jnp.zeros((TPIX, 1), F32)
        seen_parts = []
        for block, span in enumerate(spans):
            alpha = alpha_ref[block]
            here_sum = summed[block * TPIX : (block + 1) * TPIX] + level
            weight = alpha * jnp.exp(-here_sum)
            edge = alpha[:, BLOCK - 1 : BLOCK]
            level = here_sum[:, BLOCK - 1 : BLOCK] + edge * (
                1.0 + edge * (0.5 + edge * (1.0 / 3.0))
            )
            q_val = mxu(shade_ref[...], color_rows[:, span]) * weight
            q_ref[block] = q_val
            q_hi, q_lo = split_two(q_val)
            high_ref[block] = q_hi
            low_part_ref[block] = q_lo
            weight_hi, weight_lo = split_two(weight)
            seen = mxu(pixel_rows, jnp.concatenate([weight_hi, weight_lo], axis=0))
            seen_parts.append(seen[0:8] + seen[8:16] + seen[16:24])
        seen = jnp.concatenate(seen_parts, axis=1)
        expo_cols = jnp.sum(color * seen, axis=1, keepdims=True)
        later = mxu(
            jnp.concatenate(
                [
                    high_ref[...].reshape(NBLK * TPIX, BLOCK),
                    low_part_ref[...].reshape(NBLK * TPIX, BLOCK),
                ],
                axis=1,
            ),
            low_ref[...],
        )
        tail = jnp.zeros((TPIX, 1), F32)
        grad_parts = [None] * NBLK
        for block in reversed(range(NBLK)):
            alpha = alpha_ref[block]
            q_val = q_ref[block]
            here_sum = later[block * TPIX : (block + 1) * TPIX] + tail
            d_exp = q_val - here_sum * (alpha * (1.0 + alpha * (1.0 + alpha)))
            tail = here_sum[:, 0:1] + q_val[:, 0:1]
            d_hi, d_lo = split_two(d_exp)
            grad_parts[block] = mxu(basis_ref[...], jnp.concatenate([d_hi, d_lo], axis=0))[0:8]
        grad = jnp.concatenate(grad_parts, axis=1)
        d_poly = [grad[k : k + 1] for k in range(6)]
        grads = [
            d_poly[1] * con_a + d_poly[2] * con_b - d_poly[0] * lin_x,
            d_poly[1] * con_b + d_poly[2] * con_c - d_poly[0] * lin_y,
            shift_x * d_poly[1] - 0.5 * (d_poly[3] + shift_x * shift_x * d_poly[0]),
            shift_y * d_poly[1] + shift_x * d_poly[2] - d_poly[4] - shift_x * shift_y * d_poly[0],
            shift_y * d_poly[2] - 0.5 * (d_poly[5] + shift_y * shift_y * d_poly[0]),
            d_poly[0],
            gains[0] * seen[0:1],
            gains[1] * seen[1:2],
            gains[2] * seen[2:3],
        ]
        high_rows = []
        low_rows = []
        for value in grads:
            high = value.astype(BF16).astype(F32)
            high_rows.append(jnp.where(here, high, 0.0))
            low_rows.append(jnp.where(here, value - high, 0.0))
        both = mxu_bt(jnp.concatenate(high_rows + low_rows, axis=0).astype(BF16), one_hot)
        fold_ref[...] += both[0:ROWS] + both[ROWS : 2 * ROWS]
        lane_at = iota((8, 128), 1) - (USED - 384) - 3 * view
        return expo + jnp.where(
            (lane_at == iota((8, 128), 0)) & (lane_at < 3), expo_cols, 0.0
        )

    for copy in copies:
        copy.wait()
    expo = lax.fori_loop(0, TILES, tile_step, jnp.zeros((8, 128), F32))
    sum_ref[USED:WIDE, :] = jnp.zeros((WIDE - USED, DEVS), F32)
    for k in range(VALS):
        for deep in range(2):
            sum_ref[k * CAP + deep * DEEP : k * CAP + (deep + 1) * DEEP, :] = fold_ref[
                k * DEEP : (k + 1) * DEEP, deep * 128 : (deep + 1) * 128
            ]
    for part in range(WIDE // 128):
        span = slice(part * 128, (part + 1) * 128)
        back = sum_ref[span, :].T
        if part == WIDE // 128 - 1:
            back = back + jnp.sum(expo, axis=0, keepdims=True)
        back_ref[:, part, :] = back


def render_of(tile_view, tile_spot, exposure, d_image, entries, arrived):
    hbm = pl.BlockSpec(memory_space=pltpu.HBM)
    vmem = pl.BlockSpec(memory_space=pltpu.VMEM)
    given = (tile_view, tile_spot, exposure, jnp.transpose(d_image, (1, 0, 2)))
    return pl.pallas_call(
        render_kernel,
        name="render",
        out_shape=jax.ShapeDtypeStruct((DEVS, WIDE // 128, 128), F32),
        in_specs=[hbm, hbm, hbm, hbm, vmem, vmem],
        out_specs=vmem,
        scratch_shapes=[
            pltpu.SMEM((TILES,), jnp.int32),
            pltpu.SMEM((TILES,), jnp.int32),
            pltpu.SMEM((4, 3), F32),
            pltpu.VMEM((3, TILES, TPIX), F32),
            pltpu.SemaphoreType.DMA((4,)),
            pltpu.VMEM((ROWS, 6 * DEVS), BF16),
            pltpu.VMEM((2 * BLOCK, BLOCK), BF16),
            pltpu.VMEM((2 * BLOCK, BLOCK), BF16),
            pltpu.VMEM((TPIX, 128), BF16),
            pltpu.VMEM((16, 2 * TPIX), BF16),
            pltpu.VMEM((NBLK, TPIX, BLOCK), F32),
            pltpu.VMEM((NBLK, TPIX, BLOCK), F32),
            pltpu.VMEM((TPIX, 128), BF16),
            pltpu.VMEM((WIDE, DEVS), F32),
            pltpu.VMEM((NBLK, TPIX, BLOCK), BF16),
            pltpu.VMEM((NBLK, TPIX, BLOCK), BF16),
            pltpu.VMEM((ROWS, 2 * DEVS), F32),
        ],
        compiler_params=pltpu.CompilerParams(vmem_limit_bytes=32 << 20),
    )(*[in_hbm(value) for value in given], entries, arrived)


PARTS = 8
SPAN = GDEV // PARTS


def update_kernel(
    camera_ref,
    code_ref,
    arrived_ref,
    rows_ref,
    params_hbm,
    m_hbm,
    v_hbm,
    params_out,
    m_out,
    v_out,
    expo_ref,
    code_t_ref,
    row_t_ref,
    row_smem,
    cot_ref,
    grad_ref,
    spread_ref,
    flip_ref,
    params_ref,
    m_ref,
    v_ref,
    in_sems,
    out_sems,
    row_sem,
    *tables,
):
    held = ((params_hbm, params_ref, params_out), (m_hbm, m_ref, m_out), (v_hbm, v_ref, v_out))

    fetches = [
        pltpu.make_async_copy(source, kept, in_sems.at[at])
        for at, (source, kept, unused) in enumerate(held)
    ]

    def give(part):
        span = pl.ds(pl.multiple_of(part * SPAN, SPAN), SPAN)
        return [
            pltpu.make_async_copy(kept.at[:, span], target.at[:, span], out_sems.at[at, part])
            for at, (unused, kept, target) in enumerate(held)
        ]

    code_t_ref[...] = code_ref[...].T
    row_t_ref[...] = code_t_ref[0:CAP, :] & (HALF - 1)
    send_rows = pltpu.make_async_copy(row_t_ref, row_smem, row_sem)
    send_rows.start()
    for copy in fetches:
        copy.start()
    shares = jnp.sum(arrived_ref[:, 3, :], axis=0, keepdims=True) * (1.0 / DEVS)
    for view in range(TILES):
        first = USED - 384 + 3 * view
        expo_ref[view : view + 1, :] = shares[:, first : first + 3]
    for part in range(WIDE // 128):
        cot_ref[part * 128 : (part + 1) * 128, :] = arrived_ref[:, part, :].T
    for table in tables:
        table[...] = jnp.zeros_like(table)
    grad_ref[PARAMS * CAP :, :] = jnp.zeros(((64 - PARAMS) * CAP, DEVS), F32)

    def chunk(at, carry):
        base = pl.multiple_of(at * 8, 8)
        values = [rows_ref[pl.ds(k * CAP + base, 8), :] for k in range(PARAMS)]
        code = code_t_ref[pl.ds(base, 8), :]
        camera = cameras_of(camera_ref, (code >> 14) & 3)
        unused, pull = jax.vjp(lambda given: project(given, camera), values)
        (grads,) = pull([cot_ref[pl.ds(k * CAP + base, 8), :] for k in range(VALS)])
        for k in range(PARAMS):
            grad_ref[pl.ds(k * CAP + base, 8), :] = jnp.where(code >= 0, grads[k], 0.0)
        return carry

    lax.fori_loop(0, CAP // 8, chunk, 0)
    send_rows.wait()

    def scatter(step, carry):
        for odd in range(12):
            rank = step * 12 + odd
            half = (code_t_ref[pl.ds(rank, 1), :] >> 13) & 1
            mine = jnp.concatenate(
                [grad_ref[pl.ds(group * 8 * CAP + rank, 8, stride=CAP), :] for group in range(8)],
                axis=0,
            )
            both = jnp.concatenate(
                [jnp.where(half == 0, mine, 0.0), jnp.where(half == 1, mine, 0.0)], axis=0
            )
            spread_ref[odd] = both.T
            for first in range(0, DEVS, 2 * TABLES):
                rows = [row_smem[rank, first + at] for at in range(2 * TABLES)]
                olds = [
                    tables[at % TABLES][pl.ds(rows[at], 1), :] for at in range(2 * TABLES)
                ]
                news = [
                    olds[at] + spread_ref[odd, first + at : first + at + 1, :]
                    for at in range(TABLES)
                ]
                for at in range(TABLES, 2 * TABLES):
                    old = jnp.where(rows[at] == rows[at - TABLES], news[at - TABLES], olds[at])
                    news.append(old + spread_ref[odd, first + at : first + at + 1, :])
                for at in range(2 * TABLES):
                    tables[at % TABLES][pl.ds(rows[at], 1), :] = news[at]
        return carry

    lax.fori_loop(0, CAP // 12, scatter, 0)

    for copy in fetches:
        copy.wait()

    def finish(part, carry):
        for at in range(SPAN // 256):
            rows = pl.ds(pl.multiple_of(part * (SPAN // 2) + at * 128, 128), 128)
            total = tables[0][rows, :]
            for table in tables[1:]:
                total = total + table[rows, :]
            flip_ref[at] = total.T
            for half in range(2):
                span = pl.ds(pl.multiple_of(part * SPAN + at * 256 + half * 128, 128), 128)
                gradient = flip_ref[at, half * 64 : half * 64 + PARAMS, :]
                new_m = beta_first * m_ref[:, span] + (1.0 - beta_first) * gradient
                new_v = beta_second * v_ref[:, span] + (1.0 - beta_second) * gradient * gradient
                m_ref[:, span] = new_m
                v_ref[:, span] = new_v
                params_ref[:, span] = params_ref[:, span] - learn_rate * (new_m / fix_first) / (
                    jnp.sqrt(new_v / fix_second) + adam_eps
                )
        for copy in give(part):
            copy.start()
        return carry

    lax.fori_loop(0, PARTS, finish, 0)
    for part in range(PARTS):
        for copy in give(part):
            copy.wait()


def update_of(codes, cameras, arrived, rows, params, adam_m, adam_v):
    smem = pl.BlockSpec(memory_space=pltpu.SMEM)
    vmem = pl.BlockSpec(memory_space=pltpu.VMEM)
    hbm = pl.BlockSpec(memory_space=pltpu.HBM)
    whole = jax.ShapeDtypeStruct((PARAMS, GDEV), F32)
    return pl.pallas_call(
        update_kernel,
        name="update",
        out_shape=(whole, whole, whole, jax.ShapeDtypeStruct((4, 3), F32)),
        in_specs=[smem, vmem, vmem, vmem, hbm, hbm, hbm],
        out_specs=(hbm, hbm, hbm, vmem),
        scratch_shapes=[
            pltpu.VMEM((DEVS, DEVS), jnp.int32),
            pltpu.VMEM((CAP, DEVS), jnp.int32),
            pltpu.SMEM((CAP, DEVS), jnp.int32),
            pltpu.VMEM((WIDE, DEVS), F32),
            pltpu.VMEM((64 * CAP, DEVS), F32),
            pltpu.VMEM((12, DEVS, 128), F32),
            pltpu.VMEM((SPAN // 256, 128, 128), F32),
        ]
        + [pltpu.VMEM((PARAMS, GDEV), F32)] * 3
        + [pltpu.SemaphoreType.DMA((3,)), pltpu.SemaphoreType.DMA((3, PARTS))]
        + [pltpu.SemaphoreType.DMA]
        + [pltpu.VMEM((HALF, 128), F32)] * TABLES,
        compiler_params=pltpu.CompilerParams(vmem_limit_bytes=48 << 20),
    )(cameras, codes, arrived, rows, in_hbm(params), in_hbm(adam_m), in_hbm(adam_v))


def exchange(value):
    return lax.all_to_all(value, AXES, split_axis=0, concat_axis=0, tiled=True)


def body(
    params,
    adam_m,
    adam_v,
    cameras,
    exposure,
    entry_owner,
    entry_local,
    block_counts,
    tile_view,
    tile_spot,
    d_image,
):
    requests, entries = route(tile_view, block_counts, entry_owner, entry_local)
    codes = exchange(requests)
    table = table_of(params)
    reply, rows = reply_of(codes, cameras, table)
    arrived = exchange(reply)
    back = render_of(tile_view, tile_spot, exposure, d_image, entries, arrived)
    returned = exchange(back)
    new_params, new_m, new_v, exposure_grad = update_of(
        codes, cameras, returned, rows, params, adam_m, adam_v
    )
    return (new_params, new_m, new_v, exposure_grad)


def solution(mesh):
    both = ("tiles", "gauss")
    placed = (
        P(None, both),
        P(None, both),
        P(None, both),
        P(),
        P(),
        P(both, None),
        P(both, None),
        P(both),
        P(both),
        P(both),
        P(both, None, None),
    )
    return jax.shard_map(
        body,
        mesh=mesh,
        in_specs=placed,
        out_specs=(P(None, both), P(None, both), P(None, both), P()),
        check_vma=False,
    )
```

```python
import jax
import jax.numpy as jnp
from jax import lax
from jax.experimental import pallas as pl
from jax.experimental.pallas import tpu as pltpu
from jax.sharding import PartitionSpec as P

AXES = ("tiles", "gauss")
DEVS = 128
CAP = 48
TILES = 4
SLOTS = 1024
BLOCK = 256
NBLK = 4
TPIX = 256
TILE = 16
ACROSS = 240
IMG_W = 3840
IMG_H = 2160
PARAMS = 59
GDEV = 16384
HALF = GDEV // 2
VALS = 9
USED = CAP * VALS
DEEP = CAP // 2
ROWS = DEEP * VALS
WIDE = 512
TABLES = 4
UNROLL = 16

sh_c0 = 0.28209479177387814
sh_c1 = 0.4886025119029199
sh_c2 = (
    1.0925484305920792,
    -1.0925484305920792,
    0.31539156525252005,
    -1.0925484305920792,
    0.5462742152960396,
)
sh_c3 = (
    -0.5900435899266435,
    2.890611442640554,
    -0.4570457994644658,
    0.3731763325901154,
    -0.4570457994644658,
    1.445305721320277,
    -0.5900435899266435,
)
beta_first = 0.9
beta_second = 0.999
learn_rate = 0.01
adam_eps = 1e-08
fix_first = 1.0
fix_second = 0.632304575229036
blur_add = 0.3

F32 = jnp.float32
BF16 = jnp.bfloat16


def sh_color(coefficients, unit_x, unit_y, unit_z):
    square_x = unit_x * unit_x
    square_y = unit_y * unit_y
    square_z = unit_z * unit_z
    basis_list = [
        -sh_c1 * unit_y,
        sh_c1 * unit_z,
        -sh_c1 * unit_x,
        sh_c2[0] * unit_x * unit_y,
        sh_c2[1] * unit_y * unit_z,
        sh_c2[2] * (2.0 * square_z - square_x - square_y),
        sh_c2[3] * unit_x * unit_z,
        sh_c2[4] * (square_x - square_y),
        sh_c3[0] * unit_y * (3.0 * square_x - square_y),
        sh_c3[1] * unit_x * unit_y * unit_z,
        sh_c3[2] * unit_y * (4.0 * square_z - square_x - square_y),
        sh_c3[3] * unit_z * (2.0 * square_z - 3.0 * square_x - 3.0 * square_y),
        sh_c3[4] * unit_x * (4.0 * square_z - square_x - square_y),
        sh_c3[5] * unit_z * (square_x - square_y),
        sh_c3[6] * unit_x * (square_x - 3.0 * square_y),
    ]
    colors = []
    for channel in range(3):
        summed = 0.5 + sh_c0 * coefficients[channel]
        for index_k in range(15):
            summed = summed + basis_list[index_k] * coefficients[3 * (index_k + 1) + channel]
        colors.append(jnp.maximum(summed, 0.0))
    return colors


def project(values, camera):
    points = [values[0], values[1], values[2]]
    matrix = [[camera[3 * row_at + col_at] for col_at in range(3)] for row_at in range(3)]
    translation = [camera[9], camera[10], camera[11]]
    focal_len = camera[12]
    viewed = [
        matrix[row_at][0] * points[0]
        + matrix[row_at][1] * points[1]
        + matrix[row_at][2] * points[2]
        + translation[row_at]
        for row_at in range(3)
    ]
    inverse_depth = 1.0 / viewed[2]
    screen_x = focal_len * viewed[0] * inverse_depth + 0.5 * IMG_W
    screen_y = focal_len * viewed[1] * inverse_depth + 0.5 * IMG_H
    slope_x = focal_len * viewed[0] * inverse_depth * inverse_depth
    slope_y = focal_len * viewed[1] * inverse_depth * inverse_depth
    jac_w = [
        [
            focal_len * inverse_depth * matrix[0][col_at] - slope_x * matrix[2][col_at]
            for col_at in range(3)
        ],
        [
            focal_len * inverse_depth * matrix[1][col_at] - slope_y * matrix[2][col_at]
            for col_at in range(3)
        ],
    ]
    quat_len = jnp.sqrt(
        values[6] * values[6]
        + values[7] * values[7]
        + values[8] * values[8]
        + values[9] * values[9]
    )
    quat_w = values[6] / quat_len
    quat_x = values[7] / quat_len
    quat_y = values[8] / quat_len
    quat_z = values[9] / quat_len
    rotation = [
        [
            1.0 - 2.0 * (quat_y * quat_y + quat_z * quat_z),
            2.0 * (quat_x * quat_y - quat_w * quat_z),
            2.0 * (quat_x * quat_z + quat_w * quat_y),
        ],
        [
            2.0 * (quat_x * quat_y + quat_w * quat_z),
            1.0 - 2.0 * (quat_x * quat_x + quat_z * quat_z),
            2.0 * (quat_y * quat_z - quat_w * quat_x),
        ],
        [
            2.0 * (quat_x * quat_z - quat_w * quat_y),
            2.0 * (quat_y * quat_z + quat_w * quat_x),
            1.0 - 2.0 * (quat_x * quat_x + quat_y * quat_y),
        ],
    ]
    extent = [jnp.exp(values[3]), jnp.exp(values[4]), jnp.exp(values[5])]
    spread = [
        [
            (
                jac_w[row_at][0] * rotation[0][col_at]
                + jac_w[row_at][1] * rotation[1][col_at]
                + jac_w[row_at][2] * rotation[2][col_at]
            )
            * extent[col_at]
            for col_at in range(3)
        ]
        for row_at in range(2)
    ]
    cov_a = (
        spread[0][0] * spread[0][0]
        + spread[0][1] * spread[0][1]
        + spread[0][2] * spread[0][2]
        + blur_add
    )
    cov_b = spread[0][0] * spread[1][0] + spread[0][1] * spread[1][1] + spread[0][2] * spread[1][2]
    cov_c = (
        spread[1][0] * spread[1][0]
        + spread[1][1] * spread[1][1]
        + spread[1][2] * spread[1][2]
        + blur_add
    )
    determinant = cov_a * cov_c - cov_b * cov_b
    logit = values[10]
    log_opacity = jnp.minimum(logit, 0.0) - jnp.log(1.0 + jnp.exp(-jnp.abs(logit)))
    center = [
        -(
            matrix[0][col_at] * translation[0]
            + matrix[1][col_at] * translation[1]
            + matrix[2][col_at] * translation[2]
        )
        for col_at in range(3)
    ]
    offset = [points[col_at] - center[col_at] for col_at in range(3)]
    distance = jnp.sqrt(offset[0] * offset[0] + offset[1] * offset[1] + offset[2] * offset[2])
    colors = sh_color(
        values[11:PARAMS], offset[0] / distance, offset[1] / distance, offset[2] / distance
    )
    return [
        screen_x,
        screen_y,
        cov_c / determinant,
        -cov_b / determinant,
        cov_a / determinant,
        log_opacity,
    ] + colors


def in_hbm(value):
    return pltpu.with_memory_space_constraint(value, pltpu.HBM)


def iota(shape, dim):
    return lax.broadcasted_iota(jnp.int32, shape, dim)


def mxu(left, right):
    return jnp.dot(left, right, preferred_element_type=F32)


def mxu_bt(left, right):
    return lax.dot_general(left, right, (((1,), (1,)), ((), ())), preferred_element_type=F32)


def split_two(value):
    high = value.astype(BF16)
    low = (value - high.astype(F32)).astype(BF16)
    return high, low


def split_three(value):
    high = value.astype(BF16).astype(F32)
    rest = value - high
    middle = rest.astype(BF16).astype(F32)
    low = (rest - middle).astype(BF16).astype(F32)
    return high, middle, low


def upper_strict():
    return (iota((BLOCK, BLOCK), 0) < iota((BLOCK, BLOCK), 1)).astype(F32).astype(BF16)


def route_kernel(
    view_hbm,
    count_hbm,
    owner_hbm,
    local_hbm,
    req_ref,
    entry_ref,
    view_ref,
    count_ref,
    owner_ref,
    local_ref,
    flip_ref,
    sems,
):
    copies = [
        pltpu.make_async_copy(source, target, sems.at[at])
        for at, (source, target) in enumerate(
            (
                (view_hbm, view_ref),
                (count_hbm, count_ref),
                (owner_hbm, owner_ref),
                (local_hbm, local_ref),
            )
        )
    ]
    for copy in copies:
        copy.start()
    tri = upper_strict()
    for copy in copies:
        copy.wait()
    before = jnp.zeros((DEVS, 1), F32)
    total = jnp.zeros((2 * CAP, DEVS), F32)
    for tile in range(TILES):
        view = view_ref[tile]
        slots = slice(tile * SLOTS, (tile + 1) * SLOTS)
        alive = (iota((1, SLOTS), 1) >> 8) < count_ref[tile]
        owner = jnp.where(alive, owner_ref[tile : tile + 1, :], -1)
        local = local_ref[tile : tile + 1, :]
        one_hot = (iota((DEVS, SLOTS), 0) == owner).astype(F32)
        one_hot_b = one_hot.astype(BF16)
        ranks = []
        for block in range(NBLK):
            span = slice(block * BLOCK, (block + 1) * BLOCK)
            earlier = mxu(one_hot_b[:, span], tri) + before
            ranks.append(jnp.sum(one_hot[:, span] * earlier, axis=0, keepdims=True))
            last = (block + 1) * BLOCK
            before = earlier[:, BLOCK - 1 : BLOCK] + one_hot[:, last - 1 : last]
        rank = jnp.where(owner >= 0, jnp.concatenate(ranks, axis=1).astype(jnp.int32), -1)
        code = (
            view * GDEV + ((local >> 7) & 1) * HALF + ((local >> 8) << 7) + (local & 127) + 1
        )
        here = iota((CAP, SLOTS), 0) == rank
        high = jnp.where(here, (code >> 8).astype(F32), 0.0).astype(BF16)
        low = jnp.where(here, (code & 255).astype(F32), 0.0).astype(BF16)
        total = total + mxu_bt(jnp.concatenate([high, low], axis=0), one_hot_b)
        entry_ref[0:1, slots] = owner
        entry_ref[1:2, slots] = rank
    flip_ref[...] = jnp.zeros_like(flip_ref)
    flip_ref[0:CAP, :] = total[0:CAP] * 256.0 + total[CAP : 2 * CAP]
    req_ref[...] = flip_ref[...].T.astype(jnp.int32) - 1


def route(tile_view, block_counts, entry_owner, entry_local):
    hbm = pl.BlockSpec(memory_space=pltpu.HBM)
    vmem = pl.BlockSpec(memory_space=pltpu.VMEM)
    return pl.pallas_call(
        route_kernel,
        name="route",
        out_shape=(
            jax.ShapeDtypeStruct((DEVS, DEVS), jnp.int32),
            jax.ShapeDtypeStruct((8, TILES * SLOTS), jnp.int32),
        ),
        in_specs=[hbm, hbm, hbm, hbm],
        out_specs=(vmem, vmem),
        scratch_shapes=[
            pltpu.SMEM((TILES,), jnp.int32),
            pltpu.SMEM((TILES,), jnp.int32),
            pltpu.VMEM((TILES, SLOTS), jnp.int32),
            pltpu.VMEM((TILES, SLOTS), jnp.int32),
            pltpu.VMEM((DEVS, DEVS), F32),
            pltpu.SemaphoreType.DMA((4,)),
        ],
        compiler_params=pltpu.CompilerParams(vmem_limit_bytes=16 << 20),
    )(*[in_hbm(given) for given in (tile_view, block_counts, entry_owner, entry_local)])


PIECES = 8
PIECE = HALF // PIECES


def table_kernel(params_hbm, table_hbm, params_ref, table_ref, in_sems, out_sems):
    takes = []
    gives = []
    for piece in range(PIECES):
        cols = pl.ds(piece * 2 * PIECE, 2 * PIECE)
        takes.append(
            pltpu.make_async_copy(params_hbm.at[:, cols], params_ref.at[:, cols], in_sems.at[piece])
        )
        rows = pl.ds(piece * PIECE, PIECE)
        gives.append(
            pltpu.make_async_copy(table_ref.at[rows], table_hbm.at[rows], out_sems.at[piece])
        )
    for copy in takes:
        copy.start()
    gap = jnp.zeros((64 - PARAMS, 128), F32)
    for piece in range(PIECES):
        takes[piece].wait()
        for at in range(piece * (PIECE // 128), (piece + 1) * (PIECE // 128)):
            both = jnp.concatenate(
                [
                    params_ref[:, at * 256 : at * 256 + 128],
                    gap,
                    params_ref[:, at * 256 + 128 : at * 256 + 256],
                    gap,
                ],
                axis=0,
            )
            table_ref[at * 128 : (at + 1) * 128, :] = both.T
        gives[piece].start()
    for copy in gives:
        copy.wait()


def table_of(params):
    hbm = pl.BlockSpec(memory_space=pltpu.HBM)
    return pl.pallas_call(
        table_kernel,
        name="table",
        out_shape=pltpu.HBM((HALF, 128), F32),
        in_specs=[hbm],
        out_specs=hbm,
        scratch_shapes=[
            pltpu.VMEM((PARAMS, GDEV), F32),
            pltpu.VMEM((HALF, 128), F32),
            pltpu.SemaphoreType.DMA((PIECES,)),
            pltpu.SemaphoreType.DMA((PIECES,)),
        ],
        compiler_params=pltpu.CompilerParams(vmem_limit_bytes=24 << 20),
        cost_estimate=pl.CostEstimate(flops=1 << 20, bytes_accessed=9 << 20, transcendentals=0),
    )(in_hbm(params))


def cameras_of(camera_ref, view):
    return [
        jnp.where(
            view == 0,
            camera_ref[0, at],
            jnp.where(
                view == 1,
                camera_ref[1, at],
                jnp.where(view == 2, camera_ref[2, at], camera_ref[3, at]),
            ),
        )
        for at in range(13)
    ]


def reply_kernel(
    camera_ref,
    code_ref,
    table_hbm,
    reply_ref,
    rows_ref,
    code_t_ref,
    row_t_ref,
    row_smem,
    table_ref,
    got_ref,
    proj_ref,
    table_sem,
    row_sem,
):
    take_table = pltpu.make_async_copy(table_hbm, table_ref, table_sem)
    take_table.start()
    code_t_ref[...] = code_ref[...].T
    row_t_ref[...] = code_t_ref[0:CAP, :] & (HALF - 1)
    send_rows = pltpu.make_async_copy(row_t_ref, row_smem, row_sem)
    send_rows.start()
    proj_ref[USED:WIDE, :] = jnp.zeros((WIDE - USED, DEVS), F32)
    send_rows.wait()
    take_table.wait()

    def gather(step, carry):
        for odd in range(16):
            rank = step * 16 + odd
            for src in range(DEVS):
                got_ref[odd, src : src + 1, :] = table_ref[pl.ds(row_smem[rank, src], 1), :]
            both = got_ref[odd].T
            half = (code_t_ref[pl.ds(rank, 1), :] >> 13) & 1
            picked = jnp.where(half == 0, both[0:64], both[64:128])
            for group in range(8):
                rows_ref[pl.ds(group * 8 * CAP + rank, 8, stride=CAP), :] = picked[
                    group * 8 : (group + 1) * 8
                ]
        return carry

    lax.fori_loop(0, CAP // 16, gather, 0)

    def chunk(at, carry):
        base = pl.multiple_of(at * 8, 8)
        values = [rows_ref[pl.ds(k * CAP + base, 8), :] for k in range(PARAMS)]
        view = (code_t_ref[pl.ds(base, 8), :] >> 14) & 3
        for k, value in enumerate(project(values, cameras_of(camera_ref, view))):
            proj_ref[pl.ds(k * CAP + base, 8), :] = value
        return carry

    lax.fori_loop(0, CAP // 8, chunk, 0, unroll=2)
    for part in range(WIDE // 128):
        reply_ref[:, part, :] = proj_ref[part * 128 : (part + 1) * 128, :].T


def reply_of(codes, cameras, table):
    smem = pl.BlockSpec(memory_space=pltpu.SMEM)
    vmem = pl.BlockSpec(memory_space=pltpu.VMEM)
    hbm = pl.BlockSpec(memory_space=pltpu.HBM)
    return pl.pallas_call(
        reply_kernel,
        name="reply",
        out_shape=(
            jax.ShapeDtypeStruct((DEVS, WIDE // 128, 128), F32),
            jax.ShapeDtypeStruct((64 * CAP, DEVS), F32),
        ),
        in_specs=[smem, vmem, hbm],
        out_specs=(vmem, vmem),
        scratch_shapes=[
            pltpu.VMEM((DEVS, DEVS), jnp.int32),
            pltpu.VMEM((CAP, DEVS), jnp.int32),
            pltpu.SMEM((CAP, DEVS), jnp.int32),
            pltpu.VMEM((HALF, 128), F32),
            pltpu.VMEM((16, DEVS, 128), F32),
            pltpu.VMEM((WIDE, DEVS), F32),
            pltpu.SemaphoreType.DMA,
            pltpu.SemaphoreType.DMA,
        ],
        compiler_params=pltpu.CompilerParams(vmem_limit_bytes=48 << 20),
    )(cameras, codes, in_hbm(table))


def render_kernel(
    view_hbm,
    spot_hbm,
    gain_hbm,
    d_image_hbm,
    entry_ref,
    arrived_ref,
    back_ref,
    view_ref,
    spot_ref,
    gain_ref,
    d_image_ref,
    sems,
    split_ref,
    tri_ref,
    low_ref,
    basis_t_ref,
    basis_ref,
    alpha_ref,
    q_ref,
    shade_ref,
    sum_ref,
    high_ref,
    low_part_ref,
    fold_ref,
):
    copies = [
        pltpu.make_async_copy(source, target, sems.at[at])
        for at, (source, target) in enumerate(
            (
                (view_hbm, view_ref),
                (spot_hbm, spot_ref),
                (gain_hbm, gain_ref),
                (d_image_hbm, d_image_ref),
            )
        )
    ]
    for copy in copies:
        copy.start()
    for part in range(WIDE // 128):
        sum_ref[part * 128 : (part + 1) * 128, 0:128] = arrived_ref[:, part, :].T
    for k in range(VALS):
        for deep in range(2):
            fold_ref[k * DEEP : (k + 1) * DEEP, deep * 128 : (deep + 1) * 128] = sum_ref[
                k * CAP + deep * DEEP : k * CAP + (deep + 1) * DEEP, 0:128
            ]
    for piece, value in enumerate(split_three(fold_ref[...])):
        split_ref[:, piece * 256 : (piece + 1) * 256] = value.astype(BF16)
    upper = upper_strict()
    lower = (iota((BLOCK, BLOCK), 0) > iota((BLOCK, BLOCK), 1)).astype(F32).astype(BF16)
    tri_ref[0:BLOCK, :] = upper
    tri_ref[BLOCK : 2 * BLOCK, :] = upper
    low_ref[0:BLOCK, :] = lower
    low_ref[BLOCK : 2 * BLOCK, :] = lower

    def monomial(which, x, y):
        return jnp.where(
            which == 0,
            1.0,
            jnp.where(
                which == 1,
                x,
                jnp.where(
                    which == 2,
                    y,
                    jnp.where(
                        which == 3,
                        x * x,
                        jnp.where(which == 4, x * y, jnp.where(which == 5, y * y, 0.0)),
                    ),
                ),
            ),
        )

    pixel = iota((TPIX, 128), 0)
    lane = iota((TPIX, 128), 1)
    basis_t_ref[...] = jnp.where(
        lane < 24,
        monomial(lane & 7, (pixel & 15).astype(F32) - 7.5, (pixel >> 4).astype(F32) - 7.5),
        0.0,
    ).astype(BF16)
    pixel = iota((16, TPIX), 1)
    basis = monomial(
        iota((16, TPIX), 0), (pixel & 15).astype(F32) - 7.5, (pixel >> 4).astype(F32) - 7.5
    ).astype(BF16)
    basis_ref[:, 0:TPIX] = basis
    basis_ref[:, TPIX : 2 * TPIX] = basis
    fold_ref[...] = jnp.zeros_like(fold_ref)

    def rows8(rows):
        at_row = iota((8, rows[0].shape[1]), 0)
        out = jnp.zeros((8, rows[0].shape[1]), F32)
        for at, row in enumerate(rows):
            out = jnp.where(at_row == at, row, out)
        return out

    def tile_step(tile, expo):
        view = view_ref[tile]
        spot = spot_ref[tile]
        line = spot // ACROSS
        mid_x = ((spot - line * ACROSS) * TILE + TILE // 2).astype(F32)
        mid_y = (line * TILE + TILE // 2).astype(F32)
        gains = [gain_ref[view, ch] for ch in range(3)]
        d_rows = [d_image_ref[ch, pl.ds(tile, 1), :] for ch in range(3)]
        d1, d2, d3 = split_three(rows8(d_rows))
        pixel_rows = jnp.concatenate([d1, d2, d3, jnp.zeros((8, TPIX), F32)], axis=0).astype(BF16)
        pixel_rows = jnp.concatenate([pixel_rows, pixel_rows], axis=1)
        g1, g2, g3 = split_three(rows8([gains[ch] * d_rows[ch] for ch in range(3)]))
        shade_ref[tile % 2] = (
            jnp.concatenate([g1, g1, g2, g2, g1, g3, jnp.zeros((80, TPIX), F32)], axis=0)
            .T.astype(BF16)
        )
        slots = slice(tile * SLOTS, (tile + 1) * SLOTS)
        owner = entry_ref[0:1, slots]
        rank = entry_ref[1:2, slots]
        deep = (rank >= DEEP).astype(jnp.int32)
        one_hot = (iota((2 * DEVS, SLOTS), 0) == owner + DEVS * deep).astype(F32).astype(BF16)
        found = mxu(split_ref[...], jnp.concatenate([one_hot, one_hot, one_hot], axis=0))
        here = iota((DEEP, SLOTS), 0) == rank - DEEP * deep
        vals = [
            jnp.sum(jnp.where(here, found[k * DEEP : (k + 1) * DEEP], 0.0), axis=0, keepdims=True)
            for k in range(VALS)
        ]
        shift_x = vals[0] - mid_x
        shift_y = vals[1] - mid_y
        con_a, con_b, con_c = vals[2], vals[3], vals[4]
        lin_x = con_a * shift_x + con_b * shift_y
        lin_y = con_c * shift_y + con_b * shift_x
        level_row = vals[5] - 0.5 * (lin_x * shift_x + lin_y * shift_y)
        poly = rows8(
            [
                jnp.where(owner >= 0, level_row, -200.0),
                lin_x,
                lin_y,
                -0.5 * con_a,
                -con_b,
                -0.5 * con_c,
            ]
        )
        poly = jnp.where(owner >= 0, poly, jnp.where(iota((8, SLOTS), 0) == 0, -200.0, 0.0))
        k1, k2, k3 = split_three(poly)
        poly_rows = jnp.concatenate([k1, k2, k3, jnp.zeros((104, SLOTS), F32)], axis=0).astype(
            BF16
        )
        color = rows8(vals[6:9])
        c1, c2, c3 = split_three(color)
        color_rows = jnp.concatenate(
            [c1, c2, c1, c2, c3, c1, jnp.zeros((80, SLOTS), F32)], axis=0
        ).astype(BF16)
        spans = [slice(block * BLOCK, (block + 1) * BLOCK) for block in range(NBLK)]
        for block, span in enumerate(spans):
            alpha = jnp.exp(mxu(basis_t_ref[:, 0:32], poly_rows[0:32, span]))
            alpha_ref[tile % 2, block] = alpha
            fade = alpha * (1.0 + alpha * (0.5 + alpha * (1.0 / 3.0)))
            fade_hi, fade_lo = split_two(fade)
            high_ref[tile % 2, block] = fade_hi
            low_part_ref[tile % 2, block] = fade_lo
        summed = mxu(
            jnp.concatenate(
                [
                    high_ref[tile % 2].reshape(NBLK * TPIX, BLOCK),
                    low_part_ref[tile % 2].reshape(NBLK * TPIX, BLOCK),
                ],
                axis=1,
            ),
            tri_ref[...],
        )
        level = jnp.zeros((TPIX, 1), F32)
        seen_parts = []
        for block, span in enumerate(spans):
            alpha = alpha_ref[tile % 2, block]
            here_sum = summed[block * TPIX : (block + 1) * TPIX] + level
            weight = alpha * jnp.exp(-here_sum)
            edge = alpha[:, BLOCK - 1 : BLOCK]
            level = here_sum[:, BLOCK - 1 : BLOCK] + edge * (
                1.0 + edge * (0.5 + edge * (1.0 / 3.0))
            )
            q_val = mxu(shade_ref[tile % 2, :, 0:48], color_rows[0:48, span]) * weight
            q_ref[tile % 2, block] = q_val
            q_hi, q_lo = split_two(q_val)
            high_ref[tile % 2, block] = q_hi
            low_part_ref[tile % 2, block] = q_lo
            weight_hi, weight_lo = split_two(weight)
            seen = mxu(pixel_rows, jnp.concatenate([weight_hi, weight_lo], axis=0))
            seen_parts.append(seen[0:8] + seen[8:16] + seen[16:24])
        seen = jnp.concatenate(seen_parts, axis=1)
        expo_cols = jnp.sum(color * seen, axis=1, keepdims=True)
        later = mxu(
            jnp.concatenate(
                [
                    high_ref[tile % 2].reshape(NBLK * TPIX, BLOCK),
                    low_part_ref[tile % 2].reshape(NBLK * TPIX, BLOCK),
                ],
                axis=1,
            ),
            low_ref[...],
        )
        tail = jnp.zeros((TPIX, 1), F32)
        grad_parts = [None] * NBLK
        for block in reversed(range(NBLK)):
            alpha = alpha_ref[tile % 2, block]
            q_val = q_ref[tile % 2, block]
            here_sum = later[block * TPIX : (block + 1) * TPIX] + tail
            d_exp = q_val - here_sum * (alpha * (1.0 + alpha * (1.0 + alpha)))
            tail = here_sum[:, 0:1] + q_val[:, 0:1]
            d_hi, d_lo = split_two(d_exp)
            grad_parts[block] = mxu(basis_ref[...], jnp.concatenate([d_hi, d_lo], axis=0))[0:8]
        grad = jnp.concatenate(grad_parts, axis=1)
        d_poly = [grad[k : k + 1] for k in range(6)]
        grads = [
            d_poly[1] * con_a + d_poly[2] * con_b - d_poly[0] * lin_x,
            d_poly[1] * con_b + d_poly[2] * con_c - d_poly[0] * lin_y,
            shift_x * d_poly[1] - 0.5 * (d_poly[3] + shift_x * shift_x * d_poly[0]),
            shift_y * d_poly[1] + shift_x * d_poly[2] - d_poly[4] - shift_x * shift_y * d_poly[0],
            shift_y * d_poly[2] - 0.5 * (d_poly[5] + shift_y * shift_y * d_poly[0]),
            d_poly[0],
            gains[0] * seen[0:1],
            gains[1] * seen[1:2],
            gains[2] * seen[2:3],
        ]
        high_rows = []
        low_rows = []
        for value in grads:
            high = value.astype(BF16).astype(F32)
            high_rows.append(jnp.where(here, high, 0.0))
            low_rows.append(jnp.where(here, value - high, 0.0))
        both = mxu_bt(jnp.concatenate(high_rows + low_rows, axis=0).astype(BF16), one_hot)
        fold_ref[...] += both[0:ROWS] + both[ROWS : 2 * ROWS]
        lane_at = iota((8, 128), 1) - (USED - 384) - 3 * view
        return expo + jnp.where(
            (lane_at == iota((8, 128), 0)) & (lane_at < 3), expo_cols, 0.0
        )

    for copy in copies:
        copy.wait()
    expo = jnp.zeros((8, 128), F32)
    for tile in range(TILES):
        expo = tile_step(tile, expo)
    sum_ref[USED:WIDE, :] = jnp.zeros((WIDE - USED, DEVS), F32)
    for k in range(VALS):
        for deep in range(2):
            sum_ref[k * CAP + deep * DEEP : k * CAP + (deep + 1) * DEEP, :] = fold_ref[
                k * DEEP : (k + 1) * DEEP, deep * 128 : (deep + 1) * 128
            ]
    for part in range(WIDE // 128):
        span = slice(part * 128, (part + 1) * 128)
        back = sum_ref[span, :].T
        if part == WIDE // 128 - 1:
            back = back + jnp.sum(expo, axis=0, keepdims=True)
        back_ref[:, part, :] = back


def render_of(tile_view, tile_spot, exposure, d_image, entries, arrived):
    hbm = pl.BlockSpec(memory_space=pltpu.HBM)
    vmem = pl.BlockSpec(memory_space=pltpu.VMEM)
    given = (tile_view, tile_spot, exposure, jnp.transpose(d_image, (1, 0, 2)))
    return pl.pallas_call(
        render_kernel,
        name="render",
        out_shape=jax.ShapeDtypeStruct((DEVS, WIDE // 128, 128), F32),
        in_specs=[hbm, hbm, hbm, hbm, vmem, vmem],
        out_specs=vmem,
        scratch_shapes=[
            pltpu.SMEM((TILES,), jnp.int32),
            pltpu.SMEM((TILES,), jnp.int32),
            pltpu.SMEM((4, 3), F32),
            pltpu.VMEM((3, TILES, TPIX), F32),
            pltpu.SemaphoreType.DMA((4,)),
            pltpu.VMEM((ROWS, 6 * DEVS), BF16),
            pltpu.VMEM((2 * BLOCK, BLOCK), BF16),
            pltpu.VMEM((2 * BLOCK, BLOCK), BF16),
            pltpu.VMEM((TPIX, 128), BF16),
            pltpu.VMEM((16, 2 * TPIX), BF16),
            pltpu.VMEM((2, NBLK, TPIX, BLOCK), F32),
            pltpu.VMEM((2, NBLK, TPIX, BLOCK), F32),
            pltpu.VMEM((2, TPIX, 128), BF16),
            pltpu.VMEM((WIDE, DEVS), F32),
            pltpu.VMEM((2, NBLK, TPIX, BLOCK), BF16),
            pltpu.VMEM((2, NBLK, TPIX, BLOCK), BF16),
            pltpu.VMEM((ROWS, 2 * DEVS), F32),
        ],
        compiler_params=pltpu.CompilerParams(vmem_limit_bytes=32 << 20),
    )(*[in_hbm(value) for value in given], entries, arrived)


PARTS = 8
SPAN = GDEV // PARTS


def update_kernel(
    camera_ref,
    code_ref,
    arrived_ref,
    rows_ref,
    params_hbm,
    m_hbm,
    v_hbm,
    params_out,
    m_out,
    v_out,
    expo_ref,
    code_t_ref,
    row_t_ref,
    row_smem,
    cot_ref,
    grad_ref,
    spread_ref,
    flip_ref,
    params_ref,
    m_ref,
    v_ref,
    in_sems,
    out_sems,
    row_sem,
    *tables,
):
    held = ((params_hbm, params_ref, params_out), (m_hbm, m_ref, m_out), (v_hbm, v_ref, v_out))

    fetches = [
        pltpu.make_async_copy(source, kept, in_sems.at[at])
        for at, (source, kept, unused) in enumerate(held)
    ]

    def give(part):
        span = pl.ds(pl.multiple_of(part * SPAN, SPAN), SPAN)
        return [
            pltpu.make_async_copy(kept.at[:, span], target.at[:, span], out_sems.at[at, part])
            for at, (unused, kept, target) in enumerate(held)
        ]

    code_t_ref[...] = code_ref[...].T
    row_t_ref[...] = code_t_ref[0:CAP, :] & (HALF - 1)
    send_rows = pltpu.make_async_copy(row_t_ref, row_smem, row_sem)
    send_rows.start()
    for copy in fetches:
        copy.start()
    shares = jnp.sum(arrived_ref[:, 3, :], axis=0, keepdims=True) * (1.0 / DEVS)
    for view in range(TILES):
        first = USED - 384 + 3 * view
        expo_ref[view : view + 1, :] = shares[:, first : first + 3]
    for part in range(WIDE // 128):
        cot_ref[part * 128 : (part + 1) * 128, :] = arrived_ref[:, part, :].T
    for table in tables:
        table[...] = jnp.zeros_like(table)
    grad_ref[PARAMS * CAP :, :] = jnp.zeros(((64 - PARAMS) * CAP, DEVS), F32)

    def chunk(at, carry):
        base = pl.multiple_of(at * 8, 8)
        values = [rows_ref[pl.ds(k * CAP + base, 8), :] for k in range(PARAMS)]
        code = code_t_ref[pl.ds(base, 8), :]
        camera = cameras_of(camera_ref, (code >> 14) & 3)
        unused, pull = jax.vjp(lambda given: project(given, camera), values)
        (grads,) = pull([cot_ref[pl.ds(k * CAP + base, 8), :] for k in range(VALS)])
        for k in range(PARAMS):
            grad_ref[pl.ds(k * CAP + base, 8), :] = jnp.where(code >= 0, grads[k], 0.0)
        return carry

    lax.fori_loop(0, CAP // 8, chunk, 0, unroll=2)
    send_rows.wait()

    def scatter(step, carry):
        for odd in range(16):
            rank = step * 16 + odd
            half = (code_t_ref[pl.ds(rank, 1), :] >> 13) & 1
            mine = jnp.concatenate(
                [grad_ref[pl.ds(group * 8 * CAP + rank, 8, stride=CAP), :] for group in range(8)],
                axis=0,
            )
            both = jnp.concatenate(
                [jnp.where(half == 0, mine, 0.0), jnp.where(half == 1, mine, 0.0)], axis=0
            )
            spread_ref[odd] = both.T
            for first in range(0, DEVS, 2 * TABLES):
                rows = [row_smem[rank, first + at] for at in range(2 * TABLES)]
                olds = [
                    tables[at % TABLES][pl.ds(rows[at], 1), :] for at in range(2 * TABLES)
                ]
                news = [
                    olds[at] + spread_ref[odd, first + at : first + at + 1, :]
                    for at in range(TABLES)
                ]
                for at in range(TABLES, 2 * TABLES):
                    old = jnp.where(rows[at] == rows[at - TABLES], news[at - TABLES], olds[at])
                    news.append(old + spread_ref[odd, first + at : first + at + 1, :])
                for at in range(2 * TABLES):
                    tables[at % TABLES][pl.ds(rows[at], 1), :] = news[at]
        return carry

    lax.fori_loop(0, CAP // 16, scatter, 0)

    for copy in fetches:
        copy.wait()

    def finish(part, carry):
        for at in range(SPAN // 256):
            rows = pl.ds(pl.multiple_of(part * (SPAN // 2) + at * 128, 128), 128)
            total = tables[0][rows, :]
            for table in tables[1:]:
                total = total + table[rows, :]
            flip_ref[at] = total.T
            for half in range(2):
                span = pl.ds(pl.multiple_of(part * SPAN + at * 256 + half * 128, 128), 128)
                gradient = flip_ref[at, half * 64 : half * 64 + PARAMS, :]
                new_m = beta_first * m_ref[:, span] + (1.0 - beta_first) * gradient
                new_v = beta_second * v_ref[:, span] + (1.0 - beta_second) * gradient * gradient
                m_ref[:, span] = new_m
                v_ref[:, span] = new_v
                params_ref[:, span] = params_ref[:, span] - learn_rate * (new_m / fix_first) / (
                    jnp.sqrt(new_v / fix_second) + adam_eps
                )
        for copy in give(part):
            copy.start()
        return carry

    lax.fori_loop(0, PARTS, finish, 0)
    for part in range(PARTS):
        for copy in give(part):
            copy.wait()


def update_of(codes, cameras, arrived, rows, params, adam_m, adam_v):
    smem = pl.BlockSpec(memory_space=pltpu.SMEM)
    vmem = pl.BlockSpec(memory_space=pltpu.VMEM)
    hbm = pl.BlockSpec(memory_space=pltpu.HBM)
    whole = jax.ShapeDtypeStruct((PARAMS, GDEV), F32)
    return pl.pallas_call(
        update_kernel,
        name="update",
        out_shape=(whole, whole, whole, jax.ShapeDtypeStruct((4, 3), F32)),
        in_specs=[smem, vmem, vmem, vmem, hbm, hbm, hbm],
        out_specs=(hbm, hbm, hbm, vmem),
        scratch_shapes=[
            pltpu.VMEM((DEVS, DEVS), jnp.int32),
            pltpu.VMEM((CAP, DEVS), jnp.int32),
            pltpu.SMEM((CAP, DEVS), jnp.int32),
            pltpu.VMEM((WIDE, DEVS), F32),
            pltpu.VMEM((64 * CAP, DEVS), F32),
            pltpu.VMEM((16, DEVS, 128), F32),
            pltpu.VMEM((SPAN // 256, 128, 128), F32),
        ]
        + [pltpu.VMEM((PARAMS, GDEV), F32)] * 3
        + [pltpu.SemaphoreType.DMA((3,)), pltpu.SemaphoreType.DMA((3, PARTS))]
        + [pltpu.SemaphoreType.DMA]
        + [pltpu.VMEM((HALF, 128), F32)] * TABLES,
        compiler_params=pltpu.CompilerParams(vmem_limit_bytes=48 << 20),
    )(cameras, codes, arrived, rows, in_hbm(params), in_hbm(adam_m), in_hbm(adam_v))


def exchange(value):
    return lax.all_to_all(value, AXES, split_axis=0, concat_axis=0, tiled=True)


def body(
    params,
    adam_m,
    adam_v,
    cameras,
    exposure,
    entry_owner,
    entry_local,
    block_counts,
    tile_view,
    tile_spot,
    d_image,
):
    requests, entries = route(tile_view, block_counts, entry_owner, entry_local)
    codes = exchange(requests)
    table = table_of(params)
    reply, rows = reply_of(codes, cameras, table)
    arrived = exchange(reply)
    back = render_of(tile_view, tile_spot, exposure, d_image, entries, arrived)
    returned = exchange(back)
    new_params, new_m, new_v, exposure_grad = update_of(
        codes, cameras, returned, rows, params, adam_m, adam_v
    )
    return (new_params, new_m, new_v, exposure_grad)


def solution(mesh):
    both = ("tiles", "gauss")
    placed = (
        P(None, both),
        P(None, both),
        P(None, both),
        P(),
        P(),
        P(both, None),
        P(both, None),
        P(both),
        P(both),
        P(both),
        P(both, None, None),
    )
    return jax.shard_map(
        body,
        mesh=mesh,
        in_specs=placed,
        out_specs=(P(None, both), P(None, both), P(None, both), P()),
        check_vma=False,
    )
```
